512 devices in a mesh: gx: 64 (over y, z), gy: 2 (over core), ma: 4 (over x).
Axes of the slice: x: 4, y: 8, z: 8, core: 2. Of those that a mesh axis runs over, the one named last changes fastest.
Arguments:
- ensemble: float32 [80, 2, 256, 256], P('ma', None, 'gx', 'gy'), may hold values from -6 to 6
- wind_field: float32 [2, 2, 256, 256], P(None, None, 'gx', 'gy'), may hold values from -0.45 to 0.45
- obs_value: float32 [4, 1024], replicated, may hold values from -6 to 6
- obs_var: float32 [4, 1024], replicated, may hold values from 2 to 20
- obs_region: int32 [4, 1024], replicated, may hold values from 0 to 127, as said below
- obs_cell: int32 [4, 1024], replicated, may hold values from 0 to 1023
- block_order: int32 [4], replicated, may hold values from 0 to 3, each once
- localization: float32 [64, 2, 4, 1024], P('gx', 'gy'), may hold values from 0 to 1
Outputs:
- analysis: float32 [80, 2, 256, 256], P('ma', None, 'gx', 'gy')
The draws below stay inside these ranges and needn't reach their ends.
Inputs may be any that keep to these rules, and one draw needn't show every extreme that they name: `obs_region`: region index = first-dimension region * 2 + second-dimension region.
All inputs are finite; a program needn't handle non-finite values.
Results may differ from the reference program's by a relative error of at most 0.0001.
Values sent between devices are 32-bit elements; how exact they have to be, the bound alone decides.
No kernel may reach another device: no remote copies, remote signals or barrier semaphores. Data moves between devices by JAX's collectives and lax.ppermute only.
A program may use at most 64 MiB of HBM per device.

```python
import math
import jax
import jax.numpy as jnp
from jax import lax

MEMBERS = 80
LEV = 2
STEPS = 2
BLOCKS = 4
OBS = 1024
CX = 4
CY = 128
RX = 64
RY = 2
NX = 256
NY = 256
CELLS = 1024


def owner_regions(key):
    return jax.random.randint(jax.random.fold_in(key, 11), (BLOCKS, OBS), 0, RX * RY)


def draw_obs_region(key, part):
    return owner_regions(key)


def draw_localization(key, part):
    owners = owner_regions(key)
    owner_x = (owners // RY).astype(jnp.float32)
    owner_y = (owners % RY).astype(jnp.float32)
    region_x = jnp.arange(RX).astype(jnp.float32)[:, None, None, None]
    region_y = jnp.arange(RY).astype(jnp.float32)[None, :, None, None]
    gap_x = jnp.abs(region_x - owner_x[None, None])
    gap_x = jnp.minimum(gap_x, RX - gap_x)
    gap_y = jnp.abs(region_y - owner_y[None, None])
    gap_y = jnp.minimum(gap_y, RY - gap_y)
    radius = max(RX * 1.0, 1.5)
    ratio = (gap_x * gap_x + gap_y * gap_y) / (radius * radius)
    bump = jnp.maximum(1.0 - ratio, 0.0) ** 2
    factor = jax.random.uniform(jax.random.fold_in(key, 12), (RX, RY, BLOCKS, OBS), jnp.float32, 0.5, 1.0)
    return (bump * factor).astype(jnp.float32)


def plant(result, rng, low, top_value):
    longest = result.shape.index(max(result.shape))
    spots = []
    for shift in (0, 1):
        where = [jax.random.randint(jax.random.fold_in(rng, axis), (), 0, length) for axis, length in enumerate(result.shape)]
        where[longest] = (where[longest] + shift) % result.shape[longest]
        spots.append(tuple(where))
    return result.at[spots[0]].set(low).at[spots[1]].set(top_value)


def block_scale(key, shape, pieces, low, high):
    loudness, own = 1.0, jax.random.fold_in(key, 6)
    for dim, blocks in pieces:
        draws = jnp.exp(jax.random.uniform(jax.random.fold_in(own, dim), (blocks,), jnp.float32, low / len(pieces), high / len(pieces)))
        loudness = loudness * jnp.repeat(draws, shape[dim] // blocks).reshape([-1 if axis == dim else 1 for axis in range(len(shape))])
    return loudness


def scatter_about(stream_key, shape, spread, limit, cuts=(), dtype=jnp.bfloat16):
    values = spread * jax.random.normal(stream_key, shape, jnp.float32)
    if cuts:
        values = values * block_scale(stream_key, shape, cuts, -0.22, 0.18)
    return jnp.clip(values, -limit, limit).astype(dtype)


def setup_inputs(seed: int = 0) -> dict:
    seeds = jax.random.split(jax.random.key(seed), 9)
    return {
        "ensemble": scatter_about(seeds[0], (MEMBERS, LEV, NX, NY), 1.0, 6.0, ((0, 4), (2, 64), (3, 2)), jnp.float32),
        "wind_field": jnp.clip(jax.random.uniform(seeds[1], (2, LEV, NX, NY), jnp.float32, -0.45, 0.45) * block_scale(seeds[1], (2, LEV, NX, NY), ((2, 64), (3, 2)), -0.4, 0.0), -0.45, 0.45),
        "obs_value": scatter_about(seeds[2], (BLOCKS, OBS), 1.0, 6.0, (), jnp.float32),
        "obs_var": jnp.clip(jnp.exp(jax.random.uniform(seeds[3], (BLOCKS, OBS), jnp.float32, math.log(2.0), math.log(20.0))), 2.0, 20.0),
        "obs_region": draw_obs_region(jax.random.fold_in(seeds[8], 71), 0),
        "obs_cell": plant(jax.random.randint(seeds[5], (BLOCKS, OBS), 0, CELLS), jax.random.fold_in(seeds[5], 1), 0, CELLS - 1).astype(jnp.int32),
        "block_order": jax.random.permutation(seeds[6], BLOCKS).astype(jnp.int32),
        "localization": draw_localization(jax.random.fold_in(seeds[8], 71), 0),
    }


KAPPA = 0.025

def advect(tracer, wind_field):
    east_wind = wind_field[0][None]
    north_wind = wind_field[1][None]
    west_side = jnp.roll(tracer, 1, axis=2)
    east_side = jnp.roll(tracer, -1, axis=2)
    south_side = jnp.roll(tracer, 1, axis=3)
    north_side = jnp.roll(tracer, -1, axis=3)
    return tracer - jnp.maximum(east_wind, 0.0) * (tracer - west_side) - jnp.minimum(east_wind, 0.0) * (east_side - tracer) - jnp.maximum(north_wind, 0.0) * (tracer - south_side) - jnp.minimum(north_wind, 0.0) * (north_side - tracer) + KAPPA * (east_side + west_side + north_side + south_side - 4.0 * tracer)

def mixing_matrix(prior_obs, observed, error_var, taper):
    denom = MEMBERS - 1.0
    obs_mean = lax.optimization_barrier(jnp.mean(prior_obs, axis=0))
    anomaly = prior_obs - obs_mean
    variance = lax.optimization_barrier(jnp.sum(anomaly * anomaly, axis=0)) / denom
    total_var = variance + error_var
    innovation = observed - obs_mean
    shrink = 1.0 / (1.0 + jnp.sqrt(error_var / total_var))
    gain_mean = taper * innovation / (denom * total_var)
    gain_spread = taper * shrink / (denom * total_var)
    shift_terms = jnp.dot(anomaly, gain_mean, precision=lax.Precision.HIGHEST)
    weighted = anomaly * gain_spread
    return shift_terms[:, None] - jnp.dot(weighted, anomaly.T, precision=lax.Precision.HIGHEST)

def reference(ensemble, wind_field, obs_value, obs_var, obs_region, obs_cell, block_order, localization):
    state = ensemble
    for step_index in range(STEPS):
        state = advect(state, wind_field)
    per_region = jax.vmap(jax.vmap(mixing_matrix, (None, None, None, 0)), (None, None, None, 0))
    for position in range(BLOCKS):
        block_id = block_order[position]
        regions = obs_region[block_id]
        cell_index = obs_cell[block_id]
        level_index = cell_index // (CX * CY)
        x_index = cell_index // CY % CX + regions // RY * CX
        y_index = cell_index % CY + regions % RY * CY
        prior_obs = state[:, level_index, x_index, y_index]
        taper = lax.dynamic_index_in_dim(localization, block_id, 2, keepdims=False)
        mixing = per_region(prior_obs, obs_value[block_id], obs_var[block_id], taper)
        center = lax.optimization_barrier(jnp.mean(state, axis=0))
        deviation = (state - center).reshape(MEMBERS, LEV, RX, CX, RY, CY)
        update = jnp.einsum('abpm,plaxby->mlaxby', mixing, deviation, precision=lax.Precision.HIGHEST)
        state = state + update.reshape(state.shape)
    return state
```

```python
import jax
import jax.numpy as jnp
from jax import lax
from jax.experimental import pallas as pl
from jax.experimental.pallas import tpu as pltpu
from jax.sharding import PartitionSpec as P

MEMBERS = 80
OWN = 20
BLOCKS = 4
OBS = 1024
CELLS = 1024
GX = 64
MA = 4
LANES = 128
GROUPS = OBS // LANES
KAPPA = 0.025
CHUNK = 5
HALF = OWN * 2 * GROUPS
ROWS_O = 256
F32 = jnp.float32
BF16 = jnp.bfloat16
VMEM = pl.BlockSpec(memory_space=pltpu.VMEM)
SMEM = pl.BlockSpec(memory_space=pltpu.SMEM)


def split(value):
    high = value.astype(BF16)
    return high, (value - high.astype(F32)).astype(BF16)


def dot_nn(a, b):
    return lax.dot_general(a, b, (((1,), (0,)), ((), ())), preferred_element_type=F32)


def dot_nt(a, b):
    return lax.dot_general(a, b, (((1,), (1,)), ((), ())), preferred_element_type=F32)


def block_row(ref, b, columns):
    row = ref[pl.ds(0, 1), columns]
    for i in range(1, BLOCKS):
        row = jnp.where(b == i, ref[pl.ds(i, 1), columns], row)
    return row


def advect_kernel(order, own_ref, other_ref, cell_ref, region_ref, state_ref, picked_ref, work):
    lane = lax.broadcasted_iota(jnp.int32, (8, LANES), 1)
    first, last = lane == 0, lane == LANES - 1

    def step(q, beside, u, v):
        west, east = pltpu.roll(q, 1, 0), pltpu.roll(q, 7, 0)
        south = jnp.where(first, pltpu.roll(beside, 1, 1), pltpu.roll(q, 1, 1))
        north = jnp.where(last, pltpu.roll(beside, LANES - 1, 1), pltpu.roll(q, LANES - 1, 1))
        return (
            q
            - jnp.maximum(u, 0.0) * (q - west)
            - jnp.minimum(u, 0.0) * (east - q)
            - jnp.maximum(v, 0.0) * (q - south)
            - jnp.minimum(v, 0.0) * (north - q)
            + KAPPA * (east + west + north + south - 4.0 * q)
        )

    work[pl.ds(160, 32), :] = jnp.zeros((32, LANES), F32)
    for level in range(2):
        row = (OWN * 2 + level) * 8
        u, v = own_ref[pl.ds(row, 8), :], own_ref[pl.ds(row + 32 - 16, 8), :]
        u_o, v_o = other_ref[pl.ds(row, 8), :], other_ref[pl.ds(row + 32 - 16, 8), :]
        for m in range(OWN):
            at = (m * 2 + level) * 8
            q, q_o = own_ref[pl.ds(at, 8), :], other_ref[pl.ds(at, 8), :]
            once, once_o = step(q, q_o, u, v), step(q_o, q, u_o, v_o)
            twice = step(once, once_o, u, v)
            work[pl.ds(m * 8 + level * 4, 4), :] = twice[2:6]
            state_ref[pl.ds(m * 8 + level * 4, 4), :] = twice[2:6]

    own_region = lax.axis_index("gx") * 2 + lax.axis_index("gy")
    for k in range(BLOCKS):
        b = order[k]
        for g in range(GROUPS):
            columns = pl.ds(g * LANES, LANES)
            cell, region = block_row(cell_ref, b, columns), block_row(region_ref, b, columns)
            y = jnp.broadcast_to(jnp.bitwise_and(cell, LANES - 1), (24, LANES))
            part = jnp.where(region == own_region, jnp.right_shift(cell, 7), -1)
            part = jnp.broadcast_to(part, (24, LANES))
            total = jnp.zeros((24, LANES), F32)
            for c in range(8):
                source = work[pl.ds(c, 24, stride=8), :]
                found = jnp.take_along_axis(source, y, axis=1)
                total = jnp.where(part == c, found, total)
            at = (k // 2) * HALF + (k % 2) * GROUPS + g
            picked_ref[pl.ds(at, OWN, stride=16), :] = total[:OWN]


def owner_kernel(parts_ref, out_ref):
    total = parts_ref[pl.ds(0, 40), :]
    for i in range(1, 16):
        total = total + parts_ref[pl.ds(i * 40, 40), :]
    part = total[0:CHUNK]
    for i in range(1, 8):
        part = part + total[i * CHUNK : (i + 1) * CHUNK]
    eight = jnp.concatenate([part] * 8, axis=0)
    for i in range(GX * MA // 8):
        out_ref[pl.ds(i * 40, 40), :] = eight


def filter_kernel(
    order,
    prior_ref,
    prior_o_ref,
    taper_ref,
    taper_o_ref,
    taper_own_ref,
    value_ref,
    var_ref,
    region_ref,
    gathered_ref,
    state_ref,
    out_ref,
    xt,
    tapers,
    onehots,
    b_high,
    b_both,
    increments,
):
    gy = lax.axis_index("gy")
    denom = MEMBERS - 1.0

    def load_half(ref, half):
        for g in range(16):
            block = ref[pl.ds(g, MEMBERS, stride=16), :]
            mean = jnp.mean(block, axis=0, keepdims=True)
            full = jnp.concatenate(
                [block - mean, mean, jnp.zeros((LANES - MEMBERS - 1, LANES), F32)], axis=0
            )
            xt[pl.ds((half * 16 + g) * LANES, LANES), :] = full.T

    @pl.when(gy == 0)
    def _():
        load_half(prior_ref, 0)
        load_half(prior_o_ref, 1)

    @pl.when(gy == 1)
    def _():
        load_half(prior_o_ref, 0)
        load_half(prior_ref, 1)

    for k in range(BLOCKS - 1):
        b = order[k]
        for g in range(GROUPS):
            for i, ref in enumerate((taper_ref, taper_o_ref)):
                high, low = split(ref.at[pl.ds(pl.multiple_of(b * (GX * 8), GX * 8), GX * 8), :][pl.ds(g, GX, stride=8), :])
                tapers[k, pl.ds(i * GX, GX), pl.ds(g * LANES, LANES)] = high
                tapers[k, pl.ds(LANES + i * GX, GX), pl.ds(g * LANES, LANES)] = low

    rows = lax.broadcasted_iota(jnp.int32, (LANES, LANES), 0)
    for k in range(1, BLOCKS):
        b = order[k]
        for g in range(GROUPS):
            region = block_row(region_ref, b, pl.ds(g * LANES, LANES))
            place = jnp.where(
                jnp.bitwise_and(region, 1) == gy, 0, GX
            ) + jnp.right_shift(region, 1)
            hot = (rows == jnp.broadcast_to(place, (LANES, LANES))).astype(F32).T.astype(BF16)
            at = pl.ds(((k - 1) * GROUPS + g) * LANES, LANES)
            onehots[at, pl.ds(0, LANES)] = hot
            onehots[at, pl.ds(LANES, LANES)] = hot

    lane = lax.broadcasted_iota(jnp.int32, (ROWS_O, LANES), 1)
    member_row = lax.broadcasted_iota(jnp.int32, (LANES, OBS), 0)
    increments[...] = jnp.zeros((LANES, LANES), F32)
    for k in range(BLOCKS):
        b = order[k]
        now = jnp.concatenate(
            [xt[pl.ds((k * GROUPS + g) * LANES, LANES), :].T for g in range(GROUPS)], axis=1
        )
        anomaly = jnp.where(member_row < MEMBERS, now, 0.0)
        mean = now[MEMBERS : MEMBERS + 1]
        variance = jnp.sum(anomaly * anomaly, axis=0, keepdims=True) / denom
        error_var = block_row(var_ref, b, pl.ds(0, OBS))
        total_var = variance + error_var
        shrink = 1.0 / (1.0 + jnp.sqrt(error_var / total_var))
        scale = 1.0 / (denom * total_var)
        gain_mean = (block_row(value_ref, b, pl.ds(0, OBS)) - mean) * scale
        gain = jnp.where(member_row == MEMBERS, gain_mean, -(shrink * scale) * anomaly)
        gain_high, gain_low = split(gain)

        tapered_high, tapered_low = split(anomaly * block_row(taper_own_ref, b, pl.ds(0, OBS)))
        mixing = (
            dot_nt(gain_high, tapered_high)
            + dot_nt(gain_low, tapered_high)
            + dot_nt(gain_high, tapered_low)
        )
        e = increments[...]
        increments[...] = e + mixing + jnp.dot(
            mixing, e, precision=lax.Precision.HIGHEST, preferred_element_type=F32
        )

        if k == BLOCKS - 1:
            continue
        a_high, a_low = split(anomaly)
        left = jnp.concatenate([a_high[:MEMBERS], a_high[:MEMBERS], a_low[:MEMBERS], jnp.zeros((16, OBS), BF16)], axis=0)
        b_high[...] = gain_high.astype(F32).T.astype(BF16)
        b_both[:, pl.ds(0, LANES)] = b_high[...]
        b_both[:, pl.ds(LANES, LANES)] = gain_low.astype(F32).T.astype(BF16)

        def chunk(i, carry, k=k, left=left):
            at = pl.multiple_of((k + 1) * OBS + i * ROWS_O, ROWS_O)
            x = xt[pl.ds(at, ROWS_O), :]
            clean = jnp.where(lane < MEMBERS, x, 0.0)
            high = clean.astype(BF16).astype(F32)
            low = (clean - high)
            low_rolled = pltpu.roll(low, MEMBERS, 1)
            first = jnp.where(lane < MEMBERS, high, low_rolled)
            second = jnp.where(lane < 2 * MEMBERS - LANES, low_rolled, pltpu.roll(high, 2 * MEMBERS - LANES, 1))
            second = jnp.where(lane < 3 * MEMBERS - LANES, second, 0.0)
            query = jnp.concatenate([first, second], axis=1).astype(BF16)
            hot = onehots[pl.ds(pl.multiple_of(at - OBS, ROWS_O), ROWS_O), :]
            weight = dot_nn(query, left) * dot_nn(hot, tapers[k])
            w_high, w_low = split(weight)
            both = dot_nn(w_high, b_both[...])
            xt[pl.ds(at, ROWS_O), :] = (
                x + both[:, :LANES] + both[:, LANES:] + dot_nn(w_low, b_high[...])
            )
            return carry

        lax.fori_loop(0, (BLOCKS - 1 - k) * OBS // ROWS_O, chunk, 0)

    q = lax.axis_index("ma")
    e = increments[...]
    total = e + e[MEMBERS : MEMBERS + 1]
    pick_row = lax.broadcasted_iota(jnp.int32, (24, LANES), 0)
    pick_lane = lax.broadcasted_iota(jnp.int32, (24, LANES), 1)
    chosen = jnp.where((pick_lane == pick_row + q * OWN) & (pick_row < OWN), 1.0, 0.0)
    transform = jnp.dot(chosen, total, precision=lax.Precision.HIGHEST, preferred_element_type=F32)
    tiles = []
    for c in range(8):
        tile = gathered_ref[pl.ds(c, MEMBERS, stride=8), :]
        tiles.append(tile - jnp.mean(tile, axis=0, keepdims=True))
    centered = jnp.concatenate(
        [jnp.concatenate(tiles, axis=1), jnp.zeros((LANES - MEMBERS, CELLS), F32)], axis=0
    )
    update = jnp.dot(transform, centered, precision=lax.Precision.HIGHEST, preferred_element_type=F32)
    for c in range(8):
        at = pl.ds(c, OWN, stride=8)
        out_ref[at, :] = state_ref[at, :] + update[:OWN, c * LANES : (c + 1) * LANES]


def other_core(x):
    return lax.ppermute(x, "gy", [(0, 1), (1, 0)])


def local(
    ensemble, wind_field, obs_value, obs_var, obs_region, obs_cell, block_order, localization
):
    q = lax.axis_index("ma")
    both = jnp.concatenate([ensemble, wind_field], axis=0)
    forward = [(i, (i + 1) % GX) for i in range(GX)]
    backward = [(i, (i - 1) % GX) for i in range(GX)]
    low = lax.ppermute(both[:, :, 2:], "gx", forward)
    high = lax.ppermute(both[:, :, :2], "gx", backward)
    own = jnp.concatenate([low, both, high], axis=2).reshape(-1, LANES)
    beside = other_core(own)

    taper_own = localization.reshape(BLOCKS, OBS)
    taper_send = lax.dynamic_slice_in_dim(taper_own, q, 1, 0)
    taper_send = jnp.broadcast_to(taper_send[None], (MA * GX, 1, OBS))
    tapers = lax.all_to_all(taper_send, ("ma", "gx"), 0, 0, tiled=True).reshape(-1, LANES)
    tapers_beside = other_core(tapers)

    state, picked = pl.pallas_call(
        advect_kernel,
        out_shape=(
            jax.ShapeDtypeStruct((OWN * 8, LANES), F32),
            jax.ShapeDtypeStruct((2 * HALF, LANES), F32),
        ),
        in_specs=[SMEM, VMEM, VMEM, VMEM, VMEM],
        out_specs=(VMEM, VMEM),
        scratch_shapes=[pltpu.VMEM((24 * 8, LANES), F32)],
        cost_estimate=pl.CostEstimate(flops=10_000_000, bytes_accessed=1_000_000, transcendentals=0),
        name="advect",
    )(block_order, own, beside, obs_cell, obs_region)

    parts = lax.all_to_all(picked.reshape(2 * GX, 1, CHUNK * LANES), ("gy", "gx"), 0, 0, tiled=True)
    gathered = lax.all_to_all(
        jnp.broadcast_to(state[None], (MA, OWN * 8, LANES)), "ma", 0, 0, tiled=True
    ).reshape(-1, LANES)
    owned = pl.pallas_call(
        owner_kernel,
        out_shape=jax.ShapeDtypeStruct((MA * GX * CHUNK, LANES), F32),
        in_specs=[VMEM],
        out_specs=VMEM,
        name="owner",
    )(parts.reshape(-1, LANES))
    priors = lax.all_to_all(
        owned.reshape(MA * GX, 1, CHUNK * LANES), ("ma", "gx"), 0, 0, tiled=True
    ).reshape(-1, LANES)
    priors_beside = other_core(priors)

    out = pl.pallas_call(
        filter_kernel,
        out_shape=jax.ShapeDtypeStruct((OWN * 8, LANES), F32),
        in_specs=[SMEM] + [VMEM] * 10,
        out_specs=VMEM,
        scratch_shapes=[
            pltpu.VMEM((BLOCKS * OBS, LANES), F32),
            pltpu.VMEM((BLOCKS - 1, 2 * LANES, OBS), BF16),
            pltpu.VMEM(((BLOCKS - 1) * OBS, 2 * LANES), BF16),
            pltpu.VMEM((OBS, LANES), BF16),
            pltpu.VMEM((OBS, 2 * LANES), BF16),
            pltpu.VMEM((LANES, LANES), F32),
        ],
        cost_estimate=pl.CostEstimate(flops=3_000_000_000, bytes_accessed=4_000_000, transcendentals=0),
        name="filter",
    )(
        block_order,
        priors,
        priors_beside,
        tapers,
        tapers_beside,
        taper_own,
        obs_value,
        obs_var,
        obs_region,
        gathered,
        state,
    )
    return out.reshape(ensemble.shape)


def solution(mesh):
    in_specs = (
        P("ma", None, "gx", "gy"),
        P(None, None, "gx", "gy"),
        P(),
        P(),
        P(),
        P(),
        P(),
        P("gx", "gy", None, None),
    )
    out_specs = P("ma", None, "gx", "gy")
    return jax.shard_map(local, mesh=mesh, in_specs=in_specs, out_specs=out_specs, check_vma=False)
```

```python
import jax
import jax.numpy as jnp
from jax import lax
from jax.experimental import pallas as pl
from jax.experimental.pallas import tpu as pltpu
from jax.sharding import PartitionSpec as P

MEMBERS = 80
OWN = 20
BLOCKS = 4
OBS = 1024
CELLS = 1024
GX = 64
MA = 4
LANES = 128
GROUPS = OBS // LANES
KAPPA = 0.025
CHUNK = 5
HALF = OWN * 2 * GROUPS
QUARTER = (BLOCKS - 1) * GROUPS // MA
ROWS_O = 256
F32 = jnp.float32
BF16 = jnp.bfloat16
VMEM = pl.BlockSpec(memory_space=pltpu.VMEM)
SMEM = pl.BlockSpec(memory_space=pltpu.SMEM)


def split(value):
    high = value.astype(BF16)
    return high, (value - high.astype(F32)).astype(BF16)


def dot_nn(a, b):
    return lax.dot_general(a, b, (((1,), (0,)), ((), ())), preferred_element_type=F32)


def dot_nt(a, b):
    return lax.dot_general(a, b, (((1,), (1,)), ((), ())), preferred_element_type=F32)


def block_row(ref, b, columns):
    row = ref[pl.ds(0, 1), columns]
    for i in range(1, BLOCKS):
        row = jnp.where(b == i, ref[pl.ds(i, 1), columns], row)
    return row


def advect_kernel(order, own_ref, other_ref, cell_ref, region_ref, state_ref, picked_ref, work):
    gx, gy = lax.axis_index("gx"), lax.axis_index("gy")
    lane = lax.broadcasted_iota(jnp.int32, (8, LANES), 1)
    first, last = lane == 0, lane == LANES - 1

    def step(q, beside, wind):
        u_up, u_down, v_up, v_down = wind
        west, east = pltpu.roll(q, 1, 0), pltpu.roll(q, 7, 0)
        south = jnp.where(first, pltpu.roll(beside, 1, 1), pltpu.roll(q, 1, 1))
        north = jnp.where(last, pltpu.roll(beside, LANES - 1, 1), pltpu.roll(q, LANES - 1, 1))
        return (
            q
            - u_up * (q - west)
            - u_down * (east - q)
            - v_up * (q - south)
            - v_down * (north - q)
            + KAPPA * (east + west + north + south - 4.0 * q)
        )

    def winds(ref, level):
        u = ref[pl.ds((OWN * 2 + level) * 8, 8), :]
        v = ref[pl.ds((OWN * 2 + 2 + level) * 8, 8), :]
        return jnp.maximum(u, 0.0), jnp.minimum(u, 0.0), jnp.maximum(v, 0.0), jnp.minimum(v, 0.0)

    for side in range(2):
        work[side, pl.ds(OWN * 8, 32), :] = jnp.zeros((32, LANES), F32)
    for level in range(2):
        wind, wind_o = winds(own_ref, level), winds(other_ref, level)
        for m in range(OWN):
            at = (m * 2 + level) * 8
            q, q_o = own_ref[pl.ds(at, 8), :], other_ref[pl.ds(at, 8), :]
            once, once_o = step(q, q_o, wind), step(q_o, q, wind_o)
            twice, twice_o = step(once, once_o, wind), step(once_o, once, wind_o)
            at = pl.ds(m * 8 + level * 4, 4)
            state_ref[at, :] = twice[2:6]
            work[0, at, :] = twice[2:6]
            work[1, at, :] = twice_o[2:6]

    for k in range(2):
        b = order[gy * 2 + k]
        for g in range(GROUPS):
            columns = pl.ds(g * LANES, LANES)
            cell, region = block_row(cell_ref, b, columns), block_row(region_ref, b, columns)
            y = jnp.broadcast_to(jnp.bitwise_and(cell, LANES - 1), (24, LANES))
            part = jnp.right_shift(cell, 7) + jnp.where(jnp.bitwise_and(region, 1) == gy, 0, 8)
            part = jnp.where(jnp.right_shift(region, 1) == gx, part, -1)
            part = jnp.broadcast_to(part, (24, LANES))
            total = jnp.zeros((24, LANES), F32)
            for c in range(16):
                source = work[c // 8, pl.ds(c % 8, 24, stride=8), :]
                found = jnp.take_along_axis(source, y, axis=1)
                total = jnp.where(part == c, found, total)
            picked_ref[pl.ds(k * GROUPS + g, OWN, stride=16), :] = total[:OWN]


def send_kernel(order, taper_ref, out_ref):
    q = lax.axis_index("ma")
    pieces = []
    for i in range(QUARTER):
        tile = q * QUARTER + i
        b, g = order[tile // GROUPS], tile % GROUPS
        row = block_row(taper_ref, b, pl.ds(0, LANES))
        for j in range(1, GROUPS):
            row = jnp.where(g == j, block_row(taper_ref, b, pl.ds(j * LANES, LANES)), row)
        pieces.append(row)
    four = jnp.concatenate(pieces * 4, axis=0)
    for i in range(GX // 4):
        out_ref[pl.ds(i * 4 * QUARTER, 4 * QUARTER), :] = four


def owner_kernel(parts_ref, out_ref):
    total = parts_ref[pl.ds(0, 40), :]
    for i in range(1, GX // 8):
        total = total + parts_ref[pl.ds(i * 40, 40), :]
    part = total[0:CHUNK]
    for i in range(1, 8):
        part = part + total[i * CHUNK : (i + 1) * CHUNK]
    eight = jnp.concatenate([part] * 8, axis=0)
    for i in range(GX * MA // 8):
        out_ref[pl.ds(i * 40, 40), :] = eight


def prepare_kernel(order, taper_ref, taper_o_ref, region_ref, tapers, onehots):
    q, gy = lax.axis_index("ma"), lax.axis_index("gy")
    for shift in range(MA):
        for i in range(QUARTER):
            tile = lax.rem(q - shift + MA, MA) * QUARTER + i
            for side, ref in enumerate((taper_ref, taper_o_ref)):
                high, low = split(ref[pl.ds(shift * GX * QUARTER + i, GX, stride=QUARTER), :])
                tapers[tile, pl.ds(side * GX, GX), :] = high
                tapers[tile, pl.ds(LANES + side * GX, GX), :] = low

    rows = lax.broadcasted_iota(jnp.int32, (LANES, LANES), 0)
    for k in range(1, BLOCKS):
        b = order[k]
        for g in range(GROUPS):
            region = block_row(region_ref, b, pl.ds(g * LANES, LANES))
            place = jnp.where(jnp.bitwise_and(region, 1) == gy, 0, GX) + jnp.right_shift(region, 1)
            hot = (rows == jnp.broadcast_to(place, (LANES, LANES))).astype(F32).T.astype(BF16)
            at = pl.ds(((k - 1) * GROUPS + g) * LANES, LANES)
            onehots[at, pl.ds(0, LANES)] = hot
            onehots[at, pl.ds(LANES, LANES)] = hot


def filter_kernel(
    order,
    prior_ref,
    prior_o_ref,
    tapers,
    onehots,
    taper_own_ref,
    value_ref,
    var_ref,
    gathered_1,
    gathered_2,
    gathered_3,
    state_ref,
    out_ref,
    xt,
    b_high,
    b_both,
    increments,
):
    gy = lax.axis_index("gy")
    denom = MEMBERS - 1.0

    def load_half(ref, half):
        for g in range(16):
            block = ref[pl.ds(g, MEMBERS, stride=16), :]
            mean = jnp.mean(block, axis=0, keepdims=True)
            full = jnp.concatenate(
                [block - mean, mean, jnp.zeros((LANES - MEMBERS - 1, LANES), F32)], axis=0
            )
            xt[pl.ds((half * 16 + g) * LANES, LANES), :] = full.T

    @pl.when(gy == 0)
    def _():
        load_half(prior_ref, 0)
        load_half(prior_o_ref, 1)

    @pl.when(gy == 1)
    def _():
        load_half(prior_o_ref, 0)
        load_half(prior_ref, 1)

    lane = lax.broadcasted_iota(jnp.int32, (ROWS_O, LANES), 1)
    member_row = lax.broadcasted_iota(jnp.int32, (LANES, OBS), 0)
    increments[...] = jnp.zeros((LANES, LANES), F32)
    for k in range(BLOCKS):
        b = order[k]
        now = jnp.concatenate(
            [xt[pl.ds((k * GROUPS + g) * LANES, LANES), :].T for g in range(GROUPS)], axis=1
        )
        anomaly = jnp.where(member_row < MEMBERS, now, 0.0)
        mean = now[MEMBERS : MEMBERS + 1]
        variance = jnp.sum(anomaly * anomaly, axis=0, keepdims=True) / denom
        error_var = block_row(var_ref, b, pl.ds(0, OBS))
        total_var = variance + error_var
        shrink = 1.0 / (1.0 + jnp.sqrt(error_var / total_var))
        scale = 1.0 / (denom * total_var)
        gain_mean = (block_row(value_ref, b, pl.ds(0, OBS)) - mean) * scale
        gain = jnp.where(member_row == MEMBERS, gain_mean, -(shrink * scale) * anomaly)
        gain_high, gain_low = split(gain)

        tapered_high, tapered_low = split(anomaly * block_row(taper_own_ref, b, pl.ds(0, OBS)))
        mixing = (
            dot_nt(gain_high, tapered_high)
            + dot_nt(gain_low, tapered_high)
            + dot_nt(gain_high, tapered_low)
        )
        e = increments[...]
        increments[...] = e + mixing + jnp.dot(
            mixing, e, precision=lax.Precision.HIGHEST, preferred_element_type=F32
        )

        if k == BLOCKS - 1:
            continue
        a_high, a_low = split(anomaly)
        left = jnp.concatenate([a_high[:MEMBERS], a_high[:MEMBERS], a_low[:MEMBERS], jnp.zeros((16, OBS), BF16)], axis=0)
        b_high[...] = gain_high.astype(F32).T.astype(BF16)
        b_both[:, pl.ds(0, LANES)] = b_high[...]
        b_both[:, pl.ds(LANES, LANES)] = gain_low.astype(F32).T.astype(BF16)

        def chunk(i, carry, k=k, left=left):
            taper = jnp.concatenate([tapers[k * GROUPS + g] for g in range(GROUPS)], axis=1)
            at = pl.multiple_of((k + 1) * OBS + i * ROWS_O, ROWS_O)
            x = xt[pl.ds(at, ROWS_O), :]
            clean = jnp.where(lane < MEMBERS, x, 0.0)
            high = clean.astype(BF16).astype(F32)
            low = (clean - high)
            low_rolled = pltpu.roll(low, MEMBERS, 1)
            first = jnp.where(lane < MEMBERS, high, low_rolled)
            second = jnp.where(lane < 2 * MEMBERS - LANES, low_rolled, pltpu.roll(high, 2 * MEMBERS - LANES, 1))
            second = jnp.where(lane < 3 * MEMBERS - LANES, second, 0.0)
            query = jnp.concatenate([first, second], axis=1).astype(BF16)
            hot = onehots[pl.ds(pl.multiple_of(at - OBS, ROWS_O), ROWS_O), :]
            weight = dot_nn(query, left) * dot_nn(hot, taper)
            w_high, w_low = split(weight)
            both = dot_nn(w_high, b_both[...])
            xt[pl.ds(at, ROWS_O), :] = (
                x + both[:, :LANES] + both[:, LANES:] + dot_nn(w_low, b_high[...])
            )
            return carry

        lax.fori_loop(0, (BLOCKS - 1 - k) * OBS // ROWS_O, chunk, 0)

    q = lax.axis_index("ma")
    e = increments[...]
    total = e + e[MEMBERS : MEMBERS + 1]
    row = lax.broadcasted_iota(jnp.int32, (24, LANES), 0)
    col = lax.broadcasted_iota(jnp.int32, (24, LANES), 1)
    chosen = jnp.where((col == row + q * OWN) & (row < OWN), 1.0, 0.0)
    transform = jnp.dot(chosen, total, precision=lax.Precision.HIGHEST, preferred_element_type=F32)
    row = lax.broadcasted_iota(jnp.int32, (LANES, LANES), 0)
    col = lax.broadcasted_iota(jnp.int32, (LANES, LANES), 1)
    back = sum(jnp.where(col >= i * OWN, 1, 0) for i in range(1, MA))
    member = jnp.bitwise_and(q - back, MA - 1) * OWN + col - back * OWN
    shuffle = jnp.where((row == member) & (col < MEMBERS), 1.0, 0.0)
    transform = jnp.dot(transform, shuffle, precision=lax.Precision.HIGHEST, preferred_element_type=F32)
    tiles = []
    for c in range(8):
        at = pl.ds(c, OWN, stride=8)
        tile = jnp.concatenate(
            [ref[at, :] for ref in (state_ref, gathered_1, gathered_2, gathered_3)], axis=0
        )
        tiles.append(tile - jnp.mean(tile, axis=0, keepdims=True))
    centered = jnp.concatenate(
        [jnp.concatenate(tiles, axis=1), jnp.zeros((LANES - MEMBERS, CELLS), F32)], axis=0
    )
    update = jnp.dot(transform, centered, precision=lax.Precision.HIGHEST, preferred_element_type=F32)
    for c in range(8):
        at = pl.ds(c, OWN, stride=8)
        out_ref[at, :] = state_ref[at, :] + update[:OWN, c * LANES : (c + 1) * LANES]


def other_core(x):
    return lax.ppermute(x, "gy", [(0, 1), (1, 0)])


def params(mebibytes):
    return pltpu.CompilerParams(vmem_limit_bytes=mebibytes * 1024 * 1024)


def over_members(x):
    return [lax.ppermute(x, "ma", [(i, (i + s) % MA) for i in range(MA)]) for s in range(1, MA)]


def local(
    ensemble, wind_field, obs_value, obs_var, obs_region, obs_cell, block_order, localization
):
    taper_own = localization.reshape(BLOCKS, OBS)
    taper_send = pl.pallas_call(
        send_kernel,
        out_shape=jax.ShapeDtypeStruct((GX * QUARTER, LANES), F32),
        in_specs=[SMEM, VMEM],
        out_specs=VMEM,
        compiler_params=params(2),
        name="send",
    )(block_order, taper_own)
    tapers = lax.all_to_all(
        taper_send.reshape(GX, 1, QUARTER * LANES), "gx", 0, 0, tiled=True
    ).reshape(-1, LANES)

    both = jnp.concatenate([ensemble, wind_field], axis=0)
    forward = [(i, (i + 1) % GX) for i in range(GX)]
    backward = [(i, (i - 1) % GX) for i in range(GX)]
    low = lax.ppermute(both[:, :, 2:], "gx", forward)
    high = lax.ppermute(both[:, :, :2], "gx", backward)
    own = jnp.concatenate([low, both, high], axis=2).reshape(-1, LANES)
    beside = other_core(own)

    state, picked = pl.pallas_call(
        advect_kernel,
        out_shape=(
            jax.ShapeDtypeStruct((OWN * 8, LANES), F32),
            jax.ShapeDtypeStruct((HALF, LANES), F32),
        ),
        in_specs=[SMEM, VMEM, VMEM, VMEM, VMEM],
        out_specs=(VMEM, VMEM),
        scratch_shapes=[pltpu.VMEM((2, 24 * 8, LANES), F32)],
        compiler_params=params(4),
        cost_estimate=pl.CostEstimate(flops=10_000_000, bytes_accessed=1_000_000, transcendentals=0),
        name="advect",
    )(block_order, own, beside, obs_cell, obs_region)

    picked, tapers = lax.optimization_barrier((picked, tapers))
    parts = lax.all_to_all(picked.reshape(GX, 1, CHUNK * LANES), "gx", 0, 0, tiled=True)
    parts, tapers = lax.optimization_barrier((parts, [tapers] + over_members(tapers)))
    tapers = jnp.concatenate(tapers, axis=0)
    tapers_beside = other_core(tapers)
    gathered = over_members(state)
    prepared = pl.pallas_call(
        prepare_kernel,
        out_shape=(
            jax.ShapeDtypeStruct(((BLOCKS - 1) * GROUPS, 2 * LANES, LANES), BF16),
            jax.ShapeDtypeStruct(((BLOCKS - 1) * OBS, 2 * LANES), BF16),
        ),
        in_specs=[SMEM, VMEM, VMEM, VMEM],
        out_specs=(VMEM, VMEM),
        compiler_params=params(8),
        cost_estimate=pl.CostEstimate(flops=10_000_000, bytes_accessed=5_000_000, transcendentals=0),
        name="prepare",
    )(block_order, tapers, tapers_beside, obs_region)
    owned = pl.pallas_call(
        owner_kernel,
        out_shape=jax.ShapeDtypeStruct((MA * GX * CHUNK, LANES), F32),
        in_specs=[VMEM],
        out_specs=VMEM,
        compiler_params=params(4),
        name="owner",
    )(parts.reshape(-1, LANES))
    priors = lax.all_to_all(
        owned.reshape(MA * GX, 1, CHUNK * LANES), ("ma", "gx"), 0, 0, tiled=True
    ).reshape(-1, LANES)
    priors, prepared, gathered = lax.optimization_barrier((priors, prepared, gathered))
    priors_beside = other_core(priors)

    out = pl.pallas_call(
        filter_kernel,
        out_shape=jax.ShapeDtypeStruct((OWN * 8, LANES), F32),
        in_specs=[SMEM] + [VMEM] * 11,
        out_specs=VMEM,
        scratch_shapes=[
            pltpu.VMEM((BLOCKS * OBS, LANES), F32),
            pltpu.VMEM((OBS, LANES), BF16),
            pltpu.VMEM((OBS, 2 * LANES), BF16),
            pltpu.VMEM((LANES, LANES), F32),
        ],
        compiler_params=params(32),
        cost_estimate=pl.CostEstimate(flops=3_000_000_000, bytes_accessed=4_000_000, transcendentals=0),
        name="filter",
    )(
        block_order,
        priors,
        priors_beside,
        *prepared,
        taper_own,
        obs_value,
        obs_var,
        *gathered,
        state,
    )
    return out.reshape(ensemble.shape)


def solution(mesh):
    in_specs = (
        P("ma", None, "gx", "gy"),
        P(None, None, "gx", "gy"),
        P(),
        P(),
        P(),
        P(),
        P(),
        P("gx", "gy", None, None),
    )
    out_specs = P("ma", None, "gx", "gy")
    return jax.shard_map(local, mesh=mesh, in_specs=in_specs, out_specs=out_specs, check_vma=False)
```

```python
import jax
import jax.numpy as jnp
from jax import lax
from jax.experimental import pallas as pl
from jax.experimental.pallas import tpu as pltpu
from jax.sharding import PartitionSpec as P

MEMBERS = 80
OWN = 20
BLOCKS = 4
OBS = 1024
CELLS = 1024
GX = 64
MA = 4
LANES = 128
GROUPS = OBS // LANES
KAPPA = 0.025
CHUNK = 5
HALF = OWN * 2 * GROUPS
QUARTER = (BLOCKS - 1) * GROUPS // MA
SENT = CHUNK + QUARTER
ROWS_O = 256
F32 = jnp.float32
BF16 = jnp.bfloat16
VMEM = pl.BlockSpec(memory_space=pltpu.VMEM)
SMEM = pl.BlockSpec(memory_space=pltpu.SMEM)


def split(value):
    high = value.astype(BF16)
    return high, (value - high.astype(F32)).astype(BF16)


def dot_nn(a, b):
    return lax.dot_general(a, b, (((1,), (0,)), ((), ())), preferred_element_type=F32)


def dot_nt(a, b):
    return lax.dot_general(a, b, (((1,), (1,)), ((), ())), preferred_element_type=F32)


def block_row(ref, b, columns):
    row = ref[pl.ds(0, 1), columns]
    for i in range(1, BLOCKS):
        row = jnp.where(b == i, ref[pl.ds(i, 1), columns], row)
    return row


def advect_kernel(own_ref, other_ref, index_ref, state_ref, picked_ref, work):
    lane = lax.broadcasted_iota(jnp.int32, (8, LANES), 1)
    first, last = lane == 0, lane == LANES - 1

    def step(q, beside, wind):
        u_up, u_down, v_up, v_down = wind
        west, east = pltpu.roll(q, 1, 0), pltpu.roll(q, 7, 0)
        south = jnp.where(first, pltpu.roll(beside, 1, 1), pltpu.roll(q, 1, 1))
        north = jnp.where(last, pltpu.roll(beside, LANES - 1, 1), pltpu.roll(q, LANES - 1, 1))
        return (
            q
            - u_up * (q - west)
            - u_down * (east - q)
            - v_up * (q - south)
            - v_down * (north - q)
            + KAPPA * (east + west + north + south - 4.0 * q)
        )

    def winds(ref, level):
        u = ref[pl.ds((OWN * 2 + level) * 8, 8), :]
        v = ref[pl.ds((OWN * 2 + 2 + level) * 8, 8), :]
        return jnp.maximum(u, 0.0), jnp.minimum(u, 0.0), jnp.maximum(v, 0.0), jnp.minimum(v, 0.0)

    for side in range(2):
        work[side, pl.ds(OWN * 8, 32), :] = jnp.zeros((32, LANES), F32)
    for level in range(2):
        wind, wind_o = winds(own_ref, level), winds(other_ref, level)
        for m in range(OWN):
            at = (m * 2 + level) * 8
            q, q_o = own_ref[pl.ds(at, 8), :], other_ref[pl.ds(at, 8), :]
            once, once_o = step(q, q_o, wind), step(q_o, q, wind_o)
            twice, twice_o = step(once, once_o, wind), step(once_o, once, wind_o)
            at = pl.ds(m * 8 + level * 4, 4)
            state_ref[at, :] = twice[2:6]
            work[0, at, :] = twice[2:6]
            work[1, at, :] = twice_o[2:6]

    for g in range(2 * GROUPS):
        y = jnp.broadcast_to(index_ref[pl.ds(g, 1), :].astype(jnp.int32), (24, LANES))
        part = jnp.broadcast_to(index_ref[pl.ds(g + 16, 1), :].astype(jnp.int32), (24, LANES))
        total = jnp.zeros((24, LANES), F32)
        for c in range(16):
            source = work[c // 8, pl.ds(c % 8, 24, stride=8), :]
            found = jnp.take_along_axis(source, y, axis=1, mode="promise_in_bounds")
            total = jnp.where(part == c, found, total)
        for i in range(MA):
            at = (i * 2 * GROUPS + g) * CHUNK
            picked_ref[pl.ds(at, CHUNK), :] = total[i * CHUNK : (i + 1) * CHUNK]


def prepare_kernel(*refs):
    sources, results, copies, done = refs[:6], refs[6:9], refs[9:15], refs[15]
    moves = [
        pltpu.make_async_copy(source, copy, done.at[i])
        for i, (source, copy) in enumerate(zip(sources, copies))
    ]
    for move in moves:
        move.start()
    for move in moves:
        move.wait()
    order, cell_ref, region_ref, value_ref, var_ref, taper_ref = copies
    index_ref, obs_ref, onehots = results
    gx, gy, q = lax.axis_index("gx"), lax.axis_index("gy"), lax.axis_index("ma")
    for k in range(2):
        b = order[gy * 2 + k]
        for g in range(GROUPS):
            columns = pl.ds(g * LANES, LANES)
            cell, region = block_row(cell_ref, b, columns), block_row(region_ref, b, columns)
            part = jnp.right_shift(cell, 7) + jnp.where(jnp.bitwise_and(region, 1) == gy, 0, 8)
            part = jnp.where(jnp.right_shift(region, 1) == gx, part, -1)
            at = k * GROUPS + g
            index_ref[pl.ds(at, 1), :] = jnp.bitwise_and(cell, LANES - 1).astype(F32)
            index_ref[pl.ds(at + 16, 1), :] = part.astype(F32)

    for k in range(BLOCKS):
        for i, ref in enumerate((value_ref, var_ref, taper_ref)):
            obs_ref[pl.ds(i * BLOCKS + k, 1), :] = block_row(ref, order[k], pl.ds(0, OBS))

    index_ref[pl.ds(32, 8), :] = jnp.zeros((8, LANES), F32)
    for i in range(QUARTER):
        tile = q * QUARTER + i
        b, g = order[tile // GROUPS], tile % GROUPS
        row = block_row(taper_ref, b, pl.ds(0, LANES))
        for j in range(1, GROUPS):
            row = jnp.where(g == j, block_row(taper_ref, b, pl.ds(j * LANES, LANES)), row)
        index_ref[pl.ds(32 + i, 1), :] = row

    rows = lax.broadcasted_iota(jnp.int32, (LANES, LANES), 0)
    for k in range(1, BLOCKS):
        b = order[k]
        for g in range(GROUPS):
            region = block_row(region_ref, b, pl.ds(g * LANES, LANES))
            place = jnp.where(jnp.bitwise_and(region, 1) == gy, 0, GX) + jnp.right_shift(region, 1)
            hot = (rows == jnp.broadcast_to(place, (LANES, LANES))).astype(F32).T.astype(BF16)
            at = pl.ds(((k - 1) * GROUPS + g) * LANES, LANES)
            onehots[at, pl.ds(0, LANES)] = hot
            onehots[at, pl.ds(LANES, LANES)] = hot


def owner_kernel(parts_ref, index_ref, out_ref):
    total = parts_ref[pl.ds(0, 40), :]
    for i in range(1, GX // 8):
        total = total + parts_ref[pl.ds(i * 40, 40), :]
    part = total[0:CHUNK]
    for i in range(1, 8):
        part = part + total[i * CHUNK : (i + 1) * CHUNK]
    eight = jnp.concatenate([part, index_ref[pl.ds(32, QUARTER), :]] * 8, axis=0)
    for i in range(GX * MA // 8):
        out_ref[pl.ds(i * 8 * SENT, 8 * SENT), :] = eight


def filter_kernel(
    came_ref,
    came_o_ref,
    onehots,
    obs_ref,
    gathered_1,
    gathered_2,
    gathered_3,
    state_ref,
    out_ref,
    xt,
    tapers,
    b_high,
    b_both,
    increments,
):
    gy = lax.axis_index("gy")
    denom = MEMBERS - 1.0

    def load_half(ref, half):
        for g in range(16):
            block = jnp.concatenate(
                [ref[pl.ds(g * SENT + i, 16, stride=16 * SENT), :] for i in range(CHUNK)], axis=0
            )
            mean = jnp.mean(block, axis=0, keepdims=True)
            full = jnp.concatenate(
                [block - mean, mean, jnp.zeros((LANES - MEMBERS - 1, LANES), F32)], axis=0
            )
            xt[pl.ds((half * 16 + g) * LANES, LANES), :] = full.T

    @pl.when(gy == 0)
    def _():
        load_half(came_ref, 0)
        load_half(came_o_ref, 1)

    @pl.when(gy == 1)
    def _():
        load_half(came_o_ref, 0)
        load_half(came_ref, 1)

    for tile in range((BLOCKS - 1) * GROUPS):
        at = pl.ds(tile // QUARTER * GX * SENT + CHUNK + tile % QUARTER, GX, stride=SENT)
        for side, ref in enumerate((came_ref, came_o_ref)):
            high, low = split(ref[at, :])
            tapers[tile, pl.ds(side * GX, GX), :] = high
            tapers[tile, pl.ds(LANES + side * GX, GX), :] = low

    lane = lax.broadcasted_iota(jnp.int32, (ROWS_O, LANES), 1)
    member_row = lax.broadcasted_iota(jnp.int32, (LANES, OBS), 0)
    increments[...] = jnp.zeros((LANES, LANES), F32)
    for k in range(BLOCKS):
        now = jnp.concatenate(
            [xt[pl.ds((k * GROUPS + g) * LANES, LANES), :].T for g in range(GROUPS)], axis=1
        )
        anomaly = jnp.where(member_row < MEMBERS, now, 0.0)
        mean = now[MEMBERS : MEMBERS + 1]
        variance = jnp.sum(anomaly * anomaly, axis=0, keepdims=True) / denom
        error_var = obs_ref[pl.ds(BLOCKS + k, 1), :]
        total_var = variance + error_var
        shrink = 1.0 / (1.0 + jnp.sqrt(error_var / total_var))
        scale = 1.0 / (denom * total_var)
        gain_mean = (obs_ref[pl.ds(k, 1), :] - mean) * scale
        gain = jnp.where(member_row == MEMBERS, gain_mean, -(shrink * scale) * anomaly)
        gain_high, gain_low = split(gain)

        tapered_high, tapered_low = split(anomaly * obs_ref[pl.ds(2 * BLOCKS + k, 1), :])
        mixing = (
            dot_nt(gain_high, tapered_high)
            + dot_nt(gain_low, tapered_high)
            + dot_nt(gain_high, tapered_low)
        )
        e = increments[...]
        increments[...] = e + mixing + jnp.dot(
            mixing, e, precision=lax.Precision.HIGHEST, preferred_element_type=F32
        )

        if k == BLOCKS - 1:
            continue
        a_high, a_low = split(anomaly)
        left = jnp.concatenate([a_high[:MEMBERS], a_high[:MEMBERS], a_low[:MEMBERS], jnp.zeros((16, OBS), BF16)], axis=0)
        b_high[...] = gain_high.astype(F32).T.astype(BF16)
        b_both[:, pl.ds(0, LANES)] = b_high[...]
        b_both[:, pl.ds(LANES, LANES)] = gain_low.astype(F32).T.astype(BF16)

        def chunk(i, carry, k=k, left=left):
            taper = jnp.concatenate([tapers[k * GROUPS + g] for g in range(GROUPS)], axis=1)
            at = pl.multiple_of((k + 1) * OBS + i * ROWS_O, ROWS_O)
            x = xt[pl.ds(at, ROWS_O), :]
            clean = jnp.where(lane < MEMBERS, x, 0.0)
            high = clean.astype(BF16).astype(F32)
            low = (clean - high)
            low_rolled = pltpu.roll(low, MEMBERS, 1)
            first = jnp.where(lane < MEMBERS, high, low_rolled)
            second = jnp.where(lane < 2 * MEMBERS - LANES, low_rolled, pltpu.roll(high, 2 * MEMBERS - LANES, 1))
            second = jnp.where(lane < 3 * MEMBERS - LANES, second, 0.0)
            query = jnp.concatenate([first, second], axis=1).astype(BF16)
            hot = onehots[pl.ds(pl.multiple_of(at - OBS, ROWS_O), ROWS_O), :]
            weight = dot_nn(query, left) * dot_nn(hot, taper)
            w_high, w_low = split(weight)
            both = dot_nn(w_high, b_both[...])
            xt[pl.ds(at, ROWS_O), :] = (
                x + both[:, :LANES] + both[:, LANES:] + dot_nn(w_low, b_high[...])
            )
            return carry

        lax.fori_loop(0, (BLOCKS - 1 - k) * OBS // ROWS_O, chunk, 0)

    q = lax.axis_index("ma")
    e = increments[...]
    total = e + e[MEMBERS : MEMBERS + 1]
    row = lax.broadcasted_iota(jnp.int32, (24, LANES), 0)
    col = lax.broadcasted_iota(jnp.int32, (24, LANES), 1)
    fifth = sum(jnp.where(row >= i * CHUNK, 1, 0) for i in range(1, MA))
    member = (row - fifth * CHUNK) * 16 + q * MA + fifth
    chosen = jnp.where((col == member) & (row < OWN), 1.0, 0.0)
    transform = jnp.dot(chosen, total, precision=lax.Precision.HIGHEST, preferred_element_type=F32)
    row = lax.broadcasted_iota(jnp.int32, (LANES, LANES), 0)
    col = lax.broadcasted_iota(jnp.int32, (LANES, LANES), 1)
    back = sum(jnp.where(col >= i * OWN, 1, 0) for i in range(1, MA))
    place = col - back * OWN
    fifth = sum(jnp.where(place >= i * CHUNK, 1, 0) for i in range(1, MA))
    member = (place - fifth * CHUNK) * 16 + jnp.bitwise_and(q - back, MA - 1) * MA + fifth
    shuffle = jnp.where((row == member) & (col < MEMBERS), 1.0, 0.0)
    transform = jnp.dot(transform, shuffle, precision=lax.Precision.HIGHEST, preferred_element_type=F32)
    tiles = []
    for c in range(8):
        at = pl.ds(c, OWN, stride=8)
        tile = jnp.concatenate(
            [ref[at, :] for ref in (state_ref, gathered_1, gathered_2, gathered_3)], axis=0
        )
        tiles.append(tile - jnp.mean(tile, axis=0, keepdims=True))
    centered = jnp.concatenate(
        [jnp.concatenate(tiles, axis=1), jnp.zeros((LANES - MEMBERS, CELLS), F32)], axis=0
    )
    update = jnp.dot(transform, centered, precision=lax.Precision.HIGHEST, preferred_element_type=F32)
    for c in range(8):
        at = pl.ds(c, OWN, stride=8)
        out_ref[at, :] = state_ref[at, :] + update[:OWN, c * LANES : (c + 1) * LANES]


def other_core(x):
    return lax.ppermute(x, "gy", [(0, 1), (1, 0)])


def params(mebibytes):
    return pltpu.CompilerParams(vmem_limit_bytes=mebibytes * 1024 * 1024)


def over_members(x):
    return [lax.ppermute(x, "ma", [(i, (i + s) % MA) for i in range(MA)]) for s in range(1, MA)]


def local(
    ensemble, wind_field, obs_value, obs_var, obs_region, obs_cell, block_order, localization
):
    both = jnp.concatenate([ensemble, wind_field], axis=0)
    forward = [(i, (i + 1) % GX) for i in range(GX)]
    backward = [(i, (i - 1) % GX) for i in range(GX)]
    low = lax.ppermute(both[:, :, 2:], "gx", forward)
    high = lax.ppermute(both[:, :, :2], "gx", backward)
    prepared = pl.pallas_call(
        prepare_kernel,
        out_shape=(
            jax.ShapeDtypeStruct((40, LANES), F32),
            jax.ShapeDtypeStruct((3 * BLOCKS, OBS), F32),
            jax.ShapeDtypeStruct(((BLOCKS - 1) * OBS, 2 * LANES), BF16),
        ),
        in_specs=[pl.BlockSpec(memory_space=pltpu.HBM)] * 6,
        out_specs=(VMEM,) * 3,
        scratch_shapes=[pltpu.SMEM((BLOCKS,), jnp.int32)]
        + [pltpu.VMEM((BLOCKS, OBS), jnp.int32)] * 2
        + [pltpu.VMEM((BLOCKS, OBS), F32)] * 3
        + [pltpu.SemaphoreType.DMA((6,))],
        compiler_params=params(60),
        cost_estimate=pl.CostEstimate(flops=10_000_000, bytes_accessed=2_000_000, transcendentals=0),
        name="prepare",
    )(block_order, obs_cell, obs_region, obs_value, obs_var, localization.reshape(BLOCKS, OBS))
    low, high, prepared = lax.optimization_barrier((low, high, prepared))
    index, observed, onehots = prepared
    own = jnp.concatenate([low, both, high], axis=2).reshape(-1, LANES)
    beside = other_core(own)

    state, picked = pl.pallas_call(
        advect_kernel,
        out_shape=(
            jax.ShapeDtypeStruct((OWN * 8, LANES), F32),
            jax.ShapeDtypeStruct((HALF, LANES), F32),
        ),
        in_specs=[VMEM] * 3,
        out_specs=(VMEM, VMEM),
        scratch_shapes=[pltpu.VMEM((2, 24 * 8, LANES), F32)],
        compiler_params=params(4),
        cost_estimate=pl.CostEstimate(flops=10_000_000, bytes_accessed=1_000_000, transcendentals=0),
        name="advect",
    )(own, beside, index)

    parts = lax.all_to_all(picked.reshape(GX, 1, CHUNK * LANES), "gx", 0, 0, tiled=True)
    gathered = over_members(state)
    owned = pl.pallas_call(
        owner_kernel,
        out_shape=jax.ShapeDtypeStruct((MA * GX * SENT, LANES), F32),
        in_specs=[VMEM, VMEM],
        out_specs=VMEM,
        compiler_params=params(4),
        name="owner",
    )(parts.reshape(-1, LANES), index)
    came = lax.all_to_all(
        owned.reshape(MA * GX, 1, SENT * LANES), ("ma", "gx"), 0, 0, tiled=True
    ).reshape(-1, LANES)
    came, gathered = lax.optimization_barrier((came, gathered))
    came_beside = other_core(came)

    out = pl.pallas_call(
        filter_kernel,
        out_shape=jax.ShapeDtypeStruct((OWN * 8, LANES), F32),
        in_specs=[VMEM] * 8,
        out_specs=VMEM,
        scratch_shapes=[
            pltpu.VMEM((BLOCKS * OBS, LANES), F32),
            pltpu.VMEM(((BLOCKS - 1) * GROUPS, 2 * LANES, LANES), BF16),
            pltpu.VMEM((OBS, LANES), BF16),
            pltpu.VMEM((OBS, 2 * LANES), BF16),
            pltpu.VMEM((LANES, LANES), F32),
        ],
        compiler_params=params(32),
        cost_estimate=pl.CostEstimate(flops=3_000_000_000, bytes_accessed=4_000_000, transcendentals=0),
        name="filter",
    )(came, came_beside, onehots, observed, *gathered, state)
    return out.reshape(ensemble.shape)


def solution(mesh):
    in_specs = (
        P("ma", None, "gx", "gy"),
        P(None, None, "gx", "gy"),
        P(),
        P(),
        P(),
        P(),
        P(),
        P("gx", "gy", None, None),
    )
    out_specs = P("ma", None, "gx", "gy")
    return jax.shard_map(local, mesh=mesh, in_specs=in_specs, out_specs=out_specs, check_vma=False)
```

```python
import jax
import jax.numpy as jnp
from jax import lax
from jax.experimental import pallas as pl
from jax.experimental.pallas import tpu as pltpu
from jax.sharding import PartitionSpec as P

MEMBERS = 80
OWN = 20
BLOCKS = 4
OBS = 1024
CELLS = 1024
GX = 64
MA = 4
LANES = 128
GROUPS = OBS // LANES
KAPPA = 0.025
CHUNK = 5
HALF = OWN * 2 * GROUPS
QUARTER = (BLOCKS - 1) * GROUPS // MA
SENT = CHUNK + QUARTER
TAPERS = (BLOCKS - 1) * GROUPS * 2 * LANES
ROWS_O = 256
F32 = jnp.float32
BF16 = jnp.bfloat16
VMEM = pl.BlockSpec(memory_space=pltpu.VMEM)
SMEM = pl.BlockSpec(memory_space=pltpu.SMEM)


def split(value):
    high = value.astype(BF16)
    return high, (value - high.astype(F32)).astype(BF16)


def dot_nn(a, b):
    return lax.dot_general(a, b, (((1,), (0,)), ((), ())), preferred_element_type=F32)


def dot_nt(a, b):
    return lax.dot_general(a, b, (((1,), (1,)), ((), ())), preferred_element_type=F32)


def block_row(ref, b, columns):
    row = ref[pl.ds(0, 1), columns]
    for i in range(1, BLOCKS):
        row = jnp.where(b == i, ref[pl.ds(i, 1), columns], row)
    return row


def advect_kernel(own_ref, other_ref, index_ref, state_ref, picked_ref, work):
    lane = lax.broadcasted_iota(jnp.int32, (8, LANES), 1)
    first, last = lane == 0, lane == LANES - 1

    def step(q, beside, wind):
        u_up, u_down, v_up, v_down = wind
        west, east = pltpu.roll(q, 1, 0), pltpu.roll(q, 7, 0)
        south = jnp.where(first, pltpu.roll(beside, 1, 1), pltpu.roll(q, 1, 1))
        north = jnp.where(last, pltpu.roll(beside, LANES - 1, 1), pltpu.roll(q, LANES - 1, 1))
        return (
            q
            - u_up * (q - west)
            - u_down * (east - q)
            - v_up * (q - south)
            - v_down * (north - q)
            + KAPPA * (east + west + north + south - 4.0 * q)
        )

    def winds(ref, level):
        u = ref[pl.ds((OWN * 2 + level) * 8, 8), :]
        v = ref[pl.ds((OWN * 2 + 2 + level) * 8, 8), :]
        return jnp.maximum(u, 0.0), jnp.minimum(u, 0.0), jnp.maximum(v, 0.0), jnp.minimum(v, 0.0)

    for side in range(2):
        work[side, pl.ds(OWN * 8, 32), :] = jnp.zeros((32, LANES), F32)
    for level in range(2):
        wind, wind_o = winds(own_ref, level), winds(other_ref, level)
        for m in range(OWN):
            at = (m * 2 + level) * 8
            q, q_o = own_ref[pl.ds(at, 8), :], other_ref[pl.ds(at, 8), :]
            once, once_o = step(q, q_o, wind), step(q_o, q, wind_o)
            twice, twice_o = step(once, once_o, wind), step(once_o, once, wind_o)
            at = pl.ds(m * 8 + level * 4, 4)
            state_ref[at, :] = twice[2:6]
            work[0, at, :] = twice[2:6]
            work[1, at, :] = twice_o[2:6]

    send = index_ref[pl.ds(32, QUARTER), :]
    for g in range(2 * GROUPS):
        y = jnp.broadcast_to(index_ref[pl.ds(g, 1), :].astype(jnp.int32), (24, LANES))
        part = jnp.broadcast_to(index_ref[pl.ds(g + 16, 1), :].astype(jnp.int32), (24, LANES))
        total = jnp.zeros((24, LANES), F32)
        for c in range(16):
            source = work[c // 8, pl.ds(c % 8, 24, stride=8), :]
            found = jnp.take_along_axis(source, y, axis=1, mode="promise_in_bounds")
            total = jnp.where(part == c, found, total)
        for i in range(MA):
            at = (i * 2 * GROUPS + g) * SENT
            picked_ref[pl.ds(at, CHUNK), :] = total[i * CHUNK : (i + 1) * CHUNK]
            picked_ref[pl.ds(at + CHUNK, QUARTER), :] = send


def prepare_kernel(*refs):
    sources, results, copies, done = refs[:6], refs[6:8], refs[8:14], refs[14]
    moves = [
        pltpu.make_async_copy(source, copy, done.at[i])
        for i, (source, copy) in enumerate(zip(sources, copies))
    ]
    for move in moves:
        move.start()
    for move in moves:
        move.wait()
    order, cell_ref, region_ref, value_ref, var_ref, taper_ref = copies
    index_ref, obs_ref = results
    gx, gy, q = lax.axis_index("gx"), lax.axis_index("gy"), lax.axis_index("ma")
    for k in range(2):
        b = order[gy * 2 + k]
        for g in range(GROUPS):
            columns = pl.ds(g * LANES, LANES)
            cell, region = block_row(cell_ref, b, columns), block_row(region_ref, b, columns)
            part = jnp.right_shift(cell, 7) + jnp.where(jnp.bitwise_and(region, 1) == gy, 0, 8)
            part = jnp.where(jnp.right_shift(region, 1) == gx, part, -1)
            at = k * GROUPS + g
            index_ref[pl.ds(at, 1), :] = jnp.bitwise_and(cell, LANES - 1).astype(F32)
            index_ref[pl.ds(at + 16, 1), :] = part.astype(F32)

    for k in range(BLOCKS):
        for i, ref in enumerate((value_ref, var_ref, taper_ref)):
            obs_ref[pl.ds(i * BLOCKS + k, 1), :] = block_row(ref, order[k], pl.ds(0, OBS))
        region = block_row(region_ref, order[k], pl.ds(0, OBS))
        place = jnp.where(jnp.bitwise_and(region, 1) == gy, 0, GX) + jnp.right_shift(region, 1)
        obs_ref[pl.ds(3 * BLOCKS + k, 1), :] = place.astype(F32)

    index_ref[pl.ds(32, 8), :] = jnp.zeros((8, LANES), F32)
    for i in range(QUARTER):
        tile = q * QUARTER + i
        b, g = order[tile // GROUPS], tile % GROUPS
        row = block_row(taper_ref, b, pl.ds(0, LANES))
        for j in range(1, GROUPS):
            row = jnp.where(g == j, block_row(taper_ref, b, pl.ds(j * LANES, LANES)), row)
        index_ref[pl.ds(32 + i, 1), :] = row


def weights_kernel(parts_ref, weights_ref):
    for i in range(QUARTER):
        weights_ref[pl.ds(i * GX, GX), :] = parts_ref[pl.ds(CHUNK + i, GX, stride=SENT), :]


def owner_kernel(parts_ref, out_ref):
    total = parts_ref[pl.ds(0, 8 * SENT), :]
    for i in range(1, GX // 8):
        total = total + parts_ref[pl.ds(i * 8 * SENT, 8 * SENT), :]
    part = total[0:CHUNK]
    for i in range(1, 8):
        part = part + total[i * SENT : i * SENT + CHUNK]
    eight = jnp.concatenate([part] * 8, axis=0)
    for i in range(GX * MA // 8):
        out_ref[pl.ds(i * 8 * CHUNK, 8 * CHUNK), :] = eight


def tapers_kernel(own_ref, other_ref, obs_ref, out_ref):
    q = lax.axis_index("ma")
    for shift in range(MA):
        for i in range(QUARTER):
            tile = jnp.bitwise_and(q - shift, MA - 1) * QUARTER + i
            for side, ref in enumerate((own_ref, other_ref)):
                high, low = split(ref[pl.ds((shift * QUARTER + i) * GX, GX), :])
                at = pl.multiple_of(tile * 2 * LANES, 2 * LANES) + side * GX
                out_ref[pl.ds(pl.multiple_of(at, GX), GX), :] = high
                out_ref[pl.ds(pl.multiple_of(at + LANES, GX), GX), :] = low

    rows = lax.broadcasted_iota(jnp.int32, (LANES, LANES), 0).astype(F32)
    for k in range(1, BLOCKS):
        for g in range(GROUPS):
            place = obs_ref[pl.ds(3 * BLOCKS + k, 1), pl.ds(g * LANES, LANES)]
            hot = (rows == jnp.broadcast_to(place, (LANES, LANES))).astype(F32).T.astype(BF16)
            out_ref[pl.ds(TAPERS + ((k - 1) * GROUPS + g) * LANES, LANES), :] = hot


def filter_kernel(
    came_ref,
    came_o_ref,
    tapers,
    obs_ref,
    gathered_1,
    gathered_2,
    gathered_3,
    state_ref,
    out_ref,
    xt,
    b_high,
    b_both,
    increments,
):
    gy = lax.axis_index("gy")
    denom = MEMBERS - 1.0

    def load_half(ref, half):
        for g in range(16):
            block = jnp.concatenate(
                [ref[pl.ds(g * CHUNK + i, 16, stride=16 * CHUNK), :] for i in range(CHUNK)], axis=0
            )
            mean = jnp.mean(block, axis=0, keepdims=True)
            full = jnp.concatenate(
                [block - mean, mean, jnp.zeros((LANES - MEMBERS - 1, LANES), F32)], axis=0
            )
            xt[pl.ds((half * 16 + g) * LANES, LANES), :] = full.T

    @pl.when(gy == 0)
    def _():
        load_half(came_ref, 0)
        load_half(came_o_ref, 1)

    @pl.when(gy == 1)
    def _():
        load_half(came_o_ref, 0)
        load_half(came_ref, 1)

    lane = lax.broadcasted_iota(jnp.int32, (ROWS_O, LANES), 1)
    member_row = lax.broadcasted_iota(jnp.int32, (LANES, OBS), 0)
    increments[...] = jnp.zeros((LANES, LANES), F32)
    for k in range(BLOCKS):
        now = jnp.concatenate(
            [xt[pl.ds((k * GROUPS + g) * LANES, LANES), :].T for g in range(GROUPS)], axis=1
        )
        anomaly = jnp.where(member_row < MEMBERS, now, 0.0)
        mean = now[MEMBERS : MEMBERS + 1]
        variance = jnp.sum(anomaly * anomaly, axis=0, keepdims=True) / denom
        error_var = obs_ref[pl.ds(BLOCKS + k, 1), :]
        total_var = variance + error_var
        shrink = 1.0 / (1.0 + jnp.sqrt(error_var / total_var))
        scale = 1.0 / (denom * total_var)
        gain_mean = (obs_ref[pl.ds(k, 1), :] - mean) * scale
        gain = jnp.where(member_row == MEMBERS, gain_mean, -(shrink * scale) * anomaly)
        gain_high, gain_low = split(gain)

        tapered_high, tapered_low = split(anomaly * obs_ref[pl.ds(2 * BLOCKS + k, 1), :])
        mixing = (
            dot_nt(gain_high, tapered_high)
            + dot_nt(gain_low, tapered_high)
            + dot_nt(gain_high, tapered_low)
        )
        e = increments[...]
        increments[...] = e + mixing + jnp.dot(
            mixing, e, precision=lax.Precision.HIGHEST, preferred_element_type=F32
        )

        if k == BLOCKS - 1:
            continue
        a_high, a_low = split(anomaly)
        left = jnp.concatenate([a_high[:MEMBERS], a_high[:MEMBERS], a_low[:MEMBERS], jnp.zeros((16, OBS), BF16)], axis=0)
        b_high[...] = gain_high.astype(F32).T.astype(BF16)
        b_both[:, pl.ds(0, LANES)] = b_high[...]
        b_both[:, pl.ds(LANES, LANES)] = gain_low.astype(F32).T.astype(BF16)

        def chunk(i, carry, k=k, left=left):
            taper = jnp.concatenate([tapers[pl.ds((k * GROUPS + g) * 2 * LANES, 2 * LANES), :] for g in range(GROUPS)], axis=1)
            at = pl.multiple_of((k + 1) * OBS + i * ROWS_O, ROWS_O)
            x = xt[pl.ds(at, ROWS_O), :]
            clean = jnp.where(lane < MEMBERS, x, 0.0)
            high = clean.astype(BF16).astype(F32)
            low = (clean - high)
            low_rolled = pltpu.roll(low, MEMBERS, 1)
            first = jnp.where(lane < MEMBERS, high, low_rolled)
            second = jnp.where(lane < 2 * MEMBERS - LANES, low_rolled, pltpu.roll(high, 2 * MEMBERS - LANES, 1))
            second = jnp.where(lane < 3 * MEMBERS - LANES, second, 0.0)
            query = jnp.concatenate([first, second], axis=1).astype(BF16)
            hot = tapers[pl.ds(pl.multiple_of(at + TAPERS - OBS, ROWS_O), ROWS_O), :]
            hot = jnp.concatenate([hot, hot], axis=1)
            weight = dot_nn(query, left) * dot_nn(hot, taper)
            w_high, w_low = split(weight)
            both = dot_nn(w_high, b_both[...])
            xt[pl.ds(at, ROWS_O), :] = (
                x + both[:, :LANES] + both[:, LANES:] + dot_nn(w_low, b_high[...])
            )
            return carry

        lax.fori_loop(0, (BLOCKS - 1 - k) * OBS // ROWS_O, chunk, 0)

    q = lax.axis_index("ma")
    e = increments[...]
    total = e + e[MEMBERS : MEMBERS + 1]
    row = lax.broadcasted_iota(jnp.int32, (24, LANES), 0)
    col = lax.broadcasted_iota(jnp.int32, (24, LANES), 1)
    fifth = sum(jnp.where(row >= i * CHUNK, 1, 0) for i in range(1, MA))
    member = (row - fifth * CHUNK) * 16 + q * MA + fifth
    chosen = jnp.where((col == member) & (row < OWN), 1.0, 0.0)
    transform = jnp.dot(chosen, total, precision=lax.Precision.HIGHEST, preferred_element_type=F32)
    row = lax.broadcasted_iota(jnp.int32, (LANES, LANES), 0)
    col = lax.broadcasted_iota(jnp.int32, (LANES, LANES), 1)
    back = sum(jnp.where(col >= i * OWN, 1, 0) for i in range(1, MA))
    place = col - back * OWN
    fifth = sum(jnp.where(place >= i * CHUNK, 1, 0) for i in range(1, MA))
    member = (place - fifth * CHUNK) * 16 + jnp.bitwise_and(q - back, MA - 1) * MA + fifth
    shuffle = jnp.where((row == member) & (col < MEMBERS), 1.0, 0.0)
    transform = jnp.dot(transform, shuffle, precision=lax.Precision.HIGHEST, preferred_element_type=F32)
    tiles = []
    for c in range(8):
        at = pl.ds(c, OWN, stride=8)
        tile = jnp.concatenate(
            [ref[at, :] for ref in (state_ref, gathered_1, gathered_2, gathered_3)], axis=0
        )
        tiles.append(tile - jnp.mean(tile, axis=0, keepdims=True))
    centered = jnp.concatenate(
        [jnp.concatenate(tiles, axis=1), jnp.zeros((LANES - MEMBERS, CELLS), F32)], axis=0
    )
    update = jnp.dot(transform, centered, precision=lax.Precision.HIGHEST, preferred_element_type=F32)
    for c in range(8):
        at = pl.ds(c, OWN, stride=8)
        out_ref[at, :] = state_ref[at, :] + update[:OWN, c * LANES : (c + 1) * LANES]


def other_core(x):
    return lax.ppermute(x, "gy", [(0, 1), (1, 0)])


def params(mebibytes):
    return pltpu.CompilerParams(vmem_limit_bytes=mebibytes * 1024 * 1024)


def over_members(x):
    return [lax.ppermute(x, "ma", [(i, (i + s) % MA) for i in range(MA)]) for s in range(1, MA)]


def local(
    ensemble, wind_field, obs_value, obs_var, obs_region, obs_cell, block_order, localization
):
    both = jnp.concatenate([ensemble, wind_field], axis=0)
    forward = [(i, (i + 1) % GX) for i in range(GX)]
    backward = [(i, (i - 1) % GX) for i in range(GX)]
    low = lax.ppermute(both[:, :, 2:], "gx", forward)
    high = lax.ppermute(both[:, :, :2], "gx", backward)
    prepared = pl.pallas_call(
        prepare_kernel,
        out_shape=(
            jax.ShapeDtypeStruct((40, LANES), F32),
            jax.ShapeDtypeStruct((4 * BLOCKS, OBS), F32),
        ),
        in_specs=[pl.BlockSpec(memory_space=pltpu.HBM)] * 6,
        out_specs=(VMEM,) * 2,
        scratch_shapes=[pltpu.SMEM((BLOCKS,), jnp.int32)]
        + [pltpu.VMEM((BLOCKS, OBS), jnp.int32)] * 2
        + [pltpu.VMEM((BLOCKS, OBS), F32)] * 3
        + [pltpu.SemaphoreType.DMA((6,))],
        compiler_params=params(60),
        cost_estimate=pl.CostEstimate(flops=10_000_000, bytes_accessed=2_000_000, transcendentals=0),
        name="prepare",
    )(block_order, obs_cell, obs_region, obs_value, obs_var, localization.reshape(BLOCKS, OBS))
    low, high, prepared = lax.optimization_barrier((low, high, prepared))
    index, observed = prepared
    own = jnp.concatenate([low, both, high], axis=2).reshape(-1, LANES)
    beside = other_core(own)

    state, picked = pl.pallas_call(
        advect_kernel,
        out_shape=(
            jax.ShapeDtypeStruct((OWN * 8, LANES), F32),
            jax.ShapeDtypeStruct((GX * SENT, LANES), F32),
        ),
        in_specs=[VMEM] * 3,
        out_specs=(VMEM, VMEM),
        scratch_shapes=[pltpu.VMEM((2, 24 * 8, LANES), F32)],
        compiler_params=params(4),
        cost_estimate=pl.CostEstimate(flops=10_000_000, bytes_accessed=1_000_000, transcendentals=0),
        name="advect",
    )(own, beside, index)

    parts = lax.all_to_all(picked.reshape(GX, 1, SENT * LANES), "gx", 0, 0, tiled=True)
    gathered = over_members(state)
    parts, gathered = lax.optimization_barrier((parts, gathered))
    parts = parts.reshape(-1, LANES)
    owned = pl.pallas_call(
        owner_kernel,
        out_shape=jax.ShapeDtypeStruct((MA * GX * CHUNK, LANES), F32),
        in_specs=[VMEM],
        out_specs=VMEM,
        compiler_params=params(4),
        name="owner",
    )(parts)
    weights = pl.pallas_call(
        weights_kernel,
        out_shape=jax.ShapeDtypeStruct((QUARTER * GX, LANES), F32),
        in_specs=[VMEM],
        out_specs=VMEM,
        compiler_params=params(4),
        name="weights",
    )(parts)
    came = lax.all_to_all(
        owned.reshape(MA * GX, 1, CHUNK * LANES), ("ma", "gx"), 0, 0, tiled=True
    ).reshape(-1, LANES)
    weights = jnp.concatenate([weights] + over_members(weights), axis=0)
    tapers = pl.pallas_call(
        tapers_kernel,
        out_shape=jax.ShapeDtypeStruct((TAPERS + (BLOCKS - 1) * OBS, LANES), BF16),
        in_specs=[VMEM] * 3,
        out_specs=VMEM,
        compiler_params=params(4),
        name="tapers",
    )(weights, other_core(weights), observed)
    came, tapers = lax.optimization_barrier((came, tapers))
    came_beside = other_core(came)

    out = pl.pallas_call(
        filter_kernel,
        out_shape=jax.ShapeDtypeStruct((OWN * 8, LANES), F32),
        in_specs=[VMEM] * 8,
        out_specs=VMEM,
        scratch_shapes=[
            pltpu.VMEM((BLOCKS * OBS, LANES), F32),
            pltpu.VMEM((OBS, LANES), BF16),
            pltpu.VMEM((OBS, 2 * LANES), BF16),
            pltpu.VMEM((LANES, LANES), F32),
        ],
        compiler_params=params(32),
        cost_estimate=pl.CostEstimate(flops=3_000_000_000, bytes_accessed=4_000_000, transcendentals=0),
        name="filter",
    )(came, came_beside, tapers, observed, *gathered, state)
    return out.reshape(ensemble.shape)


def solution(mesh):
    in_specs = (
        P("ma", None, "gx", "gy"),
        P(None, None, "gx", "gy"),
        P(),
        P(),
        P(),
        P(),
        P(),
        P("gx", "gy", None, None),
    )
    out_specs = P("ma", None, "gx", "gy")
    return jax.shard_map(local, mesh=mesh, in_specs=in_specs, out_specs=out_specs, check_vma=False)
```

```python
import jax
import jax.numpy as jnp
from jax import lax
from jax.experimental import pallas as pl
from jax.experimental.pallas import tpu as pltpu
from jax.sharding import PartitionSpec as P

MEMBERS = 80
OWN = 20
BLOCKS = 4
OBS = 1024
CELLS = 1024
GX = 64
MA = 4
LANES = 128
GROUPS = OBS // LANES
KAPPA = 0.025
CHUNK = 5
HALF = OWN * 2 * GROUPS
QUARTER = (BLOCKS - 1) * GROUPS // MA
SENT = CHUNK + QUARTER
TAPERS = (BLOCKS - 1) * GROUPS * 2 * LANES
ROWS_O = 256
F32 = jnp.float32
BF16 = jnp.bfloat16
VMEM = pl.BlockSpec(memory_space=pltpu.VMEM)
SMEM = pl.BlockSpec(memory_space=pltpu.SMEM)


def split(value):
    high = value.astype(BF16)
    return high, (value - high.astype(F32)).astype(BF16)


def dot_nn(a, b):
    return lax.dot_general(a, b, (((1,), (0,)), ((), ())), preferred_element_type=F32)


def dot_nt(a, b):
    return lax.dot_general(a, b, (((1,), (1,)), ((), ())), preferred_element_type=F32)


def block_row(ref, b, columns):
    row = ref[pl.ds(0, 1), columns]
    for i in range(1, BLOCKS):
        row = jnp.where(b == i, ref[pl.ds(i, 1), columns], row)
    return row


def advect_kernel(own_ref, other_ref, index_ref, state_ref, picked_ref, work):
    lane = lax.broadcasted_iota(jnp.int32, (8, LANES), 1)
    first, last = lane == 0, lane == LANES - 1

    def step(q, beside, wind):
        u_up, u_down, v_up, v_down = wind
        west, east = pltpu.roll(q, 1, 0), pltpu.roll(q, 7, 0)
        south = jnp.where(first, pltpu.roll(beside, 1, 1), pltpu.roll(q, 1, 1))
        north = jnp.where(last, pltpu.roll(beside, LANES - 1, 1), pltpu.roll(q, LANES - 1, 1))
        return (
            q
            - u_up * (q - west)
            - u_down * (east - q)
            - v_up * (q - south)
            - v_down * (north - q)
            + KAPPA * (east + west + north + south - 4.0 * q)
        )

    def winds(ref, level):
        u = ref[pl.ds((OWN * 2 + level) * 8, 8), :]
        v = ref[pl.ds((OWN * 2 + 2 + level) * 8, 8), :]
        return jnp.maximum(u, 0.0), jnp.minimum(u, 0.0), jnp.maximum(v, 0.0), jnp.minimum(v, 0.0)

    for side in range(2):
        work[side, pl.ds(OWN * 8, 32), :] = jnp.zeros((32, LANES), F32)
    for level in range(2):
        wind, wind_o = winds(own_ref, level), winds(other_ref, level)
        for m in range(OWN):
            at = (m * 2 + level) * 8
            q, q_o = own_ref[pl.ds(at, 8), :], other_ref[pl.ds(at, 8), :]
            once, once_o = step(q, q_o, wind), step(q_o, q, wind_o)
            twice, twice_o = step(once, once_o, wind), step(once_o, once, wind_o)
            at = pl.ds(m * 8 + level * 4, 4)
            state_ref[at, :] = twice[2:6]
            work[0, at, :] = twice[2:6]
            work[1, at, :] = twice_o[2:6]

    send = index_ref[pl.ds(32, QUARTER), :]
    for g in range(2 * GROUPS):
        y = jnp.broadcast_to(index_ref[pl.ds(g, 1), :].astype(jnp.int32), (24, LANES))
        part = jnp.broadcast_to(index_ref[pl.ds(g + 16, 1), :].astype(jnp.int32), (24, LANES))
        total = jnp.zeros((24, LANES), F32)
        for c in range(16):
            source = work[c // 8, pl.ds(c % 8, 24, stride=8), :]
            found = jnp.take_along_axis(source, y, axis=1, mode="promise_in_bounds")
            total = jnp.where(part == c, found, total)
        for i in range(MA):
            at = (i * 2 * GROUPS + g) * SENT
            picked_ref[pl.ds(at, CHUNK), :] = total[i * CHUNK : (i + 1) * CHUNK]
            picked_ref[pl.ds(at + CHUNK, QUARTER), :] = send


def prepare_kernel(*refs):
    sources, results, copies, done = refs[:6], refs[6:8], refs[8:14], refs[14]
    moves = [
        pltpu.make_async_copy(source, copy, done.at[i])
        for i, (source, copy) in enumerate(zip(sources, copies))
    ]
    for move in moves:
        move.start()
    for move in moves:
        move.wait()
    order, cell_ref, region_ref, value_ref, var_ref, taper_ref = copies
    index_ref, obs_ref = results
    gx, gy, q = lax.axis_index("gx"), lax.axis_index("gy"), lax.axis_index("ma")
    for k in range(2):
        b = order[gy * 2 + k]
        for g in range(GROUPS):
            columns = pl.ds(g * LANES, LANES)
            cell, region = block_row(cell_ref, b, columns), block_row(region_ref, b, columns)
            part = jnp.right_shift(cell, 7) + jnp.where(jnp.bitwise_and(region, 1) == gy, 0, 8)
            part = jnp.where(jnp.right_shift(region, 1) == gx, part, -1)
            at = k * GROUPS + g
            index_ref[pl.ds(at, 1), :] = jnp.bitwise_and(cell, LANES - 1).astype(F32)
            index_ref[pl.ds(at + 16, 1), :] = part.astype(F32)

    for k in range(BLOCKS):
        for i, ref in enumerate((value_ref, var_ref, taper_ref)):
            obs_ref[pl.ds(i * BLOCKS + k, 1), :] = block_row(ref, order[k], pl.ds(0, OBS))
        region = block_row(region_ref, order[k], pl.ds(0, OBS))
        place = jnp.where(jnp.bitwise_and(region, 1) == gy, 0, GX) + jnp.right_shift(region, 1)
        obs_ref[pl.ds(3 * BLOCKS + k, 1), :] = place.astype(F32)

    index_ref[pl.ds(32, 8), :] = jnp.zeros((8, LANES), F32)
    for i in range(QUARTER):
        tile = q * QUARTER + i
        b, g = order[tile // GROUPS], tile % GROUPS
        row = block_row(taper_ref, b, pl.ds(0, LANES))
        for j in range(1, GROUPS):
            row = jnp.where(g == j, block_row(taper_ref, b, pl.ds(j * LANES, LANES)), row)
        index_ref[pl.ds(32 + i, 1), :] = row


def weights_kernel(parts_ref, state_ref, out_ref):
    for i in range(QUARTER):
        out_ref[pl.ds(i * GX, GX), :] = parts_ref[pl.ds(CHUNK + i, GX, stride=SENT), :]
    out_ref[pl.ds(QUARTER * GX, OWN * 8), :] = state_ref[...]


def merge_kernel(*refs):
    weights_ref, state_ref = refs[MA:]
    for i in range(MA):
        weights_ref[pl.ds(i * QUARTER * GX, QUARTER * GX), :] = refs[i][pl.ds(0, QUARTER * GX), :]
        state_ref[pl.ds(i * OWN * 8, OWN * 8), :] = refs[i][pl.ds(QUARTER * GX, OWN * 8), :]


def owner_kernel(parts_ref, out_ref):
    total = parts_ref[pl.ds(0, 8 * SENT), :]
    for i in range(1, GX // 8):
        total = total + parts_ref[pl.ds(i * 8 * SENT, 8 * SENT), :]
    part = total[0:CHUNK]
    for i in range(1, 8):
        part = part + total[i * SENT : i * SENT + CHUNK]
    eight = jnp.concatenate([part] * 8, axis=0)
    for i in range(GX * MA // 8):
        out_ref[pl.ds(i * 8 * CHUNK, 8 * CHUNK), :] = eight


def tapers_kernel(own_ref, other_ref, obs_ref, out_ref):
    q = lax.axis_index("ma")
    for shift in range(MA):
        for i in range(QUARTER):
            tile = jnp.bitwise_and(q - shift, MA - 1) * QUARTER + i
            for side, ref in enumerate((own_ref, other_ref)):
                high, low = split(ref[pl.ds((shift * QUARTER + i) * GX, GX), :])
                at = pl.multiple_of(tile * 2 * LANES, 2 * LANES) + side * GX
                out_ref[pl.ds(pl.multiple_of(at, GX), GX), :] = high
                out_ref[pl.ds(pl.multiple_of(at + LANES, GX), GX), :] = low

    rows = lax.broadcasted_iota(jnp.int32, (LANES, LANES), 0).astype(F32)
    for k in range(1, BLOCKS):
        for g in range(GROUPS):
            place = obs_ref[pl.ds(3 * BLOCKS + k, 1), pl.ds(g * LANES, LANES)]
            hot = (rows == jnp.broadcast_to(place, (LANES, LANES))).astype(F32).T.astype(BF16)
            out_ref[pl.ds(TAPERS + ((k - 1) * GROUPS + g) * LANES, LANES), :] = hot


def filter_kernel(
    came_ref,
    came_o_ref,
    tapers,
    obs_ref,
    state_ref,
    out_ref,
    xt,
    b_high,
    b_both,
    increments,
):
    gy = lax.axis_index("gy")
    denom = MEMBERS - 1.0

    def load_half(ref, half):
        for g in range(16):
            block = jnp.concatenate(
                [ref[pl.ds(g * CHUNK + i, 16, stride=16 * CHUNK), :] for i in range(CHUNK)], axis=0
            )
            mean = jnp.mean(block, axis=0, keepdims=True)
            full = jnp.concatenate(
                [block - mean, mean, jnp.zeros((LANES - MEMBERS - 1, LANES), F32)], axis=0
            )
            xt[pl.ds((half * 16 + g) * LANES, LANES), :] = full.T

    @pl.when(gy == 0)
    def _():
        load_half(came_ref, 0)
        load_half(came_o_ref, 1)

    @pl.when(gy == 1)
    def _():
        load_half(came_o_ref, 0)
        load_half(came_ref, 1)

    lane = lax.broadcasted_iota(jnp.int32, (ROWS_O, LANES), 1)
    member_row = lax.broadcasted_iota(jnp.int32, (LANES, OBS), 0)
    increments[...] = jnp.zeros((LANES, LANES), F32)
    for k in range(BLOCKS):
        now = jnp.concatenate(
            [xt[pl.ds((k * GROUPS + g) * LANES, LANES), :].T for g in range(GROUPS)], axis=1
        )
        anomaly = jnp.where(member_row < MEMBERS, now, 0.0)
        mean = now[MEMBERS : MEMBERS + 1]
        variance = jnp.sum(anomaly * anomaly, axis=0, keepdims=True) / denom
        error_var = obs_ref[pl.ds(BLOCKS + k, 1), :]
        total_var = variance + error_var
        shrink = 1.0 / (1.0 + jnp.sqrt(error_var / total_var))
        scale = 1.0 / (denom * total_var)
        gain_mean = (obs_ref[pl.ds(k, 1), :] - mean) * scale
        gain = jnp.where(member_row == MEMBERS, gain_mean, -(shrink * scale) * anomaly)
        gain_high, gain_low = split(gain)

        tapered_high, tapered_low = split(anomaly * obs_ref[pl.ds(2 * BLOCKS + k, 1), :])
        mixing = (
            dot_nt(gain_high, tapered_high)
            + dot_nt(gain_low, tapered_high)
            + dot_nt(gain_high, tapered_low)
        )
        e = increments[...]
        increments[...] = e + mixing + jnp.dot(
            mixing, e, precision=lax.Precision.HIGHEST, preferred_element_type=F32
        )

        if k == BLOCKS - 1:
            continue
        a_high, a_low = split(anomaly)
        left = jnp.concatenate([a_high[:MEMBERS], a_high[:MEMBERS], a_low[:MEMBERS], jnp.zeros((16, OBS), BF16)], axis=0)
        b_high[...] = gain_high.astype(F32).T.astype(BF16)
        b_both[:, pl.ds(0, LANES)] = b_high[...]
        b_both[:, pl.ds(LANES, LANES)] = gain_low.astype(F32).T.astype(BF16)

        def chunk(i, carry, k=k, left=left):
            taper = jnp.concatenate([tapers[pl.ds((k * GROUPS + g) * 2 * LANES, 2 * LANES), :] for g in range(GROUPS)], axis=1)
            at = pl.multiple_of((k + 1) * OBS + i * ROWS_O, ROWS_O)
            x = xt[pl.ds(at, ROWS_O), :]
            clean = jnp.where(lane < MEMBERS, x, 0.0)
            high = clean.astype(BF16).astype(F32)
            low = (clean - high)
            low_rolled = pltpu.roll(low, MEMBERS, 1)
            first = jnp.where(lane < MEMBERS, high, low_rolled)
            second = jnp.where(lane < 2 * MEMBERS - LANES, low_rolled, pltpu.roll(high, 2 * MEMBERS - LANES, 1))
            second = jnp.where(lane < 3 * MEMBERS - LANES, second, 0.0)
            query = jnp.concatenate([first, second], axis=1).astype(BF16)
            hot = tapers[pl.ds(pl.multiple_of(at + TAPERS - OBS, ROWS_O), ROWS_O), :]
            hot = jnp.concatenate([hot, hot], axis=1)
            weight = dot_nn(query, left) * dot_nn(hot, taper)
            w_high, w_low = split(weight)
            both = dot_nn(w_high, b_both[...])
            xt[pl.ds(at, ROWS_O), :] = (
                x + both[:, :LANES] + both[:, LANES:] + dot_nn(w_low, b_high[...])
            )
            return carry

        lax.fori_loop(0, (BLOCKS - 1 - k) * OBS // ROWS_O, chunk, 0)

    q = lax.axis_index("ma")
    e = increments[...]
    total = e + e[MEMBERS : MEMBERS + 1]
    row = lax.broadcasted_iota(jnp.int32, (24, LANES), 0)
    col = lax.broadcasted_iota(jnp.int32, (24, LANES), 1)
    fifth = sum(jnp.where(row >= i * CHUNK, 1, 0) for i in range(1, MA))
    member = (row - fifth * CHUNK) * 16 + q * MA + fifth
    chosen = jnp.where((col == member) & (row < OWN), 1.0, 0.0)
    transform = jnp.dot(chosen, total, precision=lax.Precision.HIGHEST, preferred_element_type=F32)
    row = lax.broadcasted_iota(jnp.int32, (LANES, LANES), 0)
    col = lax.broadcasted_iota(jnp.int32, (LANES, LANES), 1)
    back = sum(jnp.where(col >= i * OWN, 1, 0) for i in range(1, MA))
    place = col - back * OWN
    fifth = sum(jnp.where(place >= i * CHUNK, 1, 0) for i in range(1, MA))
    member = (place - fifth * CHUNK) * 16 + jnp.bitwise_and(q - back, MA - 1) * MA + fifth
    shuffle = jnp.where((row == member) & (col < MEMBERS), 1.0, 0.0)
    transform = jnp.dot(transform, shuffle, precision=lax.Precision.HIGHEST, preferred_element_type=F32)
    tiles = []
    for c in range(8):
        tile = state_ref[pl.ds(c, MEMBERS, stride=8), :]
        tiles.append(tile - jnp.mean(tile, axis=0, keepdims=True))
    centered = jnp.concatenate(
        [jnp.concatenate(tiles, axis=1), jnp.zeros((LANES - MEMBERS, CELLS), F32)], axis=0
    )
    update = jnp.dot(transform, centered, precision=lax.Precision.HIGHEST, preferred_element_type=F32)
    for c in range(8):
        at = pl.ds(c, OWN, stride=8)
        out_ref[at, :] = state_ref[at, :] + update[:OWN, c * LANES : (c + 1) * LANES]


def other_core(x):
    return lax.ppermute(x, "gy", [(0, 1), (1, 0)])


def params(mebibytes):
    return pltpu.CompilerParams(vmem_limit_bytes=mebibytes * 1024 * 1024)


def over_members(x):
    return [lax.ppermute(x, "ma", [(i, (i + s) % MA) for i in range(MA)]) for s in range(1, MA)]


def local(
    ensemble, wind_field, obs_value, obs_var, obs_region, obs_cell, block_order, localization
):
    both = jnp.concatenate([ensemble, wind_field], axis=0)
    forward = [(i, (i + 1) % GX) for i in range(GX)]
    backward = [(i, (i - 1) % GX) for i in range(GX)]
    low = lax.ppermute(both[:, :, 2:], "gx", forward)
    high = lax.ppermute(both[:, :, :2], "gx", backward)
    prepared = pl.pallas_call(
        prepare_kernel,
        out_shape=(
            jax.ShapeDtypeStruct((40, LANES), F32),
            jax.ShapeDtypeStruct((4 * BLOCKS, OBS), F32),
        ),
        in_specs=[pl.BlockSpec(memory_space=pltpu.HBM)] * 6,
        out_specs=(VMEM,) * 2,
        scratch_shapes=[pltpu.SMEM((BLOCKS,), jnp.int32)]
        + [pltpu.VMEM((BLOCKS, OBS), jnp.int32)] * 2
        + [pltpu.VMEM((BLOCKS, OBS), F32)] * 3
        + [pltpu.SemaphoreType.DMA((6,))],
        compiler_params=params(60),
        cost_estimate=pl.CostEstimate(flops=10_000_000, bytes_accessed=2_000_000, transcendentals=0),
        name="prepare",
    )(block_order, obs_cell, obs_region, obs_value, obs_var, localization.reshape(BLOCKS, OBS))
    low, high, prepared = lax.optimization_barrier((low, high, prepared))
    index, observed = prepared
    own = jnp.concatenate([low, both, high], axis=2).reshape(-1, LANES)
    beside = other_core(own)

    state, picked = pl.pallas_call(
        advect_kernel,
        out_shape=(
            jax.ShapeDtypeStruct((OWN * 8, LANES), F32),
            jax.ShapeDtypeStruct((GX * SENT, LANES), F32),
        ),
        in_specs=[VMEM] * 3,
        out_specs=(VMEM, VMEM),
        scratch_shapes=[pltpu.VMEM((2, 24 * 8, LANES), F32)],
        compiler_params=params(4),
        cost_estimate=pl.CostEstimate(flops=10_000_000, bytes_accessed=1_000_000, transcendentals=0),
        name="advect",
    )(own, beside, index)

    parts = lax.all_to_all(picked.reshape(GX, 1, SENT * LANES), "gx", 0, 0, tiled=True)
    parts = parts.reshape(-1, LANES)
    owned = pl.pallas_call(
        owner_kernel,
        out_shape=jax.ShapeDtypeStruct((MA * GX * CHUNK, LANES), F32),
        in_specs=[VMEM],
        out_specs=VMEM,
        compiler_params=params(4),
        name="owner",
    )(parts)
    parts, owned = lax.optimization_barrier((parts, owned))
    weights = pl.pallas_call(
        weights_kernel,
        out_shape=jax.ShapeDtypeStruct((QUARTER * GX + OWN * 8, LANES), F32),
        in_specs=[VMEM, VMEM],
        out_specs=VMEM,
        compiler_params=params(4),
        cost_estimate=pl.CostEstimate(flops=1000, bytes_accessed=1000, transcendentals=0),
        name="weights",
    )(parts, state)
    came = lax.all_to_all(
        owned.reshape(MA * GX, 1, CHUNK * LANES), ("ma", "gx"), 0, 0, tiled=True
    ).reshape(-1, LANES)
    members = [weights] + over_members(weights)
    weights, gathered = pl.pallas_call(
        merge_kernel,
        out_shape=(
            jax.ShapeDtypeStruct((MA * QUARTER * GX, LANES), F32),
            jax.ShapeDtypeStruct((MEMBERS * 8, LANES), F32),
        ),
        in_specs=[VMEM] * MA,
        out_specs=(VMEM, VMEM),
        compiler_params=params(4),
        cost_estimate=pl.CostEstimate(flops=1000, bytes_accessed=1000, transcendentals=0),
        name="merge",
    )(*members)
    tapers = pl.pallas_call(
        tapers_kernel,
        out_shape=jax.ShapeDtypeStruct((TAPERS + (BLOCKS - 1) * OBS, LANES), BF16),
        in_specs=[VMEM] * 3,
        out_specs=VMEM,
        compiler_params=params(4),
        cost_estimate=pl.CostEstimate(flops=1000, bytes_accessed=1000, transcendentals=0),
        name="tapers",
    )(weights, other_core(weights), observed)
    came, tapers, gathered = lax.optimization_barrier((came, tapers, gathered))
    came_beside = other_core(came)

    out = pl.pallas_call(
        filter_kernel,
        out_shape=jax.ShapeDtypeStruct((OWN * 8, LANES), F32),
        in_specs=[VMEM] * 5,
        out_specs=VMEM,
        scratch_shapes=[
            pltpu.VMEM((BLOCKS * OBS, LANES), F32),
            pltpu.VMEM((OBS, LANES), BF16),
            pltpu.VMEM((OBS, 2 * LANES), BF16),
            pltpu.VMEM((LANES, LANES), F32),
        ],
        compiler_params=params(16),
        cost_estimate=pl.CostEstimate(flops=3_000_000_000, bytes_accessed=4_000_000, transcendentals=0),
        name="filter",
    )(came, came_beside, tapers, observed, gathered)
    return out.reshape(ensemble.shape)


def solution(mesh):
    in_specs = (
        P("ma", None, "gx", "gy"),
        P(None, None, "gx", "gy"),
        P(),
        P(),
        P(),
        P(),
        P(),
        P("gx", "gy", None, None),
    )
    out_specs = P("ma", None, "gx", "gy")
    return jax.shard_map(local, mesh=mesh, in_specs=in_specs, out_specs=out_specs, check_vma=False)
```

```python
import jax
import jax.numpy as jnp
from jax import lax
from jax.experimental import pallas as pl
from jax.experimental.pallas import tpu as pltpu
from jax.sharding import PartitionSpec as P

MEMBERS = 80
OWN = 20
BLOCKS = 4
OBS = 1024
CELLS = 1024
GX = 64
MA = 4
LANES = 128
GROUPS = OBS // LANES
KAPPA = 0.025
CHUNK = 5
HALF = OWN * 2 * GROUPS
QUARTER = (BLOCKS - 1) * GROUPS // MA
SENT = CHUNK + QUARTER
TAPERS = (BLOCKS - 1) * GROUPS * 2 * LANES
ROWS_O = 1024
F32 = jnp.float32
BF16 = jnp.bfloat16
VMEM = pl.BlockSpec(memory_space=pltpu.VMEM)
SMEM = pl.BlockSpec(memory_space=pltpu.SMEM)


def split(value):
    high = value.astype(BF16)
    return high, (value - high.astype(F32)).astype(BF16)


def dot_nn(a, b):
    return lax.dot_general(a, b, (((1,), (0,)), ((), ())), preferred_element_type=F32)


def dot_nt(a, b):
    return lax.dot_general(a, b, (((1,), (1,)), ((), ())), preferred_element_type=F32)


def block_row(ref, b, columns):
    row = ref[pl.ds(0, 1), columns]
    for i in range(1, BLOCKS):
        row = jnp.where(b == i, ref[pl.ds(i, 1), columns], row)
    return row


def advect_kernel(own_ref, other_ref, index_ref, state_ref, picked_ref, work):
    lane = lax.broadcasted_iota(jnp.int32, (8, LANES), 1)
    first, last = lane == 0, lane == LANES - 1

    def step(q, beside, wind):
        u_up, u_down, v_up, v_down = wind
        west, east = pltpu.roll(q, 1, 0), pltpu.roll(q, 7, 0)
        south = jnp.where(first, pltpu.roll(beside, 1, 1), pltpu.roll(q, 1, 1))
        north = jnp.where(last, pltpu.roll(beside, LANES - 1, 1), pltpu.roll(q, LANES - 1, 1))
        return (
            q
            - u_up * (q - west)
            - u_down * (east - q)
            - v_up * (q - south)
            - v_down * (north - q)
            + KAPPA * (east + west + north + south - 4.0 * q)
        )

    def winds(ref, level):
        u = ref[pl.ds((OWN * 2 + level) * 8, 8), :]
        v = ref[pl.ds((OWN * 2 + 2 + level) * 8, 8), :]
        return jnp.maximum(u, 0.0), jnp.minimum(u, 0.0), jnp.maximum(v, 0.0), jnp.minimum(v, 0.0)

    for side in range(2):
        work[side, pl.ds(OWN * 8, 32), :] = jnp.zeros((32, LANES), F32)
    for level in range(2):
        wind, wind_o = winds(own_ref, level), winds(other_ref, level)
        for m in range(OWN):
            at = (m * 2 + level) * 8
            q, q_o = own_ref[pl.ds(at, 8), :], other_ref[pl.ds(at, 8), :]
            once, once_o = step(q, q_o, wind), step(q_o, q, wind_o)
            twice, twice_o = step(once, once_o, wind), step(once_o, once, wind_o)
            at = pl.ds(m * 8 + level * 4, 4)
            state_ref[at, :] = twice[2:6]
            work[0, at, :] = twice[2:6]
            work[1, at, :] = twice_o[2:6]

    eight = jnp.concatenate(
        [jnp.zeros((CHUNK, LANES), F32), index_ref[pl.ds(32, QUARTER), :]] * 8, axis=0
    )
    for i in range(GX // 8):
        picked_ref[pl.ds(i * 8 * SENT, 8 * SENT), :] = eight
    for half in range(2):
        groups = range(half * GROUPS, (half + 1) * GROUPS)
        ys = [jnp.broadcast_to(index_ref[pl.ds(g, 1), :].astype(jnp.int32), (24, LANES)) for g in groups]
        parts = [jnp.broadcast_to(index_ref[pl.ds(g + 16, 1), :], (24, LANES)) for g in groups]
        totals = [jnp.zeros((24, LANES), F32)] * GROUPS
        for c in range(16):
            source = work[c // 8, pl.ds(c % 8, 24, stride=8), :]
            for j in range(GROUPS):
                found = jnp.take_along_axis(source, ys[j], axis=1, mode="promise_in_bounds")
                totals[j] = jnp.where(parts[j] == c, found, totals[j])
        for j, g in enumerate(groups):
            for i in range(MA):
                at = (i * 2 * GROUPS + g) * SENT
                picked_ref[pl.ds(at, CHUNK), :] = totals[j][i * CHUNK : (i + 1) * CHUNK]


def prepare_kernel(*refs):
    sources, results, copies, done = refs[:6], refs[6:8], refs[8:14], refs[14]
    moves = [
        pltpu.make_async_copy(source, copy, done.at[i])
        for i, (source, copy) in enumerate(zip(sources, copies))
    ]
    for move in moves:
        move.start()
    for move in moves:
        move.wait()
    order, cell_ref, region_ref, value_ref, var_ref, taper_ref = copies
    index_ref, obs_ref = results
    gx, gy, q = lax.axis_index("gx"), lax.axis_index("gy"), lax.axis_index("ma")
    for k in range(2):
        b = order[gy * 2 + k]
        for g in range(GROUPS):
            columns = pl.ds(g * LANES, LANES)
            cell, region = block_row(cell_ref, b, columns), block_row(region_ref, b, columns)
            part = jnp.right_shift(cell, 7) + jnp.where(jnp.bitwise_and(region, 1) == gy, 0, 8)
            part = jnp.where(jnp.right_shift(region, 1) == gx, part, -1)
            at = k * GROUPS + g
            index_ref[pl.ds(at, 1), :] = jnp.bitwise_and(cell, LANES - 1).astype(F32)
            index_ref[pl.ds(at + 16, 1), :] = part.astype(F32)

    for k in range(BLOCKS):
        for i, ref in enumerate((value_ref, var_ref, taper_ref)):
            obs_ref[pl.ds(i * BLOCKS + k, 1), :] = block_row(ref, order[k], pl.ds(0, OBS))
        region = block_row(region_ref, order[k], pl.ds(0, OBS))
        place = jnp.where(jnp.bitwise_and(region, 1) == gy, 0, GX) + jnp.right_shift(region, 1)
        obs_ref[pl.ds(3 * BLOCKS + k, 1), :] = place.astype(F32)

    index_ref[pl.ds(32, 8), :] = jnp.zeros((8, LANES), F32)
    for i in range(QUARTER):
        tile = q * QUARTER + i
        b, g = order[tile // GROUPS], tile % GROUPS
        row = block_row(taper_ref, b, pl.ds(0, LANES))
        for j in range(1, GROUPS):
            row = jnp.where(g == j, block_row(taper_ref, b, pl.ds(j * LANES, LANES)), row)
        index_ref[pl.ds(32 + i, 1), :] = row


def weights_kernel(parts_ref, weights_ref):
    for i in range(QUARTER):
        weights_ref[pl.ds(i * GX, GX), :] = parts_ref[pl.ds(CHUNK + i, GX, stride=SENT), :]


def owner_kernel(parts_ref, out_ref):
    total = parts_ref[pl.ds(0, 8 * SENT), :]
    for i in range(1, GX // 8):
        total = total + parts_ref[pl.ds(i * 8 * SENT, 8 * SENT), :]
    part = total[0:CHUNK]
    for i in range(1, 8):
        part = part + total[i * SENT : i * SENT + CHUNK]
    eight = jnp.concatenate([part] * 8, axis=0)
    for i in range(GX * MA // 8):
        out_ref[pl.ds(i * 8 * CHUNK, 8 * CHUNK), :] = eight


def tapers_kernel(own_ref, other_ref, obs_ref, out_ref):
    q = lax.axis_index("ma")
    for shift in range(MA):
        for i in range(QUARTER):
            tile = jnp.bitwise_and(q - shift, MA - 1) * QUARTER + i
            for side, ref in enumerate((own_ref, other_ref)):
                high, low = split(ref[pl.ds((shift * QUARTER + i) * GX, GX), :])
                at = pl.multiple_of(tile * 2 * LANES, 2 * LANES) + side * GX
                out_ref[pl.ds(pl.multiple_of(at, GX), GX), :] = high
                out_ref[pl.ds(pl.multiple_of(at + LANES, GX), GX), :] = low

    rows = lax.broadcasted_iota(jnp.int32, (LANES, LANES), 0).astype(F32)
    for k in range(1, BLOCKS):
        for g in range(GROUPS):
            place = obs_ref[pl.ds(3 * BLOCKS + k, 1), pl.ds(g * LANES, LANES)]
            hot = (rows == jnp.broadcast_to(place, (LANES, LANES))).astype(F32).T.astype(BF16)
            out_ref[pl.ds(TAPERS + ((k - 1) * GROUPS + g) * LANES, LANES), :] = hot


def filter_kernel(
    came_ref,
    came_o_ref,
    tapers,
    obs_ref,
    gathered_1,
    gathered_2,
    gathered_3,
    state_ref,
    out_ref,
    xt,
    b_high,
    b_both,
    increments,
    first_block,
):
    gy = lax.axis_index("gy")
    denom = MEMBERS - 1.0

    def load_half(ref, half):
        for g in range(16):
            block = jnp.concatenate(
                [ref[pl.ds(g * CHUNK + i, 16, stride=16 * CHUNK), :] for i in range(CHUNK)], axis=0
            )
            mean = jnp.mean(block, axis=0, keepdims=True)
            full = jnp.concatenate(
                [block - mean, mean, jnp.zeros((LANES - MEMBERS - 1, LANES), F32)], axis=0
            )
            if half == 0 and g < GROUPS:
                first_block[:, pl.ds(g * LANES, LANES)] = full
            else:
                xt[pl.ds((half * 16 + g) * LANES, LANES), :] = full.T

    @pl.when(gy == 0)
    def _():
        load_half(came_ref, 0)
        load_half(came_o_ref, 1)

    @pl.when(gy == 1)
    def _():
        load_half(came_o_ref, 0)
        load_half(came_ref, 1)

    lane = lax.broadcasted_iota(jnp.int32, (ROWS_O, LANES), 1)
    member_row = lax.broadcasted_iota(jnp.int32, (LANES, OBS), 0)
    increments[...] = jnp.zeros((LANES, LANES), F32)
    for k in range(BLOCKS):
        if k == 0:
            now = first_block[...]
        else:
            now = jnp.concatenate(
                [xt[pl.ds((k * GROUPS + g) * LANES, LANES), :].T for g in range(GROUPS)], axis=1
            )
        anomaly = jnp.where(member_row < MEMBERS, now, 0.0)
        mean = now[MEMBERS : MEMBERS + 1]
        variance = jnp.sum(anomaly * anomaly, axis=0, keepdims=True) / denom
        error_var = obs_ref[pl.ds(BLOCKS + k, 1), :]
        total_var = variance + error_var
        shrink = 1.0 / (1.0 + jnp.sqrt(error_var / total_var))
        scale = 1.0 / (denom * total_var)
        gain_mean = (obs_ref[pl.ds(k, 1), :] - mean) * scale
        gain = jnp.where(member_row == MEMBERS, gain_mean, -(shrink * scale) * anomaly)
        gain_high, gain_low = split(gain)

        tapered_high, tapered_low = split(anomaly * obs_ref[pl.ds(2 * BLOCKS + k, 1), :])
        mixing = (
            dot_nt(gain_high, tapered_high)
            + dot_nt(gain_low, tapered_high)
            + dot_nt(gain_high, tapered_low)
        )
        e = increments[...]
        increments[...] = e + mixing + jnp.dot(
            mixing, e, precision=lax.Precision.HIGHEST, preferred_element_type=F32
        )

        if k == BLOCKS - 1:
            continue
        a_high, a_low = split(anomaly)
        left = jnp.concatenate([a_high[:MEMBERS], a_high[:MEMBERS], a_low[:MEMBERS], jnp.zeros((16, OBS), BF16)], axis=0)
        b_high[...] = gain_high.astype(F32).T.astype(BF16)
        b_both[:, pl.ds(0, LANES)] = b_high[...]
        b_both[:, pl.ds(LANES, LANES)] = gain_low.astype(F32).T.astype(BF16)

        def chunk(i, carry, k=k, left=left):
            taper = jnp.concatenate([tapers[pl.ds((k * GROUPS + g) * 2 * LANES, 2 * LANES), :] for g in range(GROUPS)], axis=1)
            at = pl.multiple_of((k + 1) * OBS + i * ROWS_O, ROWS_O)
            x = xt[pl.ds(at, ROWS_O), :]
            clean = jnp.where(lane < MEMBERS, x, 0.0)
            high = clean.astype(BF16).astype(F32)
            low = (clean - high)
            low_rolled = pltpu.roll(low, MEMBERS, 1)
            first = jnp.where(lane < MEMBERS, high, low_rolled)
            second = jnp.where(lane < 2 * MEMBERS - LANES, low_rolled, pltpu.roll(high, 2 * MEMBERS - LANES, 1))
            second = jnp.where(lane < 3 * MEMBERS - LANES, second, 0.0)
            query = jnp.concatenate([first, second], axis=1).astype(BF16)
            hot = tapers[pl.ds(pl.multiple_of(at + TAPERS - OBS, ROWS_O), ROWS_O), :]
            hot = jnp.concatenate([hot, hot], axis=1)
            weight = dot_nn(query, left) * dot_nn(hot, taper)
            w_high, w_low = split(weight)
            both = dot_nn(w_high, b_both[...])
            xt[pl.ds(at, ROWS_O), :] = (
                x + both[:, :LANES] + both[:, LANES:] + dot_nn(w_low, b_high[...])
            )
            return carry

        lax.fori_loop(0, (BLOCKS - 1 - k) * OBS // ROWS_O, chunk, 0)

    q = lax.axis_index("ma")
    e = increments[...]
    total = e + e[MEMBERS : MEMBERS + 1]
    row = lax.broadcasted_iota(jnp.int32, (24, LANES), 0)
    col = lax.broadcasted_iota(jnp.int32, (24, LANES), 1)
    fifth = sum(jnp.where(row >= i * CHUNK, 1, 0) for i in range(1, MA))
    member = (row - fifth * CHUNK) * 16 + q * MA + fifth
    chosen = jnp.where((col == member) & (row < OWN), 1.0, 0.0)
    transform = jnp.dot(chosen, total, precision=lax.Precision.HIGHEST, preferred_element_type=F32)
    row = lax.broadcasted_iota(jnp.int32, (LANES, LANES), 0)
    col = lax.broadcasted_iota(jnp.int32, (LANES, LANES), 1)
    back = sum(jnp.where(col >= i * OWN, 1, 0) for i in range(1, MA))
    place = col - back * OWN
    fifth = sum(jnp.where(place >= i * CHUNK, 1, 0) for i in range(1, MA))
    member = (place - fifth * CHUNK) * 16 + jnp.bitwise_and(q - back, MA - 1) * MA + fifth
    shuffle = jnp.where((row == member) & (col < MEMBERS), 1.0, 0.0)
    transform = jnp.dot(transform, shuffle, precision=lax.Precision.HIGHEST, preferred_element_type=F32)
    tiles = []
    for c in range(8):
        at = pl.ds(c, OWN, stride=8)
        tile = jnp.concatenate(
            [ref[at, :] for ref in (state_ref, gathered_1, gathered_2, gathered_3)], axis=0
        )
        tiles.append(tile - jnp.mean(tile, axis=0, keepdims=True))
    centered = jnp.concatenate(
        [jnp.concatenate(tiles, axis=1), jnp.zeros((LANES - MEMBERS, CELLS), F32)], axis=0
    )
    c_high, c_low = split(centered)
    t_high, t_low = split(transform)
    update = dot_nn(t_high, c_high) + dot_nn(t_low, c_high) + dot_nn(t_high, c_low)
    for c in range(8):
        at = pl.ds(c, OWN, stride=8)
        out_ref[at, :] = state_ref[at, :] + update[:OWN, c * LANES : (c + 1) * LANES]


def other_core(x):
    return lax.ppermute(x, "gy", [(0, 1), (1, 0)])


def params(mebibytes):
    return pltpu.CompilerParams(vmem_limit_bytes=mebibytes * 1024 * 1024)


def over_members(x):
    return [lax.ppermute(x, "ma", [(i, (i + s) % MA) for i in range(MA)]) for s in range(1, MA)]


def local(
    ensemble, wind_field, obs_value, obs_var, obs_region, obs_cell, block_order, localization
):
    both = jnp.concatenate([ensemble, wind_field], axis=0)
    forward = [(i, (i + 1) % GX) for i in range(GX)]
    backward = [(i, (i - 1) % GX) for i in range(GX)]
    low = lax.ppermute(both[:, :, 2:], "gx", forward)
    high = lax.ppermute(both[:, :, :2], "gx", backward)
    prepared = pl.pallas_call(
        prepare_kernel,
        out_shape=(
            jax.ShapeDtypeStruct((40, LANES), F32),
            jax.ShapeDtypeStruct((4 * BLOCKS, OBS), F32),
        ),
        in_specs=[pl.BlockSpec(memory_space=pltpu.HBM)] * 6,
        out_specs=(VMEM,) * 2,
        scratch_shapes=[pltpu.SMEM((BLOCKS,), jnp.int32)]
        + [pltpu.VMEM((BLOCKS, OBS), jnp.int32)] * 2
        + [pltpu.VMEM((BLOCKS, OBS), F32)] * 3
        + [pltpu.SemaphoreType.DMA((6,))],
        compiler_params=params(60),
        cost_estimate=pl.CostEstimate(flops=10_000_000, bytes_accessed=2_000_000, transcendentals=0),
        name="prepare",
    )(block_order, obs_cell, obs_region, obs_value, obs_var, localization.reshape(BLOCKS, OBS))
    low, high, prepared = lax.optimization_barrier((low, high, prepared))
    index, observed = prepared
    own = jnp.concatenate([low, both, high], axis=2).reshape(-1, LANES)
    beside = other_core(own)

    state, picked = pl.pallas_call(
        advect_kernel,
        out_shape=(
            jax.ShapeDtypeStruct((OWN * 8, LANES), F32),
            jax.ShapeDtypeStruct((GX * SENT, LANES), F32),
        ),
        in_specs=[VMEM] * 3,
        out_specs=(VMEM, VMEM),
        scratch_shapes=[pltpu.VMEM((2, 24 * 8, LANES), F32)],
        compiler_params=params(4),
        cost_estimate=pl.CostEstimate(flops=10_000_000, bytes_accessed=1_000_000, transcendentals=0),
        name="advect",
    )(own, beside, index)

    parts = lax.all_to_all(picked.reshape(GX, 1, SENT * LANES), "gx", 0, 0, tiled=True)
    gathered = over_members(state)
    parts, gathered = lax.optimization_barrier((parts, gathered))
    parts = parts.reshape(-1, LANES)
    owned = pl.pallas_call(
        owner_kernel,
        out_shape=jax.ShapeDtypeStruct((MA * GX * CHUNK, LANES), F32),
        in_specs=[VMEM],
        out_specs=VMEM,
        compiler_params=params(4),
        name="owner",
    )(parts)
    weights = pl.pallas_call(
        weights_kernel,
        out_shape=jax.ShapeDtypeStruct((QUARTER * GX, LANES), F32),
        in_specs=[VMEM],
        out_specs=VMEM,
        compiler_params=params(4),
        name="weights",
    )(parts)
    came = lax.all_to_all(
        owned.reshape(MA * GX, 1, CHUNK * LANES), ("ma", "gx"), 0, 0, tiled=True
    ).reshape(-1, LANES)
    weights = jnp.concatenate([weights] + over_members(weights), axis=0)
    came, weights = lax.optimization_barrier((came, weights))
    tapers = pl.pallas_call(
        tapers_kernel,
        out_shape=jax.ShapeDtypeStruct((TAPERS + (BLOCKS - 1) * OBS, LANES), BF16),
        in_specs=[VMEM] * 3,
        out_specs=VMEM,
        compiler_params=params(4),
        cost_estimate=pl.CostEstimate(flops=1000, bytes_accessed=1000, transcendentals=0),
        name="tapers",
    )(weights, other_core(weights), observed)
    came_beside = other_core(came)

    out = pl.pallas_call(
        filter_kernel,
        out_shape=jax.ShapeDtypeStruct((OWN * 8, LANES), F32),
        in_specs=[VMEM] * 8,
        out_specs=VMEM,
        scratch_shapes=[
            pltpu.VMEM((BLOCKS * OBS, LANES), F32),
            pltpu.VMEM((OBS, LANES), BF16),
            pltpu.VMEM((OBS, 2 * LANES), BF16),
            pltpu.VMEM((LANES, LANES), F32),
            pltpu.VMEM((LANES, OBS), F32),
        ],
        compiler_params=params(32),
        cost_estimate=pl.CostEstimate(flops=3_000_000_000, bytes_accessed=4_000_000, transcendentals=0),
        name="filter",
    )(came, came_beside, tapers, observed, *gathered, state)
    return out.reshape(ensemble.shape)


def solution(mesh):
    in_specs = (
        P("ma", None, "gx", "gy"),
        P(None, None, "gx", "gy"),
        P(),
        P(),
        P(),
        P(),
        P(),
        P("gx", "gy", None, None),
    )
    out_specs = P("ma", None, "gx", "gy")
    return jax.shard_map(local, mesh=mesh, in_specs=in_specs, out_specs=out_specs, check_vma=False)
```

```python
import jax
import jax.numpy as jnp
from jax import lax
from jax.experimental import pallas as pl
from jax.experimental.pallas import tpu as pltpu
from jax.sharding import PartitionSpec as P

MEMBERS = 80
OWN = 20
BLOCKS = 4
OBS = 1024
CELLS = 1024
GX = 64
MA = 4
LANES = 128
GROUPS = OBS // LANES
KAPPA = 0.025
CHUNK = 5
HALF = OWN * 2 * GROUPS
QUARTER = (BLOCKS - 1) * GROUPS // MA
SENT = CHUNK + QUARTER
TAPERS = (BLOCKS - 1) * GROUPS * 2 * LANES
ROWS_O = 1024
F32 = jnp.float32
BF16 = jnp.bfloat16
VMEM = pl.BlockSpec(memory_space=pltpu.VMEM)
SMEM = pl.BlockSpec(memory_space=pltpu.SMEM)


def split(value):
    high = value.astype(BF16)
    return high, (value - high.astype(F32)).astype(BF16)


def dot_nn(a, b):
    return lax.dot_general(a, b, (((1,), (0,)), ((), ())), preferred_element_type=F32)


def dot_nt(a, b):
    return lax.dot_general(a, b, (((1,), (1,)), ((), ())), preferred_element_type=F32)


def block_row(ref, b, columns):
    row = ref[pl.ds(0, 1), columns]
    for i in range(1, BLOCKS):
        row = jnp.where(b == i, ref[pl.ds(i, 1), columns], row)
    return row


def advect_kernel(own_ref, other_ref, index_ref, state_ref, picked_ref, work):
    lane = lax.broadcasted_iota(jnp.int32, (8, LANES), 1)
    first, last = lane == 0, lane == LANES - 1

    def step(q, beside, wind):
        u_up, u_down, v_up, v_down = wind
        west, east = pltpu.roll(q, 1, 0), pltpu.roll(q, 7, 0)
        south = jnp.where(first, pltpu.roll(beside, 1, 1), pltpu.roll(q, 1, 1))
        north = jnp.where(last, pltpu.roll(beside, LANES - 1, 1), pltpu.roll(q, LANES - 1, 1))
        return (
            q
            - u_up * (q - west)
            - u_down * (east - q)
            - v_up * (q - south)
            - v_down * (north - q)
            + KAPPA * (east + west + north + south - 4.0 * q)
        )

    def winds(ref, level):
        u = ref[pl.ds((OWN * 2 + level) * 8, 8), :]
        v = ref[pl.ds((OWN * 2 + 2 + level) * 8, 8), :]
        return jnp.maximum(u, 0.0), jnp.minimum(u, 0.0), jnp.maximum(v, 0.0), jnp.minimum(v, 0.0)

    for side in range(2):
        work[side, pl.ds(OWN * 8, 32), :] = jnp.zeros((32, LANES), F32)
    for level in range(2):
        wind, wind_o = winds(own_ref, level), winds(other_ref, level)
        for m in range(OWN):
            at = (m * 2 + level) * 8
            q, q_o = own_ref[pl.ds(at, 8), :], other_ref[pl.ds(at, 8), :]
            once, once_o = step(q, q_o, wind), step(q_o, q, wind_o)
            twice, twice_o = step(once, once_o, wind), step(once_o, once, wind_o)
            at = pl.ds(m * 8 + level * 4, 4)
            state_ref[at, :] = twice[2:6]
            work[0, at, :] = twice[2:6]
            work[1, at, :] = twice_o[2:6]

    eight = jnp.concatenate(
        [jnp.zeros((CHUNK, LANES), F32), index_ref[pl.ds(32, QUARTER), :]] * 8, axis=0
    )
    for i in range(GX // 8):
        picked_ref[pl.ds(i * 8 * SENT, 8 * SENT), :] = eight
    for g in range(2 * GROUPS):
        y = jnp.broadcast_to(index_ref[pl.ds(g, 1), :].astype(jnp.int32), (24, LANES))
        part = jnp.broadcast_to(index_ref[pl.ds(g + 16, 1), :], (24, LANES))
        total = jnp.zeros((24, LANES), F32)
        for c in range(16):
            source = work[c // 8, pl.ds(c % 8, 24, stride=8), :]
            found = jnp.take_along_axis(source, y, axis=1, mode="promise_in_bounds")
            total = jnp.where(part == c, found, total)
        for i in range(MA):
            at = (i * 2 * GROUPS + g) * SENT
            picked_ref[pl.ds(at, CHUNK), :] = total[i * CHUNK : (i + 1) * CHUNK]


def prepare_kernel(*refs):
    sources, results, copies, done = refs[:6], refs[6:8], refs[8:14], refs[14]
    moves = [
        pltpu.make_async_copy(source, copy, done.at[i])
        for i, (source, copy) in enumerate(zip(sources, copies))
    ]
    for move in moves:
        move.start()
    for move in moves:
        move.wait()
    order, cell_ref, region_ref, value_ref, var_ref, taper_ref = copies
    index_ref, obs_ref = results
    gx, gy, q = lax.axis_index("gx"), lax.axis_index("gy"), lax.axis_index("ma")
    for k in range(2):
        b = order[gy * 2 + k]
        for g in range(GROUPS):
            columns = pl.ds(g * LANES, LANES)
            cell, region = block_row(cell_ref, b, columns), block_row(region_ref, b, columns)
            part = jnp.right_shift(cell, 7) + jnp.where(jnp.bitwise_and(region, 1) == gy, 0, 8)
            part = jnp.where(jnp.right_shift(region, 1) == gx, part, -1)
            at = k * GROUPS + g
            index_ref[pl.ds(at, 1), :] = jnp.bitwise_and(cell, LANES - 1).astype(F32)
            index_ref[pl.ds(at + 16, 1), :] = part.astype(F32)

    for k in range(BLOCKS):
        for i, ref in enumerate((value_ref, var_ref, taper_ref)):
            obs_ref[pl.ds(i * BLOCKS + k, 1), :] = block_row(ref, order[k], pl.ds(0, OBS))
        region = block_row(region_ref, order[k], pl.ds(0, OBS))
        place = jnp.where(jnp.bitwise_and(region, 1) == gy, 0, GX) + jnp.right_shift(region, 1)
        obs_ref[pl.ds(3 * BLOCKS + k, 1), :] = place.astype(F32)

    index_ref[pl.ds(32, 8), :] = jnp.zeros((8, LANES), F32)
    for i in range(QUARTER):
        tile = q * QUARTER + i
        b, g = order[tile // GROUPS], tile % GROUPS
        row = block_row(taper_ref, b, pl.ds(0, LANES))
        for j in range(1, GROUPS):
            row = jnp.where(g == j, block_row(taper_ref, b, pl.ds(j * LANES, LANES)), row)
        index_ref[pl.ds(32 + i, 1), :] = row


def weights_kernel(parts_ref, weights_ref):
    for i in range(QUARTER):
        weights_ref[pl.ds(i * GX, GX), :] = parts_ref[pl.ds(CHUNK + i, GX, stride=SENT), :]


def owner_kernel(parts_ref, out_ref):
    total = parts_ref[pl.ds(0, 8 * SENT), :]
    for i in range(1, GX // 8):
        total = total + parts_ref[pl.ds(i * 8 * SENT, 8 * SENT), :]
    part = total[0:CHUNK]
    for i in range(1, 8):
        part = part + total[i * SENT : i * SENT + CHUNK]
    eight = jnp.concatenate([part] * 8, axis=0)
    for i in range(GX * MA // 8):
        out_ref[pl.ds(i * 8 * CHUNK, 8 * CHUNK), :] = eight


def tapers_kernel(own_ref, other_ref, obs_ref, out_ref):
    q = lax.axis_index("ma")
    for shift in range(MA):
        for i in range(QUARTER):
            tile = jnp.bitwise_and(q - shift, MA - 1) * QUARTER + i
            for side, ref in enumerate((own_ref, other_ref)):
                high, low = split(ref[pl.ds((shift * QUARTER + i) * GX, GX), :])
                at = pl.multiple_of(tile * 2 * LANES, 2 * LANES) + side * GX
                out_ref[pl.ds(pl.multiple_of(at, GX), GX), :] = high
                out_ref[pl.ds(pl.multiple_of(at + LANES, GX), GX), :] = low

    rows = lax.broadcasted_iota(jnp.int32, (LANES, LANES), 0).astype(F32)
    for k in range(1, BLOCKS):
        for g in range(GROUPS):
            place = obs_ref[pl.ds(3 * BLOCKS + k, 1), pl.ds(g * LANES, LANES)]
            hot = (rows == jnp.broadcast_to(place, (LANES, LANES))).astype(F32).T.astype(BF16)
            out_ref[pl.ds(TAPERS + ((k - 1) * GROUPS + g) * LANES, LANES), :] = hot


def filter_kernel(
    came_ref,
    came_o_ref,
    tapers,
    obs_ref,
    gathered_1,
    gathered_2,
    gathered_3,
    state_ref,
    out_ref,
    xt,
    b_high,
    b_both,
    increments,
    first_block,
):
    gy = lax.axis_index("gy")
    denom = MEMBERS - 1.0

    def load_half(ref, half):
        for g in range(16):
            block = jnp.concatenate(
                [ref[pl.ds(g * CHUNK + i, 16, stride=16 * CHUNK), :] for i in range(CHUNK)], axis=0
            )
            mean = jnp.mean(block, axis=0, keepdims=True)
            full = jnp.concatenate(
                [block - mean, mean, jnp.zeros((LANES - MEMBERS - 1, LANES), F32)], axis=0
            )
            if half == 0 and g < GROUPS:
                first_block[:, pl.ds(g * LANES, LANES)] = full
            else:
                xt[pl.ds((half * 16 + g) * LANES, LANES), :] = full.T

    @pl.when(gy == 0)
    def _():
        load_half(came_ref, 0)
        load_half(came_o_ref, 1)

    @pl.when(gy == 1)
    def _():
        load_half(came_o_ref, 0)
        load_half(came_ref, 1)

    lane = lax.broadcasted_iota(jnp.int32, (ROWS_O, LANES), 1)
    member_row = lax.broadcasted_iota(jnp.int32, (LANES, OBS), 0)
    increments[...] = jnp.zeros((LANES, LANES), F32)
    for k in range(BLOCKS):
        if k == 0:
            now = first_block[...]
        else:
            now = jnp.concatenate(
                [xt[pl.ds((k * GROUPS + g) * LANES, LANES), :].T for g in range(GROUPS)], axis=1
            )
        anomaly = jnp.where(member_row < MEMBERS, now, 0.0)
        mean = now[MEMBERS : MEMBERS + 1]
        variance = jnp.sum(anomaly * anomaly, axis=0, keepdims=True) / denom
        error_var = obs_ref[pl.ds(BLOCKS + k, 1), :]
        total_var = variance + error_var
        shrink = 1.0 / (1.0 + jnp.sqrt(error_var / total_var))
        scale = 1.0 / (denom * total_var)
        gain_mean = (obs_ref[pl.ds(k, 1), :] - mean) * scale
        gain = jnp.where(member_row == MEMBERS, gain_mean, -(shrink * scale) * anomaly)
        gain_high, gain_low = split(gain)

        tapered_high, tapered_low = split(anomaly * obs_ref[pl.ds(2 * BLOCKS + k, 1), :])
        mixing = (
            dot_nt(gain_high, tapered_high)
            + dot_nt(gain_low, tapered_high)
            + dot_nt(gain_high, tapered_low)
        )
        e = increments[...]
        increments[...] = e + mixing + jnp.dot(
            mixing, e, precision=lax.Precision.HIGHEST, preferred_element_type=F32
        )

        if k == BLOCKS - 1:
            continue
        a_high, a_low = split(anomaly)
        left = jnp.concatenate([a_high[:MEMBERS], a_high[:MEMBERS], a_low[:MEMBERS], jnp.zeros((16, OBS), BF16)], axis=0)
        b_high[...] = gain_high.astype(F32).T.astype(BF16)
        b_both[:, pl.ds(0, LANES)] = b_high[...]
        b_both[:, pl.ds(LANES, LANES)] = gain_low.astype(F32).T.astype(BF16)

        def chunk(i, carry, k=k, left=left):
            taper = jnp.concatenate([tapers[pl.ds((k * GROUPS + g) * 2 * LANES, 2 * LANES), :] for g in range(GROUPS)], axis=1)
            at = pl.multiple_of((k + 1) * OBS + i * ROWS_O, ROWS_O)
            x = xt[pl.ds(at, ROWS_O), :]
            clean = jnp.where(lane < MEMBERS, x, 0.0)
            high = clean.astype(BF16).astype(F32)
            low = (clean - high)
            low_rolled = pltpu.roll(low, MEMBERS, 1)
            first = jnp.where(lane < MEMBERS, high, low_rolled)
            second = jnp.where(lane < 2 * MEMBERS - LANES, low_rolled, pltpu.roll(high, 2 * MEMBERS - LANES, 1))
            second = jnp.where(lane < 3 * MEMBERS - LANES, second, 0.0)
            query = jnp.concatenate([first, second], axis=1).astype(BF16)
            hot = tapers[pl.ds(pl.multiple_of(at + TAPERS - OBS, ROWS_O), ROWS_O), :]
            hot = jnp.concatenate([hot, hot], axis=1)
            weight = dot_nn(query, left) * dot_nn(hot, taper)
            w_high, w_low = split(weight)
            both = dot_nn(w_high, b_both[...])
            xt[pl.ds(at, ROWS_O), :] = (
                x + both[:, :LANES] + both[:, LANES:] + dot_nn(w_low, b_high[...])
            )
            return carry

        lax.fori_loop(0, (BLOCKS - 1 - k) * OBS // ROWS_O, chunk, 0)

    q = lax.axis_index("ma")
    e = increments[...]
    total = e + e[MEMBERS : MEMBERS + 1]
    row = lax.broadcasted_iota(jnp.int32, (24, LANES), 0)
    col = lax.broadcasted_iota(jnp.int32, (24, LANES), 1)
    fifth = sum(jnp.where(row >= i * CHUNK, 1, 0) for i in range(1, MA))
    member = (row - fifth * CHUNK) * 16 + q * MA + fifth
    chosen = jnp.where((col == member) & (row < OWN), 1.0, 0.0)
    transform = jnp.dot(chosen, total, precision=lax.Precision.HIGHEST, preferred_element_type=F32)
    row = lax.broadcasted_iota(jnp.int32, (LANES, LANES), 0)
    col = lax.broadcasted_iota(jnp.int32, (LANES, LANES), 1)
    back = sum(jnp.where(col >= i * OWN, 1, 0) for i in range(1, MA))
    place = col - back * OWN
    fifth = sum(jnp.where(place >= i * CHUNK, 1, 0) for i in range(1, MA))
    member = (place - fifth * CHUNK) * 16 + jnp.bitwise_and(q - back, MA - 1) * MA + fifth
    shuffle = jnp.where((row == member) & (col < MEMBERS), 1.0, 0.0)
    transform = jnp.dot(transform, shuffle, precision=lax.Precision.HIGHEST, preferred_element_type=F32)
    tiles = []
    for c in range(8):
        at = pl.ds(c, OWN, stride=8)
        tile = jnp.concatenate(
            [ref[at, :] for ref in (state_ref, gathered_1, gathered_2, gathered_3)], axis=0
        )
        tiles.append(tile - jnp.mean(tile, axis=0, keepdims=True))
    centered = jnp.concatenate(
        [jnp.concatenate(tiles, axis=1), jnp.zeros((LANES - MEMBERS, CELLS), F32)], axis=0
    )
    c_high, c_low = split(centered)
    t_high, t_low = split(transform)
    update = dot_nn(t_high, c_high) + dot_nn(t_low, c_high) + dot_nn(t_high, c_low)
    for c in range(8):
        at = pl.ds(c, OWN, stride=8)
        out_ref[at, :] = state_ref[at, :] + update[:OWN, c * LANES : (c + 1) * LANES]


def other_core(x):
    return lax.ppermute(x, "gy", [(0, 1), (1, 0)])


def params(mebibytes):
    return pltpu.CompilerParams(vmem_limit_bytes=mebibytes * 1024 * 1024)


def over_members(x):
    return [lax.ppermute(x, "ma", [(i, (i + s) % MA) for i in range(MA)]) for s in range(1, MA)]


def local(
    ensemble, wind_field, obs_value, obs_var, obs_region, obs_cell, block_order, localization
):
    both = jnp.concatenate([ensemble, wind_field], axis=0)
    forward = [(i, (i + 1) % GX) for i in range(GX)]
    backward = [(i, (i - 1) % GX) for i in range(GX)]
    low = lax.ppermute(both[:, :, 2:], "gx", forward)
    high = lax.ppermute(both[:, :, :2], "gx", backward)
    prepared = pl.pallas_call(
        prepare_kernel,
        out_shape=(
            jax.ShapeDtypeStruct((40, LANES), F32),
            jax.ShapeDtypeStruct((4 * BLOCKS, OBS), F32),
        ),
        in_specs=[pl.BlockSpec(memory_space=pltpu.HBM)] * 6,
        out_specs=(VMEM,) * 2,
        scratch_shapes=[pltpu.SMEM((BLOCKS,), jnp.int32)]
        + [pltpu.VMEM((BLOCKS, OBS), jnp.int32)] * 2
        + [pltpu.VMEM((BLOCKS, OBS), F32)] * 3
        + [pltpu.SemaphoreType.DMA((6,))],
        compiler_params=params(60),
        cost_estimate=pl.CostEstimate(flops=10_000_000, bytes_accessed=2_000_000, transcendentals=0),
        name="prepare",
    )(block_order, obs_cell, obs_region, obs_value, obs_var, localization.reshape(BLOCKS, OBS))
    low, high, prepared = lax.optimization_barrier((low, high, prepared))
    index, observed = prepared
    own = jnp.concatenate([low, both, high], axis=2).reshape(-1, LANES)
    beside = other_core(own)

    state, picked = pl.pallas_call(
        advect_kernel,
        out_shape=(
            jax.ShapeDtypeStruct((OWN * 8, LANES), F32),
            jax.ShapeDtypeStruct((GX * SENT, LANES), F32),
        ),
        in_specs=[VMEM] * 3,
        out_specs=(VMEM, VMEM),
        scratch_shapes=[pltpu.VMEM((2, 24 * 8, LANES), F32)],
        compiler_params=params(4),
        cost_estimate=pl.CostEstimate(flops=10_000_000, bytes_accessed=1_000_000, transcendentals=0),
        name="advect",
    )(own, beside, index)

    parts = lax.all_to_all(picked.reshape(GX, 1, SENT * LANES), "gx", 0, 0, tiled=True)
    gathered = over_members(state)
    parts = parts.reshape(-1, LANES)
    owned = pl.pallas_call(
        owner_kernel,
        out_shape=jax.ShapeDtypeStruct((MA * GX * CHUNK, LANES), F32),
        in_specs=[VMEM],
        out_specs=VMEM,
        compiler_params=params(4),
        name="owner",
    )(parts)
    weights = pl.pallas_call(
        weights_kernel,
        out_shape=jax.ShapeDtypeStruct((QUARTER * GX, LANES), F32),
        in_specs=[VMEM],
        out_specs=VMEM,
        compiler_params=params(4),
        name="weights",
    )(parts)
    came = lax.all_to_all(
        owned.reshape(MA * GX, 1, CHUNK * LANES), ("ma", "gx"), 0, 0, tiled=True
    ).reshape(-1, LANES)
    weights = [weights] + over_members(weights)
    weights, gathered = lax.optimization_barrier((weights, gathered))
    weights = jnp.concatenate(weights, axis=0)
    came, weights = lax.optimization_barrier((came, weights))
    tapers = pl.pallas_call(
        tapers_kernel,
        out_shape=jax.ShapeDtypeStruct((TAPERS + (BLOCKS - 1) * OBS, LANES), BF16),
        in_specs=[VMEM] * 3,
        out_specs=VMEM,
        compiler_params=params(4),
        cost_estimate=pl.CostEstimate(flops=1000, bytes_accessed=1000, transcendentals=0),
        name="tapers",
    )(weights, other_core(weights), observed)
    came_beside = other_core(came)

    out = pl.pallas_call(
        filter_kernel,
        out_shape=jax.ShapeDtypeStruct((OWN * 8, LANES), F32),
        in_specs=[VMEM] * 8,
        out_specs=VMEM,
        scratch_shapes=[
            pltpu.VMEM((BLOCKS * OBS, LANES), F32),
            pltpu.VMEM((OBS, LANES), BF16),
            pltpu.VMEM((OBS, 2 * LANES), BF16),
            pltpu.VMEM((LANES, LANES), F32),
            pltpu.VMEM((LANES, OBS), F32),
        ],
        compiler_params=params(32),
        cost_estimate=pl.CostEstimate(flops=3_000_000_000, bytes_accessed=4_000_000, transcendentals=0),
        name="filter",
    )(came, came_beside, tapers, observed, *gathered, state)
    return out.reshape(ensemble.shape)


def solution(mesh):
    in_specs = (
        P("ma", None, "gx", "gy"),
        P(None, None, "gx", "gy"),
        P(),
        P(),
        P(),
        P(),
        P(),
        P("gx", "gy", None, None),
    )
    out_specs = P("ma", None, "gx", "gy")
    return jax.shard_map(local, mesh=mesh, in_specs=in_specs, out_specs=out_specs, check_vma=False)
```

```python
import jax
import jax.numpy as jnp
from jax import lax
from jax.experimental import pallas as pl
from jax.experimental.pallas import tpu as pltpu
from jax.sharding import PartitionSpec as P

MEMBERS = 80
OWN = 20
BLOCKS = 4
OBS = 1024
CELLS = 1024
GX = 64
MA = 4
LANES = 128
GROUPS = OBS // LANES
KAPPA = 0.025
CHUNK = 5
HALF = OWN * 2 * GROUPS
QUARTER = (BLOCKS - 1) * GROUPS // MA
SENT = CHUNK + QUARTER
TAPERS = (BLOCKS - 1) * GROUPS * 2 * LANES
ROWS_O = 1024
F32 = jnp.float32
BF16 = jnp.bfloat16
VMEM = pl.BlockSpec(memory_space=pltpu.VMEM)
SMEM = pl.BlockSpec(memory_space=pltpu.SMEM)


def split(value):
    high = value.astype(BF16)
    return high, (value - high.astype(F32)).astype(BF16)


def dot_nn(a, b):
    return lax.dot_general(a, b, (((1,), (0,)), ((), ())), preferred_element_type=F32)


def dot_nt(a, b):
    return lax.dot_general(a, b, (((1,), (1,)), ((), ())), preferred_element_type=F32)


def block_row(ref, b, columns):
    row = ref[pl.ds(0, 1), columns]
    for i in range(1, BLOCKS):
        row = jnp.where(b == i, ref[pl.ds(i, 1), columns], row)
    return row


def advect_kernel(own_ref, other_ref, index_ref, state_ref, picked_ref, work):
    lane = lax.broadcasted_iota(jnp.int32, (8, LANES), 1)
    first, last = lane == 0, lane == LANES - 1

    def step(q, beside, wind):
        u_up, u_down, v_up, v_down = wind
        west, east = pltpu.roll(q, 1, 0), pltpu.roll(q, 7, 0)
        south = jnp.where(first, pltpu.roll(beside, 1, 1), pltpu.roll(q, 1, 1))
        north = jnp.where(last, pltpu.roll(beside, LANES - 1, 1), pltpu.roll(q, LANES - 1, 1))
        return (
            q
            - u_up * (q - west)
            - u_down * (east - q)
            - v_up * (q - south)
            - v_down * (north - q)
            + KAPPA * (east + west + north + south - 4.0 * q)
        )

    def winds(ref, level):
        u = ref[pl.ds((OWN * 2 + level) * 8, 8), :]
        v = ref[pl.ds((OWN * 2 + 2 + level) * 8, 8), :]
        return jnp.maximum(u, 0.0), jnp.minimum(u, 0.0), jnp.maximum(v, 0.0), jnp.minimum(v, 0.0)

    for side in range(2):
        work[side, pl.ds(OWN * 8, 32), :] = jnp.zeros((32, LANES), F32)
    for level in range(2):
        wind, wind_o = winds(own_ref, level), winds(other_ref, level)
        for m in range(OWN):
            at = (m * 2 + level) * 8
            q, q_o = own_ref[pl.ds(at, 8), :], other_ref[pl.ds(at, 8), :]
            once, once_o = step(q, q_o, wind), step(q_o, q, wind_o)
            twice, twice_o = step(once, once_o, wind), step(once_o, once, wind_o)
            at = pl.ds(m * 8 + level * 4, 4)
            state_ref[at, :] = twice[2:6]
            work[0, at, :] = twice[2:6]
            work[1, at, :] = twice_o[2:6]

    eight = jnp.concatenate(
        [jnp.zeros((CHUNK, LANES), F32), index_ref[pl.ds(32, QUARTER), :]] * 8, axis=0
    )
    for i in range(GX // 8):
        picked_ref[pl.ds(i * 8 * SENT, 8 * SENT), :] = eight
    for g in range(2 * GROUPS):
        y = jnp.broadcast_to(index_ref[pl.ds(g, 1), :].astype(jnp.int32), (24, LANES))
        part = jnp.broadcast_to(index_ref[pl.ds(g + 16, 1), :], (24, LANES))
        total = jnp.zeros((24, LANES), F32)
        for c in range(16):
            source = work[c // 8, pl.ds(c % 8, 24, stride=8), :]
            found = jnp.take_along_axis(source, y, axis=1, mode="promise_in_bounds")
            total = jnp.where(part == c, found, total)
        for i in range(MA):
            at = (i * 2 * GROUPS + g) * SENT
            picked_ref[pl.ds(at, CHUNK), :] = total[i * CHUNK : (i + 1) * CHUNK]


def prepare_kernel(*refs):
    sources, results, copies, done = refs[:6], refs[6:8], refs[8:14], refs[14]
    moves = [
        pltpu.make_async_copy(source, copy, done.at[i])
        for i, (source, copy) in enumerate(zip(sources, copies))
    ]
    for move in moves:
        move.start()
    for move in moves:
        move.wait()
    order, cell_ref, region_ref, value_ref, var_ref, taper_ref = copies
    index_ref, obs_ref = results
    gx, gy, q = lax.axis_index("gx"), lax.axis_index("gy"), lax.axis_index("ma")
    for k in range(2):
        b = order[gy * 2 + k]
        for g in range(GROUPS):
            columns = pl.ds(g * LANES, LANES)
            cell, region = block_row(cell_ref, b, columns), block_row(region_ref, b, columns)
            part = jnp.right_shift(cell, 7) + jnp.where(jnp.bitwise_and(region, 1) == gy, 0, 8)
            part = jnp.where(jnp.right_shift(region, 1) == gx, part, -1)
            at = k * GROUPS + g
            index_ref[pl.ds(at, 1), :] = jnp.bitwise_and(cell, LANES - 1).astype(F32)
            index_ref[pl.ds(at + 16, 1), :] = part.astype(F32)

    for k in range(BLOCKS):
        for i, ref in enumerate((value_ref, var_ref, taper_ref)):
            obs_ref[pl.ds(i * BLOCKS + k, 1), :] = block_row(ref, order[k], pl.ds(0, OBS))
        region = block_row(region_ref, order[k], pl.ds(0, OBS))
        place = jnp.where(jnp.bitwise_and(region, 1) == gy, 0, GX) + jnp.right_shift(region, 1)
        obs_ref[pl.ds(3 * BLOCKS + k, 1), :] = place.astype(F32)

    index_ref[pl.ds(32, 8), :] = jnp.zeros((8, LANES), F32)
    for i in range(QUARTER):
        tile = q * QUARTER + i
        b, g = order[tile // GROUPS], tile % GROUPS
        row = block_row(taper_ref, b, pl.ds(0, LANES))
        for j in range(1, GROUPS):
            row = jnp.where(g == j, block_row(taper_ref, b, pl.ds(j * LANES, LANES)), row)
        index_ref[pl.ds(32 + i, 1), :] = row


def weights_kernel(parts_ref, weights_ref):
    for i in range(QUARTER):
        weights_ref[pl.ds(i * GX, GX), :] = parts_ref[pl.ds(CHUNK + i, GX, stride=SENT), :]


def owner_kernel(parts_ref, out_ref):
    total = parts_ref[pl.ds(0, 8 * SENT), :]
    for i in range(1, GX // 8):
        total = total + parts_ref[pl.ds(i * 8 * SENT, 8 * SENT), :]
    part = total[0:CHUNK]
    for i in range(1, 8):
        part = part + total[i * SENT : i * SENT + CHUNK]
    eight = jnp.concatenate([part] * 8, axis=0)
    for i in range(GX * MA // 8):
        out_ref[pl.ds(i * 8 * CHUNK, 8 * CHUNK), :] = eight


def tapers_kernel(own_ref, other_ref, obs_ref, out_ref):
    q = lax.axis_index("ma")
    for shift in range(MA):
        for i in range(QUARTER):
            tile = jnp.bitwise_and(q - shift, MA - 1) * QUARTER + i
            for side, ref in enumerate((own_ref, other_ref)):
                high, low = split(ref[pl.ds((shift * QUARTER + i) * GX, GX), :])
                at = pl.multiple_of(tile * 2 * LANES, 2 * LANES) + side * GX
                out_ref[pl.ds(pl.multiple_of(at, GX), GX), :] = high
                out_ref[pl.ds(pl.multiple_of(at + LANES, GX), GX), :] = low

    rows = lax.broadcasted_iota(jnp.int32, (LANES, LANES), 0).astype(F32)
    for k in range(1, BLOCKS):
        for g in range(GROUPS):
            place = obs_ref[pl.ds(3 * BLOCKS + k, 1), pl.ds(g * LANES, LANES)]
            hot = (rows == jnp.broadcast_to(place, (LANES, LANES))).astype(F32).T.astype(BF16)
            out_ref[pl.ds(TAPERS + ((k - 1) * GROUPS + g) * LANES, LANES), :] = hot


def filter_kernel(
    came_ref,
    came_o_ref,
    tapers,
    obs_ref,
    gathered_1,
    gathered_2,
    gathered_3,
    state_ref,
    out_ref,
    xt,
    b_high,
    b_both,
    increments,
    first_block,
):
    gy = lax.axis_index("gy")
    denom = MEMBERS - 1.0

    def load_half(ref, half):
        for g in range(16):
            block = jnp.concatenate(
                [ref[pl.ds(g * CHUNK + i, 16, stride=16 * CHUNK), :] for i in range(CHUNK)], axis=0
            )
            mean = jnp.mean(block, axis=0, keepdims=True)
            full = jnp.concatenate(
                [block - mean, mean, jnp.zeros((LANES - MEMBERS - 1, LANES), F32)], axis=0
            )
            if half == 0 and g < GROUPS:
                first_block[:, pl.ds(g * LANES, LANES)] = full
            else:
                xt[pl.ds((half * 16 + g) * LANES, LANES), :] = full.T

    @pl.when(gy == 0)
    def _():
        load_half(came_ref, 0)
        load_half(came_o_ref, 1)

    @pl.when(gy == 1)
    def _():
        load_half(came_o_ref, 0)
        load_half(came_ref, 1)

    lane = lax.broadcasted_iota(jnp.int32, (ROWS_O, LANES), 1)
    member_row = lax.broadcasted_iota(jnp.int32, (LANES, OBS), 0)
    increments[...] = jnp.zeros((LANES, LANES), F32)
    for k in range(BLOCKS):
        if k == 0:
            now = first_block[...]
        else:
            now = jnp.concatenate(
                [xt[pl.ds((k * GROUPS + g) * LANES, LANES), :].T for g in range(GROUPS)], axis=1
            )
        anomaly = jnp.where(member_row < MEMBERS, now, 0.0)
        mean = now[MEMBERS : MEMBERS + 1]
        variance = jnp.sum(anomaly * anomaly, axis=0, keepdims=True) / denom
        error_var = obs_ref[pl.ds(BLOCKS + k, 1), :]
        total_var = variance + error_var
        shrink = 1.0 / (1.0 + jnp.sqrt(error_var / total_var))
        scale = 1.0 / (denom * total_var)
        gain_mean = (obs_ref[pl.ds(k, 1), :] - mean) * scale
        gain = jnp.where(member_row == MEMBERS, gain_mean, -(shrink * scale) * anomaly)
        gain_high, gain_low = split(gain)

        tapered_high, tapered_low = split(anomaly * obs_ref[pl.ds(2 * BLOCKS + k, 1), :])
        mixing = (
            dot_nt(gain_high, tapered_high)
            + dot_nt(gain_low, tapered_high)
            + dot_nt(gain_high, tapered_low)
        )
        e = increments[...]
        increments[...] = e + mixing + jnp.dot(
            mixing, e, precision=lax.Precision.HIGHEST, preferred_element_type=F32
        )

        if k == BLOCKS - 1:
            continue
        a_high, a_low = split(anomaly)
        left = jnp.concatenate([a_high[:MEMBERS], a_high[:MEMBERS], a_low[:MEMBERS], jnp.zeros((16, OBS), BF16)], axis=0)
        b_high[...] = gain_high.astype(F32).T.astype(BF16)
        b_both[:, pl.ds(0, LANES)] = b_high[...]
        b_both[:, pl.ds(LANES, LANES)] = gain_low.astype(F32).T.astype(BF16)

        def chunk(i, carry, k=k, left=left):
            taper = jnp.concatenate([tapers[pl.ds((k * GROUPS + g) * 2 * LANES, 2 * LANES), :] for g in range(GROUPS)], axis=1)
            at = pl.multiple_of((k + 1) * OBS + i * ROWS_O, ROWS_O)
            x = xt[pl.ds(at, ROWS_O), :]
            clean = jnp.where(lane < MEMBERS, x, 0.0)
            high = clean.astype(BF16).astype(F32)
            low = (clean - high)
            low_rolled = pltpu.roll(low, MEMBERS, 1)
            first = jnp.where(lane < MEMBERS, high, low_rolled)
            second = jnp.where(lane < 2 * MEMBERS - LANES, low_rolled, pltpu.roll(high, 2 * MEMBERS - LANES, 1))
            second = jnp.where(lane < 3 * MEMBERS - LANES, second, 0.0)
            query = jnp.concatenate([first, second], axis=1).astype(BF16)
            hot = tapers[pl.ds(pl.multiple_of(at + TAPERS - OBS, ROWS_O), ROWS_O), :]
            hot = jnp.concatenate([hot, hot], axis=1)
            weight = dot_nn(query, left) * dot_nn(hot, taper)
            w_high, w_low = split(weight)
            both = dot_nn(w_high, b_both[...])
            xt[pl.ds(at, ROWS_O), :] = (
                x + both[:, :LANES] + both[:, LANES:] + dot_nn(w_low, b_high[...])
            )
            return carry

        lax.fori_loop(0, (BLOCKS - 1 - k) * OBS // ROWS_O, chunk, 0)

    q = lax.axis_index("ma")
    e = increments[...]
    total = e + e[MEMBERS : MEMBERS + 1]
    row = lax.broadcasted_iota(jnp.int32, (24, LANES), 0)
    col = lax.broadcasted_iota(jnp.int32, (24, LANES), 1)
    fifth = sum(jnp.where(row >= i * CHUNK, 1, 0) for i in range(1, MA))
    member = (row - fifth * CHUNK) * 16 + q * MA + fifth
    chosen = jnp.where((col == member) & (row < OWN), 1.0, 0.0)
    transform = jnp.dot(chosen, total, precision=lax.Precision.HIGHEST, preferred_element_type=F32)
    row = lax.broadcasted_iota(jnp.int32, (LANES, LANES), 0)
    col = lax.broadcasted_iota(jnp.int32, (LANES, LANES), 1)
    back = sum(jnp.where(col >= i * OWN, 1, 0) for i in range(1, MA))
    place = col - back * OWN
    fifth = sum(jnp.where(place >= i * CHUNK, 1, 0) for i in range(1, MA))
    member = (place - fifth * CHUNK) * 16 + jnp.bitwise_and(q - back, MA - 1) * MA + fifth
    shuffle = jnp.where((row == member) & (col < MEMBERS), 1.0, 0.0)
    transform = jnp.dot(transform, shuffle, precision=lax.Precision.HIGHEST, preferred_element_type=F32)
    tiles = []
    for c in range(8):
        at = pl.ds(c, OWN, stride=8)
        tile = jnp.concatenate(
            [ref[at, :] for ref in (state_ref, gathered_1, gathered_2, gathered_3)], axis=0
        )
        tiles.append(tile - jnp.mean(tile, axis=0, keepdims=True))
    centered = jnp.concatenate(
        [jnp.concatenate(tiles, axis=1), jnp.zeros((LANES - MEMBERS, CELLS), F32)], axis=0
    )
    c_high, c_low = split(centered)
    t_high, t_low = split(transform)
    update = dot_nn(t_high, c_high) + dot_nn(t_low, c_high) + dot_nn(t_high, c_low)
    for c in range(8):
        at = pl.ds(c, OWN, stride=8)
        out_ref[at, :] = state_ref[at, :] + update[:OWN, c * LANES : (c + 1) * LANES]


def other_core(x):
    return lax.ppermute(x, "gy", [(0, 1), (1, 0)])


def params(mebibytes):
    return pltpu.CompilerParams(vmem_limit_bytes=mebibytes * 1024 * 1024)


def over_members(x):
    return [lax.ppermute(x, "ma", [(i, (i + s) % MA) for i in range(MA)]) for s in range(1, MA)]


def local(
    ensemble, wind_field, obs_value, obs_var, obs_region, obs_cell, block_order, localization
):
    both = jnp.concatenate([ensemble, wind_field], axis=0)
    forward = [(i, (i + 1) % GX) for i in range(GX)]
    backward = [(i, (i - 1) % GX) for i in range(GX)]
    low = lax.ppermute(both[:, :, 2:], "gx", forward)
    high = lax.ppermute(both[:, :, :2], "gx", backward)
    prepared = pl.pallas_call(
        prepare_kernel,
        out_shape=(
            jax.ShapeDtypeStruct((40, LANES), F32),
            jax.ShapeDtypeStruct((4 * BLOCKS, OBS), F32),
        ),
        in_specs=[pl.BlockSpec(memory_space=pltpu.HBM)] * 6,
        out_specs=(VMEM,) * 2,
        scratch_shapes=[pltpu.SMEM((BLOCKS,), jnp.int32)]
        + [pltpu.VMEM((BLOCKS, OBS), jnp.int32)] * 2
        + [pltpu.VMEM((BLOCKS, OBS), F32)] * 3
        + [pltpu.SemaphoreType.DMA((6,))],
        compiler_params=params(60),
        cost_estimate=pl.CostEstimate(flops=10_000_000, bytes_accessed=2_000_000, transcendentals=0),
        name="prepare",
    )(block_order, obs_cell, obs_region, obs_value, obs_var, localization.reshape(BLOCKS, OBS))
    low, high, prepared = lax.optimization_barrier((low, high, prepared))
    index, observed = prepared
    own = jnp.concatenate([low, both, high], axis=2).reshape(-1, LANES)
    beside = other_core(own)

    state, picked = pl.pallas_call(
        advect_kernel,
        out_shape=(
            jax.ShapeDtypeStruct((OWN * 8, LANES), F32),
            jax.ShapeDtypeStruct((GX * SENT, LANES), F32),
        ),
        in_specs=[VMEM] * 3,
        out_specs=(VMEM, VMEM),
        scratch_shapes=[pltpu.VMEM((2, 24 * 8, LANES), F32)],
        compiler_params=params(4),
        cost_estimate=pl.CostEstimate(flops=10_000_000, bytes_accessed=1_000_000, transcendentals=0),
        name="advect",
    )(own, beside, index)

    parts = lax.all_to_all(picked.reshape(GX, 1, SENT * LANES), "gx", 0, 0, tiled=True)
    parts = parts.reshape(-1, LANES)
    owned = pl.pallas_call(
        owner_kernel,
        out_shape=jax.ShapeDtypeStruct((MA * GX * CHUNK, LANES), F32),
        in_specs=[VMEM],
        out_specs=VMEM,
        compiler_params=params(4),
        name="owner",
    )(parts)
    weights = pl.pallas_call(
        weights_kernel,
        out_shape=jax.ShapeDtypeStruct((QUARTER * GX, LANES), F32),
        in_specs=[VMEM],
        out_specs=VMEM,
        compiler_params=params(4),
        name="weights",
    )(parts)
    came = lax.all_to_all(
        owned.reshape(MA * GX, 1, CHUNK * LANES), ("ma", "gx"), 0, 0, tiled=True
    ).reshape(-1, LANES)
    weights = [weights] + over_members(weights)
    weights = jnp.concatenate(weights, axis=0)
    came, weights, late = lax.optimization_barrier((came, weights, state))
    gathered = over_members(late)
    tapers = pl.pallas_call(
        tapers_kernel,
        out_shape=jax.ShapeDtypeStruct((TAPERS + (BLOCKS - 1) * OBS, LANES), BF16),
        in_specs=[VMEM] * 3,
        out_specs=VMEM,
        compiler_params=params(4),
        cost_estimate=pl.CostEstimate(flops=1000, bytes_accessed=1000, transcendentals=0),
        name="tapers",
    )(weights, other_core(weights), observed)
    came_beside = other_core(came)

    out = pl.pallas_call(
        filter_kernel,
        out_shape=jax.ShapeDtypeStruct((OWN * 8, LANES), F32),
        in_specs=[VMEM] * 8,
        out_specs=VMEM,
        scratch_shapes=[
            pltpu.VMEM((BLOCKS * OBS, LANES), F32),
            pltpu.VMEM((OBS, LANES), BF16),
            pltpu.VMEM((OBS, 2 * LANES), BF16),
            pltpu.VMEM((LANES, LANES), F32),
            pltpu.VMEM((LANES, OBS), F32),
        ],
        compiler_params=params(32),
        cost_estimate=pl.CostEstimate(flops=3_000_000_000, bytes_accessed=4_000_000, transcendentals=0),
        name="filter",
    )(came, came_beside, tapers, observed, *gathered, late)
    return out.reshape(ensemble.shape)


def solution(mesh):
    in_specs = (
        P("ma", None, "gx", "gy"),
        P(None, None, "gx", "gy"),
        P(),
        P(),
        P(),
        P(),
        P(),
        P("gx", "gy", None, None),
    )
    out_specs = P("ma", None, "gx", "gy")
    return jax.shard_map(local, mesh=mesh, in_specs=in_specs, out_specs=out_specs, check_vma=False)
```

```python
import jax
import jax.numpy as jnp
from jax import lax
from jax.experimental import pallas as pl
from jax.experimental.pallas import tpu as pltpu
from jax.sharding import PartitionSpec as P

MEMBERS = 80
OWN = 20
BLOCKS = 4
OBS = 1024
CELLS = 1024
GX = 64
MA = 4
LANES = 128
GROUPS = OBS // LANES
KAPPA = 0.025
CHUNK = 5
HALF = OWN * 2 * GROUPS
QUARTER = (BLOCKS - 1) * GROUPS // MA
SENT = CHUNK + QUARTER
TAPERS = (BLOCKS - 1) * GROUPS * 2 * LANES
ROWS_O = 1024
F32 = jnp.float32
BF16 = jnp.bfloat16
VMEM = pl.BlockSpec(memory_space=pltpu.VMEM)
SMEM = pl.BlockSpec(memory_space=pltpu.SMEM)


def split(value):
    high = value.astype(BF16)
    return high, (value - high.astype(F32)).astype(BF16)


def dot_nn(a, b):
    return lax.dot_general(a, b, (((1,), (0,)), ((), ())), preferred_element_type=F32)


def dot_nt(a, b):
    return lax.dot_general(a, b, (((1,), (1,)), ((), ())), preferred_element_type=F32)


def block_row(ref, b, columns):
    row = ref[pl.ds(0, 1), columns]
    for i in range(1, BLOCKS):
        row = jnp.where(b == i, ref[pl.ds(i, 1), columns], row)
    return row


def advect_kernel(own_ref, other_ref, index_ref, state_ref, picked_ref, work):
    lane = lax.broadcasted_iota(jnp.int32, (8, LANES), 1)
    first, last = lane == 0, lane == LANES - 1

    def step(q, beside, wind):
        u_up, u_down, v_up, v_down = wind
        west, east = pltpu.roll(q, 1, 0), pltpu.roll(q, 7, 0)
        south = jnp.where(first, pltpu.roll(beside, 1, 1), pltpu.roll(q, 1, 1))
        north = jnp.where(last, pltpu.roll(beside, LANES - 1, 1), pltpu.roll(q, LANES - 1, 1))
        return (
            q
            - u_up * (q - west)
            - u_down * (east - q)
            - v_up * (q - south)
            - v_down * (north - q)
            + KAPPA * (east + west + north + south - 4.0 * q)
        )

    def winds(ref, level):
        u = ref[pl.ds((OWN * 2 + level) * 8, 8), :]
        v = ref[pl.ds((OWN * 2 + 2 + level) * 8, 8), :]
        return jnp.maximum(u, 0.0), jnp.minimum(u, 0.0), jnp.maximum(v, 0.0), jnp.minimum(v, 0.0)

    for side in range(2):
        work[side, pl.ds(OWN * 8, 32), :] = jnp.zeros((32, LANES), F32)
    for level in range(2):
        wind, wind_o = winds(own_ref, level), winds(other_ref, level)
        for m in range(OWN):
            at = (m * 2 + level) * 8
            q, q_o = own_ref[pl.ds(at, 8), :], other_ref[pl.ds(at, 8), :]
            once, once_o = step(q, q_o, wind), step(q_o, q, wind_o)
            twice, twice_o = step(once, once_o, wind), step(once_o, once, wind_o)
            at = pl.ds(m * 8 + level * 4, 4)
            state_ref[at, :] = twice[2:6]
            work[0, at, :] = twice[2:6]
            work[1, at, :] = twice_o[2:6]

    eight = jnp.concatenate(
        [jnp.zeros((CHUNK, LANES), F32), index_ref[pl.ds(32, QUARTER), :]] * 8, axis=0
    )
    for i in range(GX // 8):
        picked_ref[pl.ds(i * 8 * SENT, 8 * SENT), :] = eight
    for g in range(2 * GROUPS):
        y = jnp.broadcast_to(index_ref[pl.ds(g, 1), :].astype(jnp.int32), (24, LANES))
        part = jnp.broadcast_to(index_ref[pl.ds(g + 16, 1), :], (24, LANES))
        total = jnp.zeros((24, LANES), F32)
        for c in range(16):
            source = work[c // 8, pl.ds(c % 8, 24, stride=8), :]
            found = jnp.take_along_axis(source, y, axis=1, mode="promise_in_bounds")
            total = jnp.where(part == c, found, total)
        for i in range(MA):
            at = (i * 2 * GROUPS + g) * SENT
            picked_ref[pl.ds(at, CHUNK), :] = total[i * CHUNK : (i + 1) * CHUNK]


def prepare_kernel(*refs):
    sources, results, copies, done = refs[:6], refs[6:8], refs[8:14], refs[14]
    moves = [
        pltpu.make_async_copy(source, copy, done.at[i])
        for i, (source, copy) in enumerate(zip(sources, copies))
    ]
    for move in moves:
        move.start()
    for move in moves:
        move.wait()
    order, cell_ref, region_ref, value_ref, var_ref, taper_ref = copies
    index_ref, obs_ref = results
    gx, gy, q = lax.axis_index("gx"), lax.axis_index("gy"), lax.axis_index("ma")
    for k in range(2):
        b = order[gy * 2 + k]
        for g in range(GROUPS):
            columns = pl.ds(g * LANES, LANES)
            cell, region = block_row(cell_ref, b, columns), block_row(region_ref, b, columns)
            part = jnp.right_shift(cell, 7) + jnp.where(jnp.bitwise_and(region, 1) == gy, 0, 8)
            part = jnp.where(jnp.right_shift(region, 1) == gx, part, -1)
            at = k * GROUPS + g
            index_ref[pl.ds(at, 1), :] = jnp.bitwise_and(cell, LANES - 1).astype(F32)
            index_ref[pl.ds(at + 16, 1), :] = part.astype(F32)

    for k in range(BLOCKS):
        for i, ref in enumerate((value_ref, var_ref, taper_ref)):
            obs_ref[pl.ds(i * BLOCKS + k, 1), :] = block_row(ref, order[k], pl.ds(0, OBS))
        region = block_row(region_ref, order[k], pl.ds(0, OBS))
        place = jnp.where(jnp.bitwise_and(region, 1) == gy, 0, GX) + jnp.right_shift(region, 1)
        obs_ref[pl.ds(3 * BLOCKS + k, 1), :] = place.astype(F32)

    index_ref[pl.ds(32, 8), :] = jnp.zeros((8, LANES), F32)
    for i in range(QUARTER):
        tile = q * QUARTER + i
        b, g = order[tile // GROUPS], tile % GROUPS
        row = block_row(taper_ref, b, pl.ds(0, LANES))
        for j in range(1, GROUPS):
            row = jnp.where(g == j, block_row(taper_ref, b, pl.ds(j * LANES, LANES)), row)
        index_ref[pl.ds(32 + i, 1), :] = row


def weights_kernel(parts_ref, weights_ref):
    for i in range(QUARTER):
        weights_ref[pl.ds(i * GX, GX), :] = parts_ref[pl.ds(CHUNK + i, GX, stride=SENT), :]


def owner_kernel(parts_ref, out_ref):
    total = parts_ref[pl.ds(0, 8 * SENT), :]
    for i in range(1, GX // 8):
        total = total + parts_ref[pl.ds(i * 8 * SENT, 8 * SENT), :]
    part = total[0:CHUNK]
    for i in range(1, 8):
        part = part + total[i * SENT : i * SENT + CHUNK]
    eight = jnp.concatenate([part] * 8, axis=0)
    for i in range(GX * MA // 8):
        out_ref[pl.ds(i * 8 * CHUNK, 8 * CHUNK), :] = eight


def tapers_kernel(own_ref, other_ref, obs_ref, out_ref):
    q = lax.axis_index("ma")
    for shift in range(MA):
        for i in range(QUARTER):
            tile = jnp.bitwise_and(q - shift, MA - 1) * QUARTER + i
            for side, ref in enumerate((own_ref, other_ref)):
                high, low = split(ref[pl.ds((shift * QUARTER + i) * GX, GX), :])
                at = pl.multiple_of(tile * 2 * LANES, 2 * LANES) + side * GX
                out_ref[pl.ds(pl.multiple_of(at, GX), GX), :] = high
                out_ref[pl.ds(pl.multiple_of(at + LANES, GX), GX), :] = low

    rows = lax.broadcasted_iota(jnp.int32, (LANES, LANES), 0).astype(F32)
    for k in range(1, BLOCKS):
        for g in range(GROUPS):
            place = obs_ref[pl.ds(3 * BLOCKS + k, 1), pl.ds(g * LANES, LANES)]
            hot = (rows == jnp.broadcast_to(place, (LANES, LANES))).astype(F32).T.astype(BF16)
            out_ref[pl.ds(TAPERS + ((k - 1) * GROUPS + g) * LANES, LANES), :] = hot


def filter_kernel(
    came_ref,
    came_o_ref,
    tapers,
    obs_ref,
    gathered_1,
    gathered_2,
    gathered_3,
    state_ref,
    out_ref,
    xt,
    b_high,
    b_both,
    increments,
    first_block,
):
    gy = lax.axis_index("gy")
    denom = MEMBERS - 1.0

    def load_half(ref, half):
        for g in range(16):
            block = jnp.concatenate(
                [ref[pl.ds(g * CHUNK + i, 16, stride=16 * CHUNK), :] for i in range(CHUNK)], axis=0
            )
            mean = jnp.mean(block, axis=0, keepdims=True)
            full = jnp.concatenate(
                [block - mean, mean, jnp.zeros((LANES - MEMBERS - 1, LANES), F32)], axis=0
            )
            if half == 0 and g < GROUPS:
                first_block[:, pl.ds(g * LANES, LANES)] = full
            else:
                xt[pl.ds((half * 16 + g) * LANES, LANES), :] = full.T

    @pl.when(gy == 0)
    def _():
        load_half(came_ref, 0)
        load_half(came_o_ref, 1)

    @pl.when(gy == 1)
    def _():
        load_half(came_o_ref, 0)
        load_half(came_ref, 1)

    lane = lax.broadcasted_iota(jnp.int32, (ROWS_O, LANES), 1)
    member_row = lax.broadcasted_iota(jnp.int32, (LANES, OBS), 0)
    increments[...] = jnp.zeros((LANES, LANES), F32)
    for k in range(BLOCKS):
        if k == 0:
            now = first_block[...]
        else:
            now = jnp.concatenate(
                [xt[pl.ds((k * GROUPS + g) * LANES, LANES), :].T for g in range(GROUPS)], axis=1
            )
        anomaly = jnp.where(member_row < MEMBERS, now, 0.0)
        mean = now[MEMBERS : MEMBERS + 1]
        variance = jnp.sum(anomaly * anomaly, axis=0, keepdims=True) / denom
        error_var = obs_ref[pl.ds(BLOCKS + k, 1), :]
        total_var = variance + error_var
        shrink = 1.0 / (1.0 + jnp.sqrt(error_var / total_var))
        scale = 1.0 / (denom * total_var)
        gain_mean = (obs_ref[pl.ds(k, 1), :] - mean) * scale
        gain = jnp.where(member_row == MEMBERS, gain_mean, -(shrink * scale) * anomaly)
        gain_high, gain_low = split(gain)

        tapered_high, tapered_low = split(anomaly * obs_ref[pl.ds(2 * BLOCKS + k, 1), :])
        mixing = (
            dot_nt(gain_high, tapered_high)
            + dot_nt(gain_low, tapered_high)
            + dot_nt(gain_high, tapered_low)
        )
        e = increments[...]
        increments[...] = e + mixing + jnp.dot(
            mixing, e, precision=lax.Precision.HIGHEST, preferred_element_type=F32
        )

        if k == BLOCKS - 1:
            continue
        a_high, a_low = split(anomaly)
        left = jnp.concatenate([a_high[:MEMBERS], a_high[:MEMBERS], a_low[:MEMBERS], jnp.zeros((16, OBS), BF16)], axis=0)
        b_high[...] = gain_high.astype(F32).T.astype(BF16)
        b_both[:, pl.ds(0, LANES)] = b_high[...]
        b_both[:, pl.ds(LANES, LANES)] = gain_low.astype(F32).T.astype(BF16)

        def chunk(i, carry, k=k, left=left):
            taper = jnp.concatenate([tapers[pl.ds((k * GROUPS + g) * 2 * LANES, 2 * LANES), :] for g in range(GROUPS)], axis=1)
            at = pl.multiple_of((k + 1) * OBS + i * ROWS_O, ROWS_O)
            x = xt[pl.ds(at, ROWS_O), :]
            clean = jnp.where(lane < MEMBERS, x, 0.0)
            high = clean.astype(BF16).astype(F32)
            low = (clean - high)
            low_rolled = pltpu.roll(low, MEMBERS, 1)
            first = jnp.where(lane < MEMBERS, high, low_rolled)
            second = jnp.where(lane < 2 * MEMBERS - LANES, low_rolled, pltpu.roll(high, 2 * MEMBERS - LANES, 1))
            second = jnp.where(lane < 3 * MEMBERS - LANES, second, 0.0)
            query = jnp.concatenate([first, second], axis=1).astype(BF16)
            hot = tapers[pl.ds(pl.multiple_of(at + TAPERS - OBS, ROWS_O), ROWS_O), :]
            hot = jnp.concatenate([hot, hot], axis=1)
            weight = dot_nn(query, left) * dot_nn(hot, taper)
            w_high, w_low = split(weight)
            both = dot_nn(w_high, b_both[...])
            xt[pl.ds(at, ROWS_O), :] = (
                x + both[:, :LANES] + both[:, LANES:] + dot_nn(w_low, b_high[...])
            )
            return carry

        lax.fori_loop(0, (BLOCKS - 1 - k) * OBS // ROWS_O, chunk, 0)

    q = lax.axis_index("ma")
    e = increments[...]
    total = e + e[MEMBERS : MEMBERS + 1]
    row = lax.broadcasted_iota(jnp.int32, (24, LANES), 0)
    col = lax.broadcasted_iota(jnp.int32, (24, LANES), 1)
    fifth = sum(jnp.where(row >= i * CHUNK, 1, 0) for i in range(1, MA))
    member = (row - fifth * CHUNK) * 16 + q * MA + fifth
    chosen = jnp.where((col == member) & (row < OWN), 1.0, 0.0)
    transform = jnp.dot(chosen, total, precision=lax.Precision.HIGHEST, preferred_element_type=F32)
    row = lax.broadcasted_iota(jnp.int32, (LANES, LANES), 0)
    col = lax.broadcasted_iota(jnp.int32, (LANES, LANES), 1)
    back = sum(jnp.where(col >= i * OWN, 1, 0) for i in range(1, MA))
    place = col - back * OWN
    fifth = sum(jnp.where(place >= i * CHUNK, 1, 0) for i in range(1, MA))
    member = (place - fifth * CHUNK) * 16 + jnp.bitwise_and(q - back, MA - 1) * MA + fifth
    shuffle = jnp.where((row == member) & (col < MEMBERS), 1.0, 0.0)
    transform = jnp.dot(transform, shuffle, precision=lax.Precision.HIGHEST, preferred_element_type=F32)
    tiles = []
    for c in range(8):
        at = pl.ds(c, OWN, stride=8)
        tile = jnp.concatenate(
            [ref[at, :] for ref in (state_ref, gathered_1, gathered_2, gathered_3)], axis=0
        )
        tiles.append(tile - jnp.mean(tile, axis=0, keepdims=True))
    centered = jnp.concatenate(
        [jnp.concatenate(tiles, axis=1), jnp.zeros((LANES - MEMBERS, CELLS), F32)], axis=0
    )
    c_high, c_low = split(centered)
    t_high, t_low = split(transform)
    update = dot_nn(t_high, c_high) + dot_nn(t_low, c_high) + dot_nn(t_high, c_low)
    for c in range(8):
        at = pl.ds(c, OWN, stride=8)
        out_ref[at, :] = state_ref[at, :] + update[:OWN, c * LANES : (c + 1) * LANES]


def other_core(x):
    return lax.ppermute(x, "gy", [(0, 1), (1, 0)])


def params(mebibytes):
    return pltpu.CompilerParams(vmem_limit_bytes=mebibytes * 1024 * 1024)


def over_members(x):
    return [lax.ppermute(x, "ma", [(i, (i + s) % MA) for i in range(MA)]) for s in range(1, MA)]


def local(
    ensemble, wind_field, obs_value, obs_var, obs_region, obs_cell, block_order, localization
):
    both = jnp.concatenate([ensemble, wind_field], axis=0)
    forward = [(i, (i + 1) % GX) for i in range(GX)]
    backward = [(i, (i - 1) % GX) for i in range(GX)]
    low = lax.ppermute(both[:, :, 2:], "gx", forward)
    high = lax.ppermute(both[:, :, :2], "gx", backward)
    prepared = pl.pallas_call(
        prepare_kernel,
        out_shape=(
            jax.ShapeDtypeStruct((40, LANES), F32),
            jax.ShapeDtypeStruct((4 * BLOCKS, OBS), F32),
        ),
        in_specs=[pl.BlockSpec(memory_space=pltpu.HBM)] * 6,
        out_specs=(VMEM,) * 2,
        scratch_shapes=[pltpu.SMEM((BLOCKS,), jnp.int32)]
        + [pltpu.VMEM((BLOCKS, OBS), jnp.int32)] * 2
        + [pltpu.VMEM((BLOCKS, OBS), F32)] * 3
        + [pltpu.SemaphoreType.DMA((6,))],
        compiler_params=params(60),
        cost_estimate=pl.CostEstimate(flops=10_000_000, bytes_accessed=2_000_000, transcendentals=0),
        name="prepare",
    )(block_order, obs_cell, obs_region, obs_value, obs_var, localization.reshape(BLOCKS, OBS))
    low, high, prepared = lax.optimization_barrier((low, high, prepared))
    index, observed = prepared
    own = jnp.concatenate([low, both, high], axis=2).reshape(-1, LANES)
    beside = other_core(own)

    state, picked = pl.pallas_call(
        advect_kernel,
        out_shape=(
            jax.ShapeDtypeStruct((OWN * 8, LANES), F32),
            jax.ShapeDtypeStruct((GX * SENT, LANES), F32),
        ),
        in_specs=[VMEM] * 3,
        out_specs=(VMEM, VMEM),
        scratch_shapes=[pltpu.VMEM((2, 24 * 8, LANES), F32)],
        compiler_params=params(4),
        cost_estimate=pl.CostEstimate(flops=10_000_000, bytes_accessed=1_000_000, transcendentals=0),
        name="advect",
    )(own, beside, index)

    parts = lax.all_to_all(picked.reshape(GX, 1, SENT * LANES), "gx", 0, 0, tiled=True)
    gathered = over_members(state)
    parts, gathered = lax.optimization_barrier((parts, gathered))
    parts = parts.reshape(-1, LANES)
    owned = pl.pallas_call(
        owner_kernel,
        out_shape=jax.ShapeDtypeStruct((MA * GX * CHUNK, LANES), F32),
        in_specs=[VMEM],
        out_specs=VMEM,
        compiler_params=params(4),
        name="owner",
    )(parts)
    weights = pl.pallas_call(
        weights_kernel,
        out_shape=jax.ShapeDtypeStruct((QUARTER * GX, LANES), F32),
        in_specs=[VMEM],
        out_specs=VMEM,
        compiler_params=params(4),
        name="weights",
    )(parts)
    came = lax.all_to_all(
        owned.reshape(MA * GX, 1, CHUNK * LANES), ("ma", "gx"), 0, 0, tiled=True
    ).reshape(-1, LANES)
    weights = jnp.concatenate([weights] + over_members(weights), axis=0)
    came, weights = lax.optimization_barrier((came, weights))
    tapers = pl.pallas_call(
        tapers_kernel,
        out_shape=jax.ShapeDtypeStruct((TAPERS + (BLOCKS - 1) * OBS, LANES), BF16),
        in_specs=[VMEM] * 3,
        out_specs=VMEM,
        compiler_params=params(4),
        cost_estimate=pl.CostEstimate(flops=1000, bytes_accessed=1000, transcendentals=0),
        name="tapers",
    )(weights, other_core(weights), observed)
    came_beside = other_core(came)

    out = pl.pallas_call(
        filter_kernel,
        out_shape=jax.ShapeDtypeStruct((OWN * 8, LANES), F32),
        in_specs=[VMEM] * 8,
        out_specs=VMEM,
        scratch_shapes=[
            pltpu.VMEM((BLOCKS * OBS, LANES), F32),
            pltpu.VMEM((OBS, LANES), BF16),
            pltpu.VMEM((OBS, 2 * LANES), BF16),
            pltpu.VMEM((LANES, LANES), F32),
            pltpu.VMEM((LANES, OBS), F32),
        ],
        compiler_params=params(32),
        cost_estimate=pl.CostEstimate(flops=3_000_000_000, bytes_accessed=4_000_000, transcendentals=0),
        name="filter",
    )(came, came_beside, tapers, observed, *gathered, state)
    return out.reshape(ensemble.shape)


def solution(mesh):
    in_specs = (
        P("ma", None, "gx", "gy"),
        P(None, None, "gx", "gy"),
        P(),
        P(),
        P(),
        P(),
        P(),
        P("gx", "gy", None, None),
    )
    out_specs = P("ma", None, "gx", "gy")
    return jax.shard_map(local, mesh=mesh, in_specs=in_specs, out_specs=out_specs, check_vma=False)
```

```python
import jax
import jax.numpy as jnp
from jax import lax
from jax.experimental import pallas as pl
from jax.experimental.pallas import tpu as pltpu
from jax.sharding import PartitionSpec as P

MEMBERS = 80
OWN = 20
BLOCKS = 4
OBS = 1024
CELLS = 1024
GX = 64
MA = 4
LANES = 128
GROUPS = OBS // LANES
KAPPA = 0.025
CHUNK = 5
HALF = OWN * 2 * GROUPS
QUARTER = (BLOCKS - 1) * GROUPS // MA
SENT = CHUNK + QUARTER
TAPERS = (BLOCKS - 1) * GROUPS * 2 * LANES
ROWS_O = 1024
F32 = jnp.float32
BF16 = jnp.bfloat16
VMEM = pl.BlockSpec(memory_space=pltpu.VMEM)
SMEM = pl.BlockSpec(memory_space=pltpu.SMEM)


def split(value):
    high = value.astype(BF16)
    return high, (value - high.astype(F32)).astype(BF16)


def dot_nn(a, b):
    return lax.dot_general(a, b, (((1,), (0,)), ((), ())), preferred_element_type=F32)


def dot_nt(a, b):
    return lax.dot_general(a, b, (((1,), (1,)), ((), ())), preferred_element_type=F32)


def block_row(ref, b, columns):
    row = ref[pl.ds(0, 1), columns]
    for i in range(1, BLOCKS):
        row = jnp.where(b == i, ref[pl.ds(i, 1), columns], row)
    return row


def advect_kernel(own_ref, other_ref, index_ref, state_ref, picked_ref, work):
    lane = lax.broadcasted_iota(jnp.int32, (8, LANES), 1)
    first, last = lane == 0, lane == LANES - 1

    def step(q, beside, wind):
        u_up, u_down, v_up, v_down = wind
        west, east = pltpu.roll(q, 1, 0), pltpu.roll(q, 7, 0)
        south = jnp.where(first, pltpu.roll(beside, 1, 1), pltpu.roll(q, 1, 1))
        north = jnp.where(last, pltpu.roll(beside, LANES - 1, 1), pltpu.roll(q, LANES - 1, 1))
        return (
            q
            - u_up * (q - west)
            - u_down * (east - q)
            - v_up * (q - south)
            - v_down * (north - q)
            + KAPPA * (east + west + north + south - 4.0 * q)
        )

    def winds(ref, level):
        u = ref[pl.ds((OWN * 2 + level) * 8, 8), :]
        v = ref[pl.ds((OWN * 2 + 2 + level) * 8, 8), :]
        return jnp.maximum(u, 0.0), jnp.minimum(u, 0.0), jnp.maximum(v, 0.0), jnp.minimum(v, 0.0)

    for side in range(2):
        work[side, pl.ds(OWN * 8, 32), :] = jnp.zeros((32, LANES), F32)
    for level in range(2):
        wind, wind_o = winds(own_ref, level), winds(other_ref, level)
        for m in range(OWN):
            at = (m * 2 + level) * 8
            q, q_o = own_ref[pl.ds(at, 8), :], other_ref[pl.ds(at, 8), :]
            once, once_o = step(q, q_o, wind), step(q_o, q, wind_o)
            twice, twice_o = step(once, once_o, wind), step(once_o, once, wind_o)
            at = pl.ds(m * 8 + level * 4, 4)
            state_ref[at, :] = twice[2:6]
            work[0, at, :] = twice[2:6]
            work[1, at, :] = twice_o[2:6]

    eight = jnp.concatenate(
        [jnp.zeros((CHUNK, LANES), F32), index_ref[pl.ds(32, QUARTER), :]] * 8, axis=0
    )
    for i in range(GX // 8):
        picked_ref[pl.ds(i * 8 * SENT, 8 * SENT), :] = eight
    for g in range(2 * GROUPS):
        y = jnp.broadcast_to(index_ref[pl.ds(g, 1), :].astype(jnp.int32), (24, LANES))
        part = jnp.broadcast_to(index_ref[pl.ds(g + 16, 1), :], (24, LANES))
        total = jnp.zeros((24, LANES), F32)
        for c in range(16):
            source = work[c // 8, pl.ds(c % 8, 24, stride=8), :]
            found = jnp.take_along_axis(source, y, axis=1, mode="promise_in_bounds")
            total = jnp.where(part == c, found, total)
        for i in range(MA):
            at = (i * 2 * GROUPS + g) * SENT
            picked_ref[pl.ds(at, CHUNK), :] = total[i * CHUNK : (i + 1) * CHUNK]


def prepare_kernel(*refs):
    sources, results, copies, done = refs[:6], refs[6:8], refs[8:14], refs[14]
    moves = [
        pltpu.make_async_copy(source, copy, done.at[i])
        for i, (source, copy) in enumerate(zip(sources, copies))
    ]
    for move in moves:
        move.start()
    for move in moves:
        move.wait()
    order, cell_ref, region_ref, value_ref, var_ref, taper_ref = copies
    index_ref, obs_ref = results
    gx, gy, q = lax.axis_index("gx"), lax.axis_index("gy"), lax.axis_index("ma")
    for k in range(2):
        b = order[gy * 2 + k]
        for g in range(GROUPS):
            columns = pl.ds(g * LANES, LANES)
            cell, region = block_row(cell_ref, b, columns), block_row(region_ref, b, columns)
            part = jnp.right_shift(cell, 7) + jnp.where(jnp.bitwise_and(region, 1) == gy, 0, 8)
            part = jnp.where(jnp.right_shift(region, 1) == gx, part, -1)
            at = k * GROUPS + g
            index_ref[pl.ds(at, 1), :] = jnp.bitwise_and(cell, LANES - 1).astype(F32)
            index_ref[pl.ds(at + 16, 1), :] = part.astype(F32)

    for k in range(BLOCKS):
        for i, ref in enumerate((value_ref, var_ref, taper_ref)):
            obs_ref[pl.ds(i * BLOCKS + k, 1), :] = block_row(ref, order[k], pl.ds(0, OBS))
        region = block_row(region_ref, order[k], pl.ds(0, OBS))
        place = jnp.where(jnp.bitwise_and(region, 1) == gy, 0, GX) + jnp.right_shift(region, 1)
        obs_ref[pl.ds(3 * BLOCKS + k, 1), :] = place.astype(F32)

    index_ref[pl.ds(32, 8), :] = jnp.zeros((8, LANES), F32)
    for i in range(QUARTER):
        tile = q * QUARTER + i
        b, g = order[tile // GROUPS], tile % GROUPS
        row = block_row(taper_ref, b, pl.ds(0, LANES))
        for j in range(1, GROUPS):
            row = jnp.where(g == j, block_row(taper_ref, b, pl.ds(j * LANES, LANES)), row)
        index_ref[pl.ds(32 + i, 1), :] = row


def weights_kernel(parts_ref, weights_ref):
    for i in range(QUARTER):
        weights_ref[pl.ds(i * GX, GX), :] = parts_ref[pl.ds(CHUNK + i, GX, stride=SENT), :]


def owner_kernel(parts_ref, out_ref):
    total = parts_ref[pl.ds(0, 8 * SENT), :]
    for i in range(1, GX // 8):
        total = total + parts_ref[pl.ds(i * 8 * SENT, 8 * SENT), :]
    part = total[0:CHUNK]
    for i in range(1, 8):
        part = part + total[i * SENT : i * SENT + CHUNK]
    eight = jnp.concatenate([part] * 8, axis=0)
    for i in range(GX * MA // 8):
        out_ref[pl.ds(i * 8 * CHUNK, 8 * CHUNK), :] = eight


def tapers_kernel(own_ref, other_ref, obs_ref, out_ref):
    q = lax.axis_index("ma")
    for shift in range(MA):
        for i in range(QUARTER):
            tile = jnp.bitwise_and(q - shift, MA - 1) * QUARTER + i
            for side, ref in enumerate((own_ref, other_ref)):
                high, low = split(ref[pl.ds((shift * QUARTER + i) * GX, GX), :])
                at = pl.multiple_of(tile * 2 * LANES, 2 * LANES) + side * GX
                out_ref[pl.ds(pl.multiple_of(at, GX), GX), :] = high
                out_ref[pl.ds(pl.multiple_of(at + LANES, GX), GX), :] = low

    rows = lax.broadcasted_iota(jnp.int32, (LANES, LANES), 0).astype(F32)
    for k in range(1, BLOCKS):
        for g in range(GROUPS):
            place = obs_ref[pl.ds(3 * BLOCKS + k, 1), pl.ds(g * LANES, LANES)]
            hot = (rows == jnp.broadcast_to(place, (LANES, LANES))).astype(F32).T.astype(BF16)
            out_ref[pl.ds(TAPERS + ((k - 1) * GROUPS + g) * LANES, LANES), :] = hot


def filter_kernel(
    came_ref,
    came_o_ref,
    tapers,
    obs_ref,
    gathered_1,
    gathered_2,
    gathered_3,
    state_ref,
    out_ref,
    xt,
    b_high,
    b_both,
    increments,
    first_block,
):
    gy = lax.axis_index("gy")
    denom = MEMBERS - 1.0

    def load_half(ref, half):
        for g in range(16):
            block = jnp.concatenate(
                [ref[pl.ds(g * CHUNK + i, 16, stride=16 * CHUNK), :] for i in range(CHUNK)], axis=0
            )
            mean = jnp.mean(block, axis=0, keepdims=True)
            full = jnp.concatenate(
                [block - mean, mean, jnp.zeros((LANES - MEMBERS - 1, LANES), F32)], axis=0
            )
            if half == 0 and g < GROUPS:
                first_block[:, pl.ds(g * LANES, LANES)] = full
            else:
                xt[pl.ds((half * 16 + g) * LANES, LANES), :] = full.T

    @pl.when(gy == 0)
    def _():
        load_half(came_ref, 0)
        load_half(came_o_ref, 1)

    @pl.when(gy == 1)
    def _():
        load_half(came_o_ref, 0)
        load_half(came_ref, 1)

    lane = lax.broadcasted_iota(jnp.int32, (ROWS_O, LANES), 1)
    member_row = lax.broadcasted_iota(jnp.int32, (LANES, OBS), 0)
    for k in range(BLOCKS):
        if k == 0:
            now = first_block[...]
        else:
            now = jnp.concatenate(
                [xt[pl.ds((k * GROUPS + g) * LANES, LANES), :].T for g in range(GROUPS)], axis=1
            )
        anomaly = jnp.where(member_row < MEMBERS, now, 0.0)
        mean = now[MEMBERS : MEMBERS + 1]
        variance = jnp.sum(anomaly * anomaly, axis=0, keepdims=True) / denom
        error_var = obs_ref[pl.ds(BLOCKS + k, 1), :]
        total_var = variance + error_var
        shrink = 1.0 / (1.0 + jnp.sqrt(error_var / total_var))
        scale = 1.0 / (denom * total_var)
        gain_mean = (obs_ref[pl.ds(k, 1), :] - mean) * scale
        gain = jnp.where(member_row == MEMBERS, gain_mean, -(shrink * scale) * anomaly)
        gain_high, gain_low = split(gain)

        tapered_high, tapered_low = split(anomaly * obs_ref[pl.ds(2 * BLOCKS + k, 1), :])
        mixing = (
            dot_nt(gain_high, tapered_high)
            + dot_nt(gain_low, tapered_high)
            + dot_nt(gain_high, tapered_low)
        )
        if k > 0:
            e = increments[...]
            e_high, e_low = split(e)
            m_high, m_low = split(mixing)
            mixing = mixing + e + dot_nn(m_high, e_high) + dot_nn(m_low, e_high) + dot_nn(m_high, e_low)
        increments[...] = mixing

        if k == BLOCKS - 1:
            continue
        a_high, a_low = split(anomaly)
        left = jnp.concatenate([a_high[:MEMBERS], a_high[:MEMBERS], a_low[:MEMBERS], jnp.zeros((16, OBS), BF16)], axis=0)
        b_high[...] = gain_high.astype(F32).T.astype(BF16)
        b_both[:, pl.ds(0, LANES)] = b_high[...]
        b_both[:, pl.ds(LANES, LANES)] = gain_low.astype(F32).T.astype(BF16)

        def chunk(i, carry, k=k, left=left):
            taper = jnp.concatenate([tapers[pl.ds((k * GROUPS + g) * 2 * LANES, 2 * LANES), :] for g in range(GROUPS)], axis=1)
            at = pl.multiple_of((k + 1) * OBS + i * ROWS_O, ROWS_O)
            x = xt[pl.ds(at, ROWS_O), :]
            clean = jnp.where(lane < MEMBERS, x, 0.0)
            high = clean.astype(BF16).astype(F32)
            low = (clean - high)
            low_rolled = pltpu.roll(low, MEMBERS, 1)
            first = jnp.where(lane < MEMBERS, high, low_rolled)
            second = jnp.where(lane < 2 * MEMBERS - LANES, low_rolled, pltpu.roll(high, 2 * MEMBERS - LANES, 1))
            second = jnp.where(lane < 3 * MEMBERS - LANES, second, 0.0)
            query = jnp.concatenate([first, second], axis=1).astype(BF16)
            hot = tapers[pl.ds(pl.multiple_of(at + TAPERS - OBS, ROWS_O), ROWS_O), :]
            hot = jnp.concatenate([hot, hot], axis=1)
            weight = dot_nn(query, left) * dot_nn(hot, taper)
            w_high, w_low = split(weight)
            both = dot_nn(w_high, b_both[...])
            xt[pl.ds(at, ROWS_O), :] = (
                x + both[:, :LANES] + both[:, LANES:] + dot_nn(w_low, b_high[...])
            )
            return carry

        lax.fori_loop(0, (BLOCKS - 1 - k) * OBS // ROWS_O, chunk, 0)

    q = lax.axis_index("ma")
    e = increments[...]
    total = e + e[MEMBERS : MEMBERS + 1]
    row = lax.broadcasted_iota(jnp.int32, (24, LANES), 0)
    col = lax.broadcasted_iota(jnp.int32, (24, LANES), 1)
    fifth = sum(jnp.where(row >= i * CHUNK, 1, 0) for i in range(1, MA))
    member = (row - fifth * CHUNK) * 16 + q * MA + fifth
    chosen = jnp.where((col == member) & (row < OWN), 1.0, 0.0)
    chosen = chosen.astype(BF16)
    row = lax.broadcasted_iota(jnp.int32, (LANES, LANES), 0)
    col = lax.broadcasted_iota(jnp.int32, (LANES, LANES), 1)
    back = sum(jnp.where(col >= i * OWN, 1, 0) for i in range(1, MA))
    place = col - back * OWN
    fifth = sum(jnp.where(place >= i * CHUNK, 1, 0) for i in range(1, MA))
    member = (place - fifth * CHUNK) * 16 + jnp.bitwise_and(q - back, MA - 1) * MA + fifth
    shuffle = jnp.where((row == member) & (col < MEMBERS), 1.0, 0.0)
    shuffle = shuffle.astype(BF16)
    t_high, t_low = [
        dot_nn(dot_nn(chosen, piece).astype(BF16), shuffle).astype(BF16) for piece in split(total)
    ]
    tiles = []
    for c in range(8):
        at = pl.ds(c, OWN, stride=8)
        tile = jnp.concatenate(
            [ref[at, :] for ref in (state_ref, gathered_1, gathered_2, gathered_3)], axis=0
        )
        tiles.append(tile - jnp.mean(tile, axis=0, keepdims=True))
    centered = jnp.concatenate(
        [jnp.concatenate(tiles, axis=1), jnp.zeros((LANES - MEMBERS, CELLS), F32)], axis=0
    )
    c_high, c_low = split(centered)
    update = dot_nn(t_high, c_high) + dot_nn(t_low, c_high) + dot_nn(t_high, c_low)
    for c in range(8):
        at = pl.ds(c, OWN, stride=8)
        out_ref[at, :] = state_ref[at, :] + update[:OWN, c * LANES : (c + 1) * LANES]


def other_core(x):
    return lax.ppermute(x, "gy", [(0, 1), (1, 0)])


def params(mebibytes):
    return pltpu.CompilerParams(vmem_limit_bytes=mebibytes * 1024 * 1024)


def over_members(x):
    return [lax.ppermute(x, "ma", [(i, (i + s) % MA) for i in range(MA)]) for s in range(1, MA)]


def local(
    ensemble, wind_field, obs_value, obs_var, obs_region, obs_cell, block_order, localization
):
    both = jnp.concatenate([ensemble, wind_field], axis=0)
    forward = [(i, (i + 1) % GX) for i in range(GX)]
    backward = [(i, (i - 1) % GX) for i in range(GX)]
    low = lax.ppermute(both[:, :, 2:], "gx", forward)
    high = lax.ppermute(both[:, :, :2], "gx", backward)
    prepared = pl.pallas_call(
        prepare_kernel,
        out_shape=(
            jax.ShapeDtypeStruct((40, LANES), F32),
            jax.ShapeDtypeStruct((4 * BLOCKS, OBS), F32),
        ),
        in_specs=[pl.BlockSpec(memory_space=pltpu.HBM)] * 6,
        out_specs=(VMEM,) * 2,
        scratch_shapes=[pltpu.SMEM((BLOCKS,), jnp.int32)]
        + [pltpu.VMEM((BLOCKS, OBS), jnp.int32)] * 2
        + [pltpu.VMEM((BLOCKS, OBS), F32)] * 3
        + [pltpu.SemaphoreType.DMA((6,))],
        compiler_params=params(60),
        cost_estimate=pl.CostEstimate(flops=10_000_000, bytes_accessed=2_000_000, transcendentals=0),
        name="prepare",
    )(block_order, obs_cell, obs_region, obs_value, obs_var, localization.reshape(BLOCKS, OBS))
    low, high, prepared = lax.optimization_barrier((low, high, prepared))
    index, observed = prepared
    own = jnp.concatenate([low, both, high], axis=2).reshape(-1, LANES)
    beside = other_core(own)

    state, picked = pl.pallas_call(
        advect_kernel,
        out_shape=(
            jax.ShapeDtypeStruct((OWN * 8, LANES), F32),
            jax.ShapeDtypeStruct((GX * SENT, LANES), F32),
        ),
        in_specs=[VMEM] * 3,
        out_specs=(VMEM, VMEM),
        scratch_shapes=[pltpu.VMEM((2, 24 * 8, LANES), F32)],
        compiler_params=params(4),
        cost_estimate=pl.CostEstimate(flops=10_000_000, bytes_accessed=1_000_000, transcendentals=0),
        name="advect",
    )(own, beside, index)

    parts = lax.all_to_all(picked.reshape(GX, 1, SENT * LANES), "gx", 0, 0, tiled=True)
    gathered = over_members(state)
    parts, gathered = lax.optimization_barrier((parts, gathered))
    parts = parts.reshape(-1, LANES)
    owned = pl.pallas_call(
        owner_kernel,
        out_shape=jax.ShapeDtypeStruct((MA * GX * CHUNK, LANES), F32),
        in_specs=[VMEM],
        out_specs=VMEM,
        compiler_params=params(4),
        name="owner",
    )(parts)
    weights = pl.pallas_call(
        weights_kernel,
        out_shape=jax.ShapeDtypeStruct((QUARTER * GX, LANES), F32),
        in_specs=[VMEM],
        out_specs=VMEM,
        compiler_params=params(4),
        name="weights",
    )(parts)
    came = lax.all_to_all(
        owned.reshape(MA * GX, 1, CHUNK * LANES), ("ma", "gx"), 0, 0, tiled=True
    ).reshape(-1, LANES)
    weights = jnp.concatenate([weights] + over_members(weights), axis=0)
    came, weights = lax.optimization_barrier((came, weights))
    tapers = pl.pallas_call(
        tapers_kernel,
        out_shape=jax.ShapeDtypeStruct((TAPERS + (BLOCKS - 1) * OBS, LANES), BF16),
        in_specs=[VMEM] * 3,
        out_specs=VMEM,
        compiler_params=params(4),
        cost_estimate=pl.CostEstimate(flops=1000, bytes_accessed=1000, transcendentals=0),
        name="tapers",
    )(weights, other_core(weights), observed)
    came_beside = other_core(came)

    out = pl.pallas_call(
        filter_kernel,
        out_shape=jax.ShapeDtypeStruct((OWN * 8, LANES), F32),
        in_specs=[VMEM] * 8,
        out_specs=VMEM,
        scratch_shapes=[
            pltpu.VMEM((BLOCKS * OBS, LANES), F32),
            pltpu.VMEM((OBS, LANES), BF16),
            pltpu.VMEM((OBS, 2 * LANES), BF16),
            pltpu.VMEM((LANES, LANES), F32),
            pltpu.VMEM((LANES, OBS), F32),
        ],
        compiler_params=params(32),
        cost_estimate=pl.CostEstimate(flops=3_000_000_000, bytes_accessed=4_000_000, transcendentals=0),
        name="filter",
    )(came, came_beside, tapers, observed, *gathered, state)
    return out.reshape(ensemble.shape)


def solution(mesh):
    in_specs = (
        P("ma", None, "gx", "gy"),
        P(None, None, "gx", "gy"),
        P(),
        P(),
        P(),
        P(),
        P(),
        P("gx", "gy", None, None),
    )
    out_specs = P("ma", None, "gx", "gy")
    return jax.shard_map(local, mesh=mesh, in_specs=in_specs, out_specs=out_specs, check_vma=False)
```
